256 devices in a mesh: seq: 64 (over x, z, core), tp: 4 (over y).
Axes of the slice: x: 4, y: 4, z: 8, core: 2. Of those that a mesh axis runs over, the one named last changes fastest.
Arguments:
- tokens: bfloat16 [4096, 2048], P('seq'), may hold values from -6 to 6
- qkv_weight: bfloat16 [2048, 3, 2048], P('seq', None, 'tp'), may hold values from -0.125 to 0.125
- out_weight: bfloat16 [2048, 2048], P('tp', 'seq'), may hold values from -0.125 to 0.125
- kv_cache: bfloat16 [64, 8, 64, 2, 2048], P(None, None, 'seq', None, 'tp')
- lengths: int32 [64], replicated, may hold values from 64 to 448, as said below
- parents: int32 [64, 64], replicated, may hold values from -1 to 62, as said below
- leaves: int32 [64], replicated, may hold values from 32 to 63
- deal: int32 [64], replicated, may hold values from 0 to 63, each once
Outputs:
- branch_out: bfloat16 [4096, 2048], P('seq', 'tp')
- new_cache: bfloat16 [64, 8, 64, 2, 2048], P(None, None, 'seq', None, 'tp')
The draws below stay inside these ranges and needn't reach their ends.
Inputs may be any that keep to these rules, and one draw needn't show every extreme that they name: `lengths`: every length is at least 64, and at most 448, both reached. parents[r, 0] = -1 and 0 <= parents[r, j] < j for j > 0.
All inputs are finite; a program needn't handle non-finite values.
Results may differ from the reference program's by a relative error of at most 0.012.
The reference program's roundings to bfloat16 on the way count: a program that leaves them out, or rounds other values in their place, can miss the bound.
Values may be sent and summed in bfloat16 or wider, within the bound.
A program may use at most 64 MiB of HBM per device.

```python
import jax
import jax.numpy as jnp
from jax import lax

D = 2048
H = 16
HD = 128
CPOS = 8
Q = 64
SINKS = 4
R = 64
TOKENS = 4096
SHARDS = 64
CAP = 512
WINDOW = 256


def draw_kv_cache(key, part):
    values = jax.random.normal(key, (R, CPOS, SHARDS, 2, H * HD), jnp.float32)
    return values.astype(jnp.bfloat16)


def draw_lengths(key, part):
    base = jax.random.randint(key, (R,), Q, CAP - Q + 1).astype(jnp.int32)
    longest = jax.random.randint(jax.random.fold_in(key, 1), (), 0, R)
    shortest = (longest + 1 + jax.random.randint(jax.random.fold_in(key, 2), (), 0, R - 1)) % R
    return base.at[shortest].set(Q).at[longest].set(CAP - Q)


def draw_parents(key, part):
    ids = jnp.arange(Q, dtype=jnp.int32)
    backward = jax.random.randint(key, (R, Q), 1, 4).astype(jnp.int32)
    parent = jnp.maximum(ids[None, :] - backward, 0)
    parent = parent.at[:, Q - 1].set(Q - 2)
    return parent.at[:, 0].set(-1)


def draw_leaves(key, part):
    base = jax.random.randint(key, (R,), Q // 2, Q).astype(jnp.int32)
    deepest = jax.random.randint(jax.random.fold_in(key, 1), (), 0, R)
    other = (deepest + 1 + jax.random.randint(jax.random.fold_in(key, 2), (), 0, R - 1)) % R
    return base.at[other].set(Q // 2).at[deepest].set(Q - 1)


def level_of(stream_key, shape, pieces, least, largest):
    def one(dim, blocks):
        draws = jax.random.uniform(jax.random.fold_in(jax.random.fold_in(stream_key, 6), dim), (blocks,), jnp.float32, least / len(pieces), largest / len(pieces))
        return jnp.repeat(jnp.exp(draws), shape[dim] // blocks).reshape((-1,) + (1,) * (len(shape) - dim - 1))

    loudness = one(*pieces[0])
    for cut in pieces[1:]:
        loudness = loudness * one(*cut)
    return loudness


def normal_values(own_key, dims, spread, bound, split=(), held_as=jnp.bfloat16):
    array = spread * jax.random.normal(own_key, dims, jnp.float32)
    if split:
        array = array * level_of(own_key, dims, split, -0.22, 0.18)
    return jnp.clip(array, -bound, bound).astype(held_as)


def setup_inputs(seed: int = 0) -> dict:
    streams_of = jax.random.split(jax.random.key(seed), 9)
    tokens = normal_values(streams_of[0], (TOKENS, D), 1.0, 6.0, ((0, 64),))
    qkv_weight = normal_values(streams_of[1], (D, 3, H * HD), D ** -0.5, 0.125, ((0, 64), (2, 4)))
    out_weight = normal_values(streams_of[2], (H * HD, D), (H * HD) ** -0.5, 0.125, ((0, 4), (1, 64)))
    kv_cache = draw_kv_cache(jax.random.fold_in(streams_of[8], 71), 0)
    lengths = draw_lengths(jax.random.fold_in(streams_of[8], 71), 0)
    parents = draw_parents(jax.random.fold_in(streams_of[8], 71), 0)
    leaves = draw_leaves(jax.random.fold_in(streams_of[8], 71), 0)
    deal = jax.random.permutation(streams_of[7], R).astype(jnp.int32)
    return {"tokens": tokens, "qkv_weight": qkv_weight, "out_weight": out_weight, "kv_cache": kv_cache, "lengths": lengths, "parents": parents, "leaves": leaves, "deal": deal}


def ancestry(parent_row):
    size = parent_row.shape[0]
    ids = jnp.arange(size, dtype=jnp.int32)
    links = (parent_row[:, None] == ids[None, :]).astype(jnp.float32)
    reach = jnp.eye(size, dtype=jnp.float32) + links
    for turn in range((size - 1).bit_length()):
        reach = jnp.minimum(jnp.dot(reach, reach, precision=lax.Precision.HIGHEST), 1.0)
    return reach

def rotate(values, places):
    width = values.shape[-1]
    half = width // 2
    frequency = 10000.0 ** (-2.0 * jnp.arange(half, dtype=jnp.float32) / width)
    angle = places.astype(jnp.float32)[:, None] * frequency[None, :]
    cosine = jnp.cos(angle)[:, None, :]
    sine_part = jnp.sin(angle)[:, None, :]
    lower_half = values[..., :half]
    upper_half = values[..., half:]
    return jnp.concatenate([lower_half * cosine - upper_half * sine_part, upper_half * cosine + lower_half * sine_part], axis=-1)

def reference(tokens, qkv_weight, out_weight, kv_cache, lengths, parents, leaves, deal):
    wide = tokens.astype(jnp.float32)
    centred = wide - lax.optimization_barrier(jnp.mean(wide, axis=-1, keepdims=True))
    normed = (centred * lax.rsqrt(lax.optimization_barrier(jnp.mean(centred * centred, axis=-1, keepdims=True)) + 1e-05)).astype(jnp.bfloat16)
    projected = jnp.dot(normed, qkv_weight.reshape(D, 3 * H * HD), preferred_element_type=jnp.float32)
    projected = projected.reshape(R, Q, 3, H, HD)
    cache = kv_cache.reshape(R, CAP, 2, H, HD)
    scale = float(HD) ** (-0.5)
    position = jnp.arange(CAP, dtype=jnp.int32)

    def per_slot(inputs):
        parts, request = inputs
        length = lengths[request]
        reach = ancestry(parents[request])
        depth = (lax.optimization_barrier(jnp.sum(reach, axis=1)) - 1.0).astype(jnp.int32)
        places = length + depth
        query = rotate(parts[:, 0], places).astype(jnp.bfloat16)
        key_new = rotate(parts[:, 1], places).astype(jnp.bfloat16)
        value_new = parts[:, 2].astype(jnp.bfloat16)
        old = cache[request]
        keys = old[:, 0].astype(jnp.float32)
        values = old[:, 1].astype(jnp.float32)
        scores = jnp.einsum('qhd,khd->qhk', query.astype(jnp.float32), keys) * scale
        valid = (position < length) & ((position < SINKS) | (position >= length - WINDOW))
        masked = jnp.where(valid[None, None, :], scores, -1e+30)
        cache_top = lax.optimization_barrier(jnp.max(masked, axis=-1))
        weights = jnp.where(valid[None, None, :], jnp.exp(masked - cache_top[..., None]), 0.0)
        cache_total = lax.optimization_barrier(jnp.sum(weights, axis=-1))
        weighted = jnp.einsum('qhk,khd->qhd', weights.astype(jnp.bfloat16).astype(jnp.float32), values)
        tree_scores = jnp.einsum('qhd,khd->qhk', query.astype(jnp.float32), key_new.astype(jnp.float32)) * scale
        tree_valid = (reach > 0.5)[:, None, :]
        tree_masked = jnp.where(tree_valid, tree_scores, -1e+30)
        joint = jnp.maximum(cache_top, lax.optimization_barrier(jnp.max(tree_masked, axis=-1)))
        tree_weights = jnp.where(tree_valid, jnp.exp(tree_masked - joint[..., None]), 0.0)
        ratio = jnp.exp(cache_top - joint)
        tree_sum = jnp.einsum('qhk,khd->qhd', tree_weights.astype(jnp.bfloat16).astype(jnp.float32), value_new.astype(jnp.float32))
        attended = (weighted * ratio[..., None] + tree_sum) / (cache_total * ratio + lax.optimization_barrier(jnp.sum(tree_weights, axis=-1)))[..., None]
        attended = attended.astype(jnp.bfloat16).reshape(Q, H * HD)
        on_path = reach[leaves[request]]
        path_end = (jnp.sum(on_path) - 1.0).astype(jnp.int32)
        levels = jnp.arange(Q, dtype=jnp.int32)
        picker = on_path[None, :] * (depth[None, :] == levels[:, None]).astype(jnp.float32)
        fresh = jnp.stack([key_new, value_new], axis=1).reshape(Q, 2 * H * HD)
        path_rows = jnp.dot(picker.astype(jnp.bfloat16), fresh, preferred_element_type=jnp.float32).astype(jnp.bfloat16)
        offset = position - length
        accept = (offset >= 0) & (offset <= path_end)
        chosen = path_rows[jnp.clip(offset, 0, Q - 1).astype(jnp.int32)]
        updated = jnp.where(accept[:, None], chosen, old.reshape(CAP, 2 * H * HD))
        return (attended, updated)
    attended_all, updated_all = lax.map(per_slot, (projected, deal))
    branch_out = jnp.dot(attended_all.reshape(TOKENS, H * HD), out_weight, preferred_element_type=jnp.float32).astype(jnp.bfloat16)
    new_cache = kv_cache.reshape(R, CAP, 2 * H * HD).at[deal].set(updated_all)
    return (branch_out, new_cache.reshape(R, CPOS, SHARDS, 2, H * HD))
```

```python
import functools

import jax
import jax.numpy as jnp
from jax import lax
from jax.experimental import pallas as pl
from jax.experimental.pallas import tpu as pltpu
from jax.sharding import PartitionSpec as P

HD = 128
SINKS = 4
X, Z, CORES = 4, 8, 2
SEQ = X * Z * CORES
TP = 4
ROWS = 64
SLOTS = 4
WIDTH = 512
HEADS = WIDTH // HD
WINDOW = 256
DEEP = 2048


def nt(a, b):
    return lax.dot_general(
        a, b, (((1,), (1,)), ((), ())), preferred_element_type=jnp.float32
    )


def nn(a, b):
    return lax.dot_general(
        a, b, (((1,), (0,)), ((), ())), preferred_element_type=jnp.float32
    )


def pre_kernel(
    deal, lengths, leaves, tokens, parents, freq, cache,
    packed, sinks, normed, reach_out, cos_out, sin_out, pick_out, depth_out,
    par_pad,
):
    me = lax.axis_index("seq")

    def pack(t, carry):
        r = deal[t]
        base = jnp.maximum(lengths[r] - WINDOW, 0)
        first = lax.shift_right_logical(base - me + (SEQ - 1), 6)
        packed[t] = cache[r, pl.ds(first, SLOTS)]
        sinks[t] = cache[r, 0]
        return carry

    lax.fori_loop(0, ROWS, pack, 0)

    wide = tokens[...].astype(jnp.float32)
    centred = wide - jnp.mean(wide, axis=-1, keepdims=True)
    scale = lax.rsqrt(jnp.mean(centred * centred, axis=-1, keepdims=True) + 1e-05)
    normed[...] = (centred * scale).astype(jnp.bfloat16)

    request = deal[me]
    length = lengths[request]
    leaf = leaves[request]
    sub = lax.broadcasted_iota(jnp.int32, (ROWS, ROWS), 0)
    lane = lax.broadcasted_iota(jnp.int32, (ROWS, ROWS), 1)
    eye = jnp.where(sub == lane, 1.0, 0.0)
    row = parents[pl.ds(request, 1), :]
    up = eye + jnp.where(row == sub, 1.0, 0.0)
    for _ in range(6):
        half = up.astype(jnp.bfloat16)
        up = jnp.minimum(nn(half, half), 1.0)
    reach = nt(eye.astype(jnp.bfloat16), up.astype(jnp.bfloat16))
    reach_out[...] = reach
    depth_row = (jnp.sum(up, axis=0, keepdims=True) - 1.0).astype(jnp.int32)
    depth_col = (jnp.sum(reach, axis=1, keepdims=True) - 1.0).astype(jnp.int32)
    places = (length + depth_col).astype(jnp.float32)
    angle = places * freq[...]
    cos_out[...] = jnp.cos(angle)
    wave = jnp.sin(angle)
    wide_lane = lax.broadcasted_iota(jnp.int32, (ROWS, HD), 1)
    sin_out[...] = jnp.where(wide_lane < HD // 2, -wave, wave)
    on_path = jnp.sum(jnp.where(sub == leaf, reach, 0.0), axis=0, keepdims=True)
    offset = lax.rem(sub - length + 8 * SEQ, SEQ)
    hit = (on_path > 0.5) & (depth_row == offset)
    pick_out[...] = jnp.where(hit, 1.0, 0.0).astype(jnp.bfloat16)

    lanes = lax.broadcasted_iota(jnp.int32, (ROWS, HD), 1)
    par_pad[...] = lanes
    par_pad[:, 0:ROWS] = parents[...]
    par = par_pad[...]
    climb = jnp.where((lanes < ROWS) & (par >= 0), 1, 0)
    jump = jnp.where(par < 0, 0, par)
    for _ in range(6):
        climb = climb + jnp.take_along_axis(climb, jump, axis=1)
        jump = jnp.take_along_axis(jump, jump, axis=1)
    depth_out[...] = climb


def comm_kernel(
    wq, wo, kv, sk, WQ, WO, KV, SK,
    own_sem, ra, rb, sa, sb, sib_sa, sib_sb, sib_ra, sib_rb,
    kv_s, kv_r, sk_s, sk_r,
):
    me = lax.axis_index("seq")
    x = me // (Z * CORES)
    z = lax.rem(me // CORES, Z)
    c = lax.rem(me, CORES)

    def idx(dx, dz):
        return (
            lax.rem(x + (dx + X), X) * Z + lax.rem(z + (dz + Z), Z)
        ) * CORES + c

    sibling = me + 1 - 2 * c
    to = {
        "x+": {"seq": idx(1, 0)},
        "x-": {"seq": idx(-1, 0)},
        "z+": {"seq": idx(0, 1)},
        "z-": {"seq": idx(0, -1)},
        "s": {"seq": sibling},
    }
    shift = {"x+": (-1, 0), "x-": (1, 0), "z+": (0, -1), "z-": (0, 1)}

    barrier = pltpu.get_barrier_semaphore()

    def greet(k, carry):
        pl.semaphore_signal(barrier, 1, device_id={"seq": lax.rem(me + k, SEQ)})
        return carry

    lax.fori_loop(1, SEQ, greet, 0)
    pl.semaphore_wait(barrier, SEQ - 1)

    def send_a(dx, dz, way):
        at = idx(dx, dz)
        src = wq if (dx, dz) == (0, 0) else WQ.at[:, at]
        if way == "s":
            send, recv = sib_sa, sib_ra
        else:
            ox, oz = shift[way]
            send, recv = sa, ra.at[(dx + ox) % X, (dz + oz) % Z]
        pltpu.make_async_remote_copy(
            src_ref=src, dst_ref=WQ.at[:, at], send_sem=send, recv_sem=recv,
            device_id=to[way],
        ).start()

    def send_b(dx, dz, way):
        at = idx(dx, dz)
        src = wo if (dx, dz) == (0, 0) else WO.at[at]
        if way == "s":
            send, recv = sib_sb, sib_rb
        else:
            ox, oz = shift[way]
            send, recv = sb, rb.at[(dx + ox) % X, (dz + oz) % Z]
        pltpu.make_async_remote_copy(
            src_ref=src, dst_ref=WO.at[at], send_sem=send, recv_sem=recv,
            device_id=to[way],
        ).start()

    def wait_a(dx, dz):
        at = idx(dx, dz)
        pltpu.make_async_copy(
            WQ.at[:, at], WQ.at[:, at], ra.at[dx % X, dz % Z]
        ).wait()

    def wait_b(dx, dz):
        at = idx(dx, dz)
        pltpu.make_async_copy(WO.at[at], WO.at[at], rb.at[dx % X, dz % Z]).wait()

    def route_a(dx, dz):
        out = []
        if dx == 0:
            if dz == 0:
                out += ["z+", "z-"]
            elif -4 < dz < 0:
                out += ["z+"]
            elif 0 < dz < 3:
                out += ["z-"]
            out += ["x+", "x-"]
        elif dx == -1 and dz % 2 == 0:
            out += ["x+"]
        elif dx == 1 and dz % 2 == 1:
            out += ["x-"]
        return out + ["s"]

    def route_b(dx, dz):
        out = []
        if dz == 0:
            if dx == 0:
                out += ["x+", "x-"]
            elif dx == -1:
                out += ["x+"]
            out += ["z+", "z-"]
        else:
            far = 4 if dx % 2 == 0 else 3
            if -far < dz < 0:
                out += ["z+"]
            elif 0 < dz < 7 - far:
                out += ["z-"]
        return out + ["s"]

    own_a = pltpu.make_async_copy(wq, WQ.at[:, me], own_sem.at[0])
    own_b = pltpu.make_async_copy(wo, WO.at[me], own_sem.at[1])
    own_kv = pltpu.make_async_copy(kv.at[me], KV.at[me], own_sem.at[2])
    for way in route_a(0, 0):
        send_a(0, 0, way)
    for way in route_b(0, 0):
        send_b(0, 0, way)
    own_a.start()
    own_b.start()
    own_kv.start()

    def scatter(k, carry):
        t = lax.rem(me + k, SEQ)
        pltpu.make_async_remote_copy(
            src_ref=kv.at[t], dst_ref=KV.at[me], send_sem=kv_s, recv_sem=kv_r,
            device_id={"seq": t},
        ).start()
        return carry

    lax.fori_loop(1, SEQ, scatter, 0)

    @pl.when(me < SINKS)
    def _():
        pltpu.make_async_copy(sk.at[me], SK.at[me], sk_r).start()

        def spread(k, carry):
            t = lax.rem(me + k, SEQ)
            pltpu.make_async_remote_copy(
                src_ref=sk.at[t], dst_ref=SK.at[me], send_sem=sk_s, recv_sem=sk_r,
                device_id={"seq": t},
            ).start()
            return carry

        lax.fori_loop(1, SEQ, spread, 0)

    steps = []
    for dz in (-1, 1, -2, 2, -3, 3, -4):
        steps.append((2 * abs(dz), "a", 0, dz))
    for dx, cost in ((-1, 1), (1, 1), (-2, 2)):
        steps.append((2 * cost + 0.2, "b", dx, 0))
    for dz in (0, -1, 1, -2, 2, -3, 3, -4):
        for dx, cost in ((-1, 1), (1, 1), (-2, 2)):
            steps.append((2 * abs(dz) + 2 * cost + 0.5, "a", dx, dz))
    for dx in (0, -1, 1, -2):
        far = 4 if dx % 2 == 0 else 3
        for dz in list(range(-far, 0)) + list(range(1, 8 - far)):
            steps.append((2 * abs(dx) + 2 * abs(dz) + 0.6, "b", dx, dz))
    for _, kind, dx, dz in sorted(steps, key=lambda s: s[0]):
        if kind == "a":
            wait_a(dx, dz)
            for way in route_a(dx, dz):
                send_a(dx, dz, way)
        else:
            wait_b(dx, dz)
            for way in route_b(dx, dz):
                send_b(dx, dz, way)

    own_a.wait()
    own_b.wait()
    own_kv.wait()

    def all_of(ref, sem):
        pltpu.make_async_copy(ref, ref, sem).wait()

    others = pl.ds(0, SEQ - 1)
    pieces = SEQ // CORES
    all_of(KV.at[others], kv_r)
    all_of(SK, sk_r)
    all_of(WQ.at[:, pl.ds(0, pieces)], sib_ra)
    all_of(WO.at[pl.ds(0, pieces)], sib_rb)
    all_of(WQ.at[:, pl.ds(0, pieces - 1)], sa)
    all_of(WO.at[pl.ds(0, pieces - 1)], sb)
    all_of(WQ.at[:, pl.ds(0, pieces)], sib_sa)
    all_of(WO.at[pl.ds(0, pieces)], sib_sb)
    all_of(kv.at[others], kv_s)

    @pl.when(me < SINKS)
    def _():
        all_of(sk.at[others], sk_s)


def main_kernel(
    deal, lengths, normed, wq, wo, kv, sk, reach, cos, sin, pick,
    part, fresh_k, fresh_v, acc, att,
):
    step = pl.program_id(0)

    @pl.when(step == 0)
    def _():
        acc[...] = jnp.zeros_like(acc)

    for kind in range(3):
        acc[kind] += nn(normed[...], wq[kind])

    @pl.when(step == pl.num_programs(0) - 1)
    def _():
        length = lengths[deal[lax.axis_index("seq")]]
        scale = float(HD) ** (-0.5)
        base = jnp.maximum(length - WINDOW, 0)
        lane = lax.broadcasted_iota(jnp.int32, (ROWS, SEQ * SLOTS * 2), 1)
        shard = lax.shift_right_logical(lane, 3)
        slot = lax.shift_right_logical(lane & 7, 1)
        first = lax.shift_right_logical(base - shard + (SEQ - 1), 6)
        place = (first + slot) * SEQ + shard
        valid = (
            ((lane & 1) == 0)
            & (place < length)
            & ((place < SINKS) | (place >= length - WINDOW))
        )
        lane_s = lax.broadcasted_iota(jnp.int32, (ROWS, 2 * SINKS), 1)
        valid_s = ((lane_s & 1) == 0) & (
            length - WINDOW > lax.shift_right_logical(lane_s, 1)
        )
        tree = reach[...] > 0.5
        cosine = cos[...]
        sine = sin[...]

        def turn(v):
            return v * cosine + pltpu.roll(v, HD // 2, 1) * sine

        for h in range(HEADS):
            cols = slice(h * HD, (h + 1) * HD)
            q = turn(acc[0, :, cols]).astype(jnp.bfloat16)
            k = turn(acc[1, :, cols]).astype(jnp.bfloat16)
            v = acc[2, :, cols].astype(jnp.bfloat16)
            old = kv[:, cols]
            old_s = sk[:, cols]
            s = jnp.where(valid, nt(q, old) * scale, -1e30)
            s_s = jnp.where(valid_s, nt(q, old_s) * scale, -1e30)
            top = jnp.maximum(
                jnp.max(s, axis=-1, keepdims=True), jnp.max(s_s, axis=-1, keepdims=True)
            )
            w = jnp.where(valid, jnp.exp(s - top), 0.0)
            w_s = jnp.where(valid_s, jnp.exp(s_s - top), 0.0)
            total = jnp.sum(w, axis=-1, keepdims=True) + jnp.sum(
                w_s, axis=-1, keepdims=True
            )
            shifted = pltpu.roll(w, 1, 1).astype(jnp.bfloat16)
            odd = lax.broadcasted_iota(jnp.int32, (2 * SINKS, 2 * SINKS), 0) + 1
            move = jnp.where(
                odd == lax.broadcasted_iota(jnp.int32, (2 * SINKS, 2 * SINKS), 1),
                1.0, 0.0,
            ).astype(jnp.bfloat16)
            shifted_s = nn(w_s.astype(jnp.bfloat16), move).astype(jnp.bfloat16)
            weighted = nn(shifted, old) + nn(shifted_s, old_s)
            t = jnp.where(tree, nt(q, k) * scale, -1e30)
            joint = jnp.maximum(top, jnp.max(t, axis=-1, keepdims=True))
            tw = jnp.where(tree, jnp.exp(t - joint), 0.0)
            ratio = jnp.exp(top - joint)
            summed = nn(tw.astype(jnp.bfloat16), v)
            below = total * ratio + jnp.sum(tw, axis=-1, keepdims=True)
            att[:, cols] = ((weighted * ratio + summed) / below).astype(jnp.bfloat16)
            fresh_k[:, cols] = nn(pick[...], k).astype(jnp.bfloat16)
            fresh_v[:, cols] = nn(pick[...], v).astype(jnp.bfloat16)

        a = att[...]
        for t in range(TP):
            part[t] = nt(a, wo[t * WIDTH:(t + 1) * WIDTH, :]).astype(jnp.bfloat16)


def tail_kernel(part, fresh, P_out, G, own_sem, ps, pr, gs, gr):
    me = lax.axis_index("seq")
    lane = lax.axis_index("tp")
    barrier = pltpu.get_barrier_semaphore()

    def greet(k, carry):
        pl.semaphore_signal(barrier, 1, device_id={"seq": lax.rem(me + k, SEQ)})
        return carry

    lax.fori_loop(1, SEQ, greet, 0)
    for k in range(1, TP):
        pl.semaphore_signal(barrier, 1, device_id={"tp": lax.rem(lane + k, TP)})
    pl.semaphore_wait(barrier, SEQ + TP - 2)

    for k in range(1, TP):
        t = lax.rem(lane + k, TP)
        pltpu.make_async_remote_copy(
            src_ref=part.at[t], dst_ref=P_out.at[lane], send_sem=ps, recv_sem=pr,
            device_id={"tp": t},
        ).start()

    def scatter(k, carry):
        t = lax.rem(me + k, SEQ)
        pltpu.make_async_remote_copy(
            src_ref=fresh.at[t], dst_ref=G.at[me], send_sem=gs, recv_sem=gr,
            device_id={"seq": t},
        ).start()
        return carry

    lax.fori_loop(1, SEQ, scatter, 0)
    own_p = pltpu.make_async_copy(part.at[lane], P_out.at[lane], own_sem.at[0])
    own_g = pltpu.make_async_copy(fresh.at[me], G.at[me], own_sem.at[1])
    own_p.start()
    own_g.start()
    own_p.wait()
    own_g.wait()

    def all_of(ref, sem):
        pltpu.make_async_copy(ref, ref, sem).wait()

    all_of(P_out.at[pl.ds(0, TP - 1)], pr)
    all_of(G.at[pl.ds(0, SEQ - 1)], gr)
    all_of(part.at[pl.ds(0, TP - 1)], ps)
    all_of(fresh.at[pl.ds(0, SEQ - 1)], gs)


def final_kernel(deal, lengths, leaves, depth, P_in, G, cache, branch, new_cache):
    me = lax.axis_index("seq")
    total = P_in[0].astype(jnp.float32)
    for t in range(1, TP):
        total = total + P_in[t].astype(jnp.float32)
    branch[...] = total.astype(jnp.bfloat16)
    new_cache[...] = cache[...]

    def place(i, carry):
        r = deal[i]
        length = lengths[r]
        offset = lax.rem(me - length + 8 * SEQ, SEQ)

        @pl.when(offset <= depth[r, leaves[r]])
        def _():
            new_cache[r, lax.shift_right_logical(length + offset, 6)] = G[i]

        return carry

    lax.fori_loop(0, ROWS, place, 0)


def whole():
    return pl.BlockSpec(memory_space=pltpu.VMEM)


def shaped(shape, dtype=jnp.bfloat16):
    return jax.ShapeDtypeStruct(shape, dtype)


def run_pre(deal, lengths, leaves, tokens, parents, freq, cache):
    return pl.pallas_call(
        pre_kernel,
        name="pre",
        grid_spec=pltpu.PrefetchScalarGridSpec(
            num_scalar_prefetch=3,
            in_specs=[whole()] * 4,
            out_specs=[whole()] * 8,
            scratch_shapes=[pltpu.VMEM((ROWS, HD), jnp.int32)],
        ),
        out_shape=[
            shaped((SEQ, SLOTS, 2, WIDTH)),
            shaped((SEQ, 2, WIDTH)),
            shaped((ROWS, DEEP)),
            shaped((ROWS, ROWS), jnp.float32),
            shaped((ROWS, HD), jnp.float32),
            shaped((ROWS, HD), jnp.float32),
            shaped((SEQ, ROWS)),
            shaped((ROWS, HD), jnp.int32),
        ],
    )(deal, lengths, leaves, tokens, parents, freq, cache)


def run_comm(wq, wo, packed, sinks):
    dma = pltpu.SemaphoreType.DMA
    return pl.pallas_call(
        comm_kernel,
        name="comm",
        in_specs=[pl.BlockSpec(memory_space=pl.ANY)] * 4,
        out_specs=[pl.BlockSpec(memory_space=pl.ANY)] * 4,
        out_shape=[
            shaped((3, SEQ, DEEP // SEQ, WIDTH)),
            shaped((SEQ, DEEP // SEQ, WIDTH)),
            shaped((SEQ, SLOTS, 2, WIDTH)),
            shaped((SINKS, 2, WIDTH)),
        ],
        scratch_shapes=[
            dma((3,)), dma((X, Z)), dma((X, Z)),
            dma, dma, dma, dma, dma, dma, dma, dma, dma, dma,
        ],
        compiler_params=pltpu.CompilerParams(collective_id=0, has_side_effects=True),
    )(wq, wo, packed, sinks)


def run_main(deal, lengths, normed, wq, wo, kv, sk, reach, cos, sin, pick):
    steps = 8
    deep = DEEP // steps
    return pl.pallas_call(
        main_kernel,
        name="main",
        grid_spec=pltpu.PrefetchScalarGridSpec(
            num_scalar_prefetch=2,
            grid=(steps,),
            in_specs=[
                pl.BlockSpec((ROWS, deep), lambda i, *_: (0, i)),
                pl.BlockSpec((3, deep, WIDTH), lambda i, *_: (0, i, 0)),
                whole(), whole(), whole(), whole(), whole(), whole(), whole(),
            ],
            out_specs=[whole()] * 3,
            scratch_shapes=[
                pltpu.VMEM((3, ROWS, WIDTH), jnp.float32),
                pltpu.VMEM((ROWS, WIDTH), jnp.bfloat16),
            ],
        ),
        out_shape=[
            shaped((TP, ROWS, WIDTH)),
            shaped((SEQ, WIDTH)),
            shaped((SEQ, WIDTH)),
        ],
    )(deal, lengths, normed, wq, wo, kv, sk, reach, cos, sin, pick)


def run_tail(part, fresh):
    dma = pltpu.SemaphoreType.DMA
    return pl.pallas_call(
        tail_kernel,
        name="tail",
        in_specs=[pl.BlockSpec(memory_space=pl.ANY)] * 2,
        out_specs=[pl.BlockSpec(memory_space=pl.ANY)] * 2,
        out_shape=[shaped((TP, ROWS, WIDTH)), shaped((SEQ, 2, WIDTH))],
        scratch_shapes=[dma((2,)), dma, dma, dma, dma],
        compiler_params=pltpu.CompilerParams(collective_id=1, has_side_effects=True),
    )(part, fresh)


def run_final(deal, lengths, leaves, depth, gathered, arrived, cache):
    return pl.pallas_call(
        final_kernel,
        name="final",
        grid_spec=pltpu.PrefetchScalarGridSpec(
            num_scalar_prefetch=4,
            in_specs=[whole()] * 3,
            out_specs=[whole()] * 2,
        ),
        out_shape=[shaped((ROWS, WIDTH)), shaped(cache.shape)],
    )(deal, lengths, leaves, depth, gathered, arrived, cache)


def on_device(tokens, qkv_weight, out_weight, kv_cache, lengths, parents, leaves, deal):
    cache = kv_cache.reshape(kv_cache.shape[0], kv_cache.shape[1], 2, WIDTH)
    half = HD // 2
    freq = 10000.0 ** (-2.0 * jnp.arange(half, dtype=jnp.float32) / HD)
    freq = jnp.concatenate([freq, freq])[None, :]
    packed, sinks, normed, reach, cos, sin, pick, depth = run_pre(
        deal, lengths, leaves, tokens, parents, freq, cache
    )
    wq = jnp.transpose(qkv_weight, (1, 0, 2))
    wo = jnp.transpose(out_weight, (1, 0))
    all_q, all_o, kv, sk = run_comm(wq, wo, packed, sinks)
    part, fresh_k, fresh_v = run_main(
        deal, lengths, normed,
        all_q.reshape(3, DEEP, WIDTH), all_o.reshape(DEEP, WIDTH),
        kv.reshape(SEQ * SLOTS * 2, WIDTH), sk.reshape(2 * SINKS, WIDTH),
        reach, cos, sin, pick,
    )
    fresh = jnp.stack([fresh_k, fresh_v], axis=1)
    gathered, arrived = run_tail(part, fresh)
    branch, new_cache = run_final(deal, lengths, leaves, depth, gathered, arrived, cache)
    return branch, new_cache.reshape(kv_cache.shape)


def solution(mesh):
    placed = (
        P("seq", None),
        P("seq", None, "tp"),
        P("tp", "seq"),
        P(None, None, "seq", None, "tp"),
        P(),
        P(),
        P(),
        P(),
    )
    return jax.shard_map(
        on_device,
        mesh=mesh,
        in_specs=placed,
        out_specs=(P("seq", "tp"), P(None, None, "seq", None, "tp")),
        check_vma=False,
    )
```

```python
import functools

import jax
import jax.numpy as jnp
from jax import lax
from jax.experimental import pallas as pl
from jax.experimental.pallas import tpu as pltpu
from jax.sharding import PartitionSpec as P

HD = 128
SINKS = 4
X, Z, CORES = 4, 8, 2
SEQ = X * Z * CORES
TP = 4
ROWS = 64
SLOTS = 4
WIDTH = 512
HEADS = WIDTH // HD
WINDOW = 256
DEEP = 2048
PROJ_AT = (10, 12, 14)


def nt(a, b):
    return lax.dot_general(
        a, b, (((1,), (1,)), ((), ())), preferred_element_type=jnp.float32
    )


def nn(a, b):
    return lax.dot_general(
        a, b, (((1,), (0,)), ((), ())), preferred_element_type=jnp.float32
    )


def whole_kernel(
    deal, lengths, leaves, tokens, parents, freq, cache, wq, wo,
    gathered, arrived, depth_out, cache_out,
    packed, sinks, WQ, WO, KV, SK, normed, acc, att, part, fresh, par_pad, G, PG,
    own_sem, ra, rb, sa, sb, sib_sa, sib_sb, sib_ra, sib_rb,
    kv_s, kv_r, sk_s, sk_r, ps, pr, gs, gr,
):
    me = lax.axis_index("seq")
    tp = lax.axis_index("tp")
    x = me // (Z * CORES)
    z = lax.rem(me // CORES, Z)
    c = lax.rem(me, CORES)

    def idx(dx, dz):
        return (
            lax.rem(x + (dx + X), X) * Z + lax.rem(z + (dz + Z), Z)
        ) * CORES + c

    barrier = pltpu.get_barrier_semaphore()

    def greet(k, carry):
        pl.semaphore_signal(barrier, 1, device_id={"seq": lax.rem(me + k, SEQ)})
        return carry

    lax.fori_loop(1, SEQ, greet, 0)
    for k in range(1, TP):
        pl.semaphore_signal(barrier, 1, device_id={"tp": lax.rem(tp + k, TP)})

    own_cache = pltpu.make_async_copy(cache, cache_out, own_sem.at[5])
    own_cache.start()
    own_a = pltpu.make_async_copy(wq, WQ.at[:, me], own_sem.at[0])
    own_b = pltpu.make_async_copy(wo, WO.at[me], own_sem.at[1])
    own_a.start()
    own_b.start()

    def pack(t, carry):
        r = deal[t]
        base = jnp.maximum(lengths[r] - WINDOW, 0)
        first = lax.shift_right_logical(base - me + (SEQ - 1), 6)
        packed[t] = cache[r, pl.ds(first, SLOTS)].reshape(2 * SLOTS, WIDTH)
        sinks[t] = cache[r, 0]
        return carry

    lax.fori_loop(0, ROWS, pack, 0)

    wide = tokens[...].astype(jnp.float32)
    centred = wide - jnp.mean(wide, axis=-1, keepdims=True)
    scaling = lax.rsqrt(jnp.mean(centred * centred, axis=-1, keepdims=True) + 1e-05)
    normed[...] = (centred * scaling).astype(jnp.bfloat16)
    acc[...] = jnp.zeros_like(acc)

    pl.semaphore_wait(barrier, SEQ + TP - 2)

    sibling = me + 1 - 2 * c
    to = {
        "x+": {"seq": idx(1, 0)},
        "x-": {"seq": idx(-1, 0)},
        "z+": {"seq": idx(0, 1)},
        "z-": {"seq": idx(0, -1)},
        "s": {"seq": sibling},
    }
    shift = {"x+": (-1, 0), "x-": (1, 0), "z+": (0, -1), "z-": (0, 1)}

    def send_a(dx, dz, way):
        at = idx(dx, dz)
        src = wq if (dx, dz) == (0, 0) else WQ.at[:, at]
        if way == "s":
            send, recv = sib_sa, sib_ra.at[dx % X]
        else:
            ox, oz = shift[way]
            send, recv = sa, ra.at[(dx + ox) % X, (dz + oz) % Z]
        pltpu.make_async_remote_copy(
            src_ref=src, dst_ref=WQ.at[:, at], send_sem=send, recv_sem=recv,
            device_id=to[way],
        ).start()

    def send_b(dx, dz, way):
        at = idx(dx, dz)
        src = wo if (dx, dz) == (0, 0) else WO.at[at]
        if way == "s":
            send, recv = sib_sb, sib_rb
        else:
            ox, oz = shift[way]
            send, recv = sb, rb.at[(dx + ox) % X, (dz + oz) % Z]
        pltpu.make_async_remote_copy(
            src_ref=src, dst_ref=WO.at[at], send_sem=send, recv_sem=recv,
            device_id=to[way],
        ).start()

    def wait_a(dx, dz):
        at = idx(dx, dz)
        pltpu.make_async_copy(
            WQ.at[:, at], WQ.at[:, at], ra.at[dx % X, dz % Z]
        ).wait()

    def wait_b(dx, dz):
        at = idx(dx, dz)
        pltpu.make_async_copy(WO.at[at], WO.at[at], rb.at[dx % X, dz % Z]).wait()

    def route_a(dx, dz):
        out = []
        if dx == 0:
            if dz == 0:
                out += ["z+", "z-"]
            elif -4 < dz < 0:
                out += ["z+"]
            elif 0 < dz < 3:
                out += ["z-"]
            out += ["x+", "x-"]
        elif dx == -1 and dz % 2 == 0:
            out += ["x+"]
        elif dx == 1 and dz % 2 == 1:
            out += ["x-"]
        return out + ["s"]

    def route_b(dx, dz):
        out = []
        if dz == 0:
            if dx == 0:
                out += ["x+", "x-"]
            elif dx == -1:
                out += ["x+"]
            out += ["z+", "z-"]
        else:
            far = 4 if dx % 2 == 0 else 3
            if -far < dz < 0:
                out += ["z+"]
            elif 0 < dz < 7 - far:
                out += ["z-"]
        return out + ["s"]

    def all_of(ref, sem):
        pltpu.make_async_copy(ref, ref, sem).wait()

    for way in route_a(0, 0):
        send_a(0, 0, way)
    for way in route_b(0, 0):
        send_b(0, 0, way)
    own_kv = pltpu.make_async_copy(packed.at[me], KV.at[me], own_sem.at[2])
    own_kv.start()

    def scatter(k, carry):
        t = lax.rem(me + k, SEQ)
        pltpu.make_async_remote_copy(
            src_ref=packed.at[t], dst_ref=KV.at[me], send_sem=kv_s, recv_sem=kv_r,
            device_id={"seq": t},
        ).start()
        return carry

    lax.fori_loop(1, SEQ, scatter, 0)

    @pl.when(me < SINKS)
    def _():
        pltpu.make_async_copy(sinks.at[me], SK.at[me], sk_r).start()

        def spread(k, carry):
            t = lax.rem(me + k, SEQ)
            pltpu.make_async_remote_copy(
                src_ref=sinks.at[t], dst_ref=SK.at[me], send_sem=sk_s, recv_sem=sk_r,
                device_id={"seq": t},
            ).start()
            return carry

        lax.fori_loop(1, SEQ, spread, 0)

    request = deal[me]
    length = lengths[request]
    leaf = leaves[request]
    sub = lax.broadcasted_iota(jnp.int32, (ROWS, ROWS), 0)
    lane = lax.broadcasted_iota(jnp.int32, (ROWS, ROWS), 1)
    eye = jnp.where(sub == lane, 1.0, 0.0)
    row = parents[pl.ds(request, 1), :]
    up = eye + jnp.where(row == sub, 1.0, 0.0)
    for _ in range(6):
        half = up.astype(jnp.bfloat16)
        up = jnp.minimum(nn(half, half), 1.0)
    reach = nt(eye.astype(jnp.bfloat16), up.astype(jnp.bfloat16))
    depth_row = (jnp.sum(up, axis=0, keepdims=True) - 1.0).astype(jnp.int32)
    depth_col = (jnp.sum(reach, axis=1, keepdims=True) - 1.0).astype(jnp.int32)
    places = (length + depth_col).astype(jnp.float32)
    angle = places * freq[...]
    cosine = jnp.cos(angle)
    wave = jnp.sin(angle)
    lanes = lax.broadcasted_iota(jnp.int32, (ROWS, HD), 1)
    sine = jnp.where(lanes < HD // 2, -wave, wave)
    on_path = jnp.sum(jnp.where(sub == leaf, reach, 0.0), axis=0, keepdims=True)
    offset = lax.rem(sub - length + 8 * SEQ, SEQ)
    hit = (on_path > 0.5) & (depth_row == offset)
    pick = jnp.where(hit, 1.0, 0.0).astype(jnp.bfloat16)

    par_pad[...] = lanes
    par_pad[:, 0:ROWS] = parents[...]
    par = par_pad[...]
    climb = jnp.where((lanes < ROWS) & (par >= 0), 1, 0)
    jump = jnp.where(par < 0, 0, par)
    for _ in range(6):
        climb = climb + jnp.take_along_axis(climb, jump, axis=1)
        jump = jnp.take_along_axis(jump, jump, axis=1)
    depth_out[...] = climb

    own_a.wait()
    own_b.wait()
    group = Z * CORES
    deep = group * (DEEP // SEQ)

    def project(dx, kind):
        block = lax.rem(x + (dx + X), X)
        left = normed[:, pl.ds(pl.multiple_of(block * deep, deep), deep)]
        right = WQ[kind, pl.ds(block * group, group)].reshape(deep, WIDTH)
        acc[kind] += nn(left, right)

    steps = []
    for dz in (-1, 1, -2, 2, -3, 3, -4):
        steps.append((2 * abs(dz), "a", 0, dz))
    for dx, cost in ((-1, 1), (1, 1), (-2, 2)):
        steps.append((2 * cost + 0.2, "b", dx, 0))
    for dz in (0, -1, 1, -2, 2, -3, 3, -4):
        for dx, cost in ((-1, 1), (1, 1), (-2, 2)):
            steps.append((2 * abs(dz) + 2 * cost + 0.5, "a", dx, dz))
    for dx in (0, -1, 1, -2):
        far = 4 if dx % 2 == 0 else 3
        for dz in list(range(-far, 0)) + list(range(1, 8 - far)):
            steps.append((2 * abs(dx) + 2 * abs(dz) + 0.6, "b", dx, dz))
    for turn, dx in enumerate((0, -1, 1)):
        for kind in range(3):
            steps.append((PROJ_AT[turn] + 0.7 + 0.01 * kind, "p", dx, kind))
    for _, kind, dx, dz in sorted(steps, key=lambda s: s[0]):
        if kind == "a":
            wait_a(dx, dz)
            for way in route_a(dx, dz):
                send_a(dx, dz, way)
        elif kind == "b":
            wait_b(dx, dz)
            for way in route_b(dx, dz):
                send_b(dx, dz, way)
        else:
            if dz == 0:
                all_of(WQ.at[:, pl.ds(0, Z)], sib_ra.at[dx % X])
            project(dx, dz)

    all_of(WQ.at[:, pl.ds(0, Z)], sib_ra.at[2])
    for kind in range(3):
        project(2, kind)

    def turn(v):
        return v * cosine + pltpu.roll(v, HD // 2, 1) * sine

    sides = [slice(h * HD, (h + 1) * HD) for h in range(HEADS)]
    keys, values = [], []
    twice = lax.broadcasted_iota(jnp.int32, (2 * SEQ, SEQ), 0)
    once = lax.broadcasted_iota(jnp.int32, (2 * SEQ, SEQ), 1)
    even = jnp.where(twice == 2 * once, 1.0, 0.0).astype(jnp.bfloat16)
    odd = jnp.where(twice == 2 * once + 1, 1.0, 0.0).astype(jnp.bfloat16)
    pick_k = nn(even, pick).astype(jnp.bfloat16)
    pick_v = nn(odd, pick).astype(jnp.bfloat16)
    for cols in sides:
        k = turn(acc[1, :, cols]).astype(jnp.bfloat16)
        v = acc[2, :, cols].astype(jnp.bfloat16)
        keys.append(k)
        values.append(v)
        mixed = (nn(pick_k, k) + nn(pick_v, v)).astype(jnp.bfloat16)
        fresh[:, :, cols] = mixed.reshape(SEQ, 2, HD)

    own_kv.wait()
    all_of(KV.at[pl.ds(0, SEQ - 1)], kv_r)
    all_of(SK, sk_r)

    scale = float(HD) ** (-0.5)
    base = jnp.maximum(length - WINDOW, 0)
    spot = lax.broadcasted_iota(jnp.int32, (ROWS, SEQ * SLOTS * 2), 1)
    shard = lax.shift_right_logical(spot, 3)
    slot = lax.shift_right_logical(spot & 7, 1)
    first = lax.shift_right_logical(base - shard + (SEQ - 1), 6)
    place = (first + slot) * SEQ + shard
    valid = (
        ((spot & 1) == 0)
        & (place < length)
        & ((place < SINKS) | (place >= length - WINDOW))
    )
    spot_s = lax.broadcasted_iota(jnp.int32, (ROWS, 2 * SINKS), 1)
    valid_s = ((spot_s & 1) == 0) & (
        length - WINDOW > lax.shift_right_logical(spot_s, 1)
    )
    tree = reach > 0.5
    small = (2 * SINKS, 2 * SINKS)
    move = jnp.where(
        lax.broadcasted_iota(jnp.int32, small, 0) + 1
        == lax.broadcasted_iota(jnp.int32, small, 1),
        1.0, 0.0,
    ).astype(jnp.bfloat16)

    def send_fresh():
        own_g = pltpu.make_async_copy(fresh.at[me], G.at[me], own_sem.at[4])
        own_g.start()

        def hand(k, carry):
            t = lax.rem(me + k, SEQ)
            pltpu.make_async_remote_copy(
                src_ref=fresh.at[t], dst_ref=G.at[me], send_sem=gs, recv_sem=gr,
                device_id={"seq": t},
            ).start()
            return carry

        lax.fori_loop(1, SEQ, hand, 0)
        return own_g

    for h, cols in enumerate(sides):
        q = turn(acc[0, :, cols]).astype(jnp.bfloat16)
        k, v = keys[h], values[h]
        old = KV[:, :, cols].reshape(SEQ * SLOTS * 2, HD)
        old_s = SK[:, :, cols].reshape(2 * SINKS, HD)
        s = jnp.where(valid, nt(q, old) * scale, -1e30)
        s_s = jnp.where(valid_s, nt(q, old_s) * scale, -1e30)
        top = jnp.maximum(
            jnp.max(s, axis=-1, keepdims=True), jnp.max(s_s, axis=-1, keepdims=True)
        )
        w = jnp.where(valid, jnp.exp(s - top), 0.0)
        w_s = jnp.where(valid_s, jnp.exp(s_s - top), 0.0)
        total = jnp.sum(w, axis=-1, keepdims=True) + jnp.sum(
            w_s, axis=-1, keepdims=True
        )
        shifted = pltpu.roll(w, 1, 1).astype(jnp.bfloat16)
        shifted_s = nn(w_s.astype(jnp.bfloat16), move).astype(jnp.bfloat16)
        weighted = nn(shifted, old) + nn(shifted_s, old_s)
        t = jnp.where(tree, nt(q, k) * scale, -1e30)
        joint = jnp.maximum(top, jnp.max(t, axis=-1, keepdims=True))
        tw = jnp.where(tree, jnp.exp(t - joint), 0.0)
        ratio = jnp.exp(top - joint)
        summed = nn(tw.astype(jnp.bfloat16), v)
        below = total * ratio + jnp.sum(tw, axis=-1, keepdims=True)
        att[:, cols] = ((weighted * ratio + summed) / below).astype(jnp.bfloat16)
        if h == 0:
            own_g = send_fresh()

    all_of(WO.at[pl.ds(0, SEQ // CORES)], sib_rb)
    a = att[...]
    wide_group = SEQ // TP
    for k in range(1, TP + 1):
        t = lax.rem(tp + k, TP)
        right = WO[pl.ds(t * wide_group, wide_group)].reshape(WIDTH, WIDTH)
        part[t] = nt(a, right).astype(jnp.bfloat16)
        if k > 1:
            t = lax.rem(tp + k - 1, TP)
            pltpu.make_async_remote_copy(
                src_ref=part.at[t], dst_ref=PG.at[tp], send_sem=ps, recv_sem=pr,
                device_id={"tp": t},
            ).start()
    own_p = pltpu.make_async_copy(part.at[tp], PG.at[tp], own_sem.at[3])
    own_p.start()

    others = pl.ds(0, SEQ - 1)
    pieces = SEQ // CORES
    all_of(WQ.at[:, pl.ds(0, pieces - 1)], sa)
    all_of(WO.at[pl.ds(0, pieces - 1)], sb)
    all_of(WQ.at[:, pl.ds(0, pieces)], sib_sa)
    all_of(WO.at[pl.ds(0, pieces)], sib_sb)
    all_of(packed.at[others], kv_s)

    @pl.when(me < SINKS)
    def _():
        all_of(sinks.at[others], sk_s)

    own_cache.wait()
    own_g.wait()
    all_of(G.at[others], gr)
    arrived[...] = G[...]
    own_p.wait()
    all_of(PG.at[pl.ds(0, TP - 1)], pr)
    below = PG[0].astype(jnp.float32)
    for t in range(1, TP):
        below = below + PG[t].astype(jnp.float32)
    gathered[...] = below.astype(jnp.bfloat16)
    all_of(part.at[pl.ds(0, TP - 1)], ps)
    all_of(fresh.at[others], gs)


def final_kernel(deal, lengths, leaves, depth, G, cache, new_cache, sems):
    me = lax.axis_index("seq")

    def each(act):
        def place(i, carry):
            r = deal[i]
            length = lengths[r]
            offset = lax.rem(me - length + 8 * SEQ, SEQ)

            @pl.when(offset <= depth[r, leaves[r]])
            def _():
                spot = lax.shift_right_logical(length + offset, 6)
                act(pltpu.make_async_copy(G.at[i], new_cache.at[r, spot], sems.at[i]))

            return carry

        lax.fori_loop(0, ROWS, place, 0)

    each(lambda copy: copy.start())
    each(lambda copy: copy.wait())


def whole():
    return pl.BlockSpec(memory_space=pltpu.VMEM)


def shaped(shape, dtype=jnp.bfloat16):
    return jax.ShapeDtypeStruct(shape, dtype)


def run_whole(deal, lengths, leaves, tokens, parents, freq, cache, wq, wo):
    dma = pltpu.SemaphoreType.DMA
    vmem = pltpu.VMEM
    half = jnp.bfloat16
    return pl.pallas_call(
        whole_kernel,
        name="whole",
        in_specs=[pl.BlockSpec(memory_space=pltpu.SMEM)] * 3 + [whole()] * 6,
        out_specs=[whole()] * 3 + [pl.BlockSpec(memory_space=pl.ANY)],
        out_shape=[
            shaped((ROWS, WIDTH)),
            shaped((SEQ, 2, WIDTH)),
            shaped((ROWS, HD), jnp.int32),
            shaped(cache.shape),
        ],
        scratch_shapes=[
            vmem((SEQ, 2 * SLOTS, WIDTH), half),
            vmem((SEQ, 2, WIDTH), half),
            vmem((3, SEQ, DEEP // SEQ, WIDTH), half),
            vmem((SEQ, DEEP // SEQ, WIDTH), half),
            vmem((SEQ, 2 * SLOTS, WIDTH), half),
            vmem((SINKS, 2, WIDTH), half),
            vmem((ROWS, DEEP), half),
            vmem((3, ROWS, WIDTH), jnp.float32),
            vmem((ROWS, WIDTH), half),
            vmem((TP, ROWS, WIDTH), half),
            vmem((SEQ, 2, WIDTH), half),
            vmem((ROWS, HD), jnp.int32),
            vmem((SEQ, 2, WIDTH), half),
            vmem((TP, ROWS, WIDTH), half),
            dma((6,)), dma((X, Z)), dma((X, Z)),
            dma, dma, dma, dma, dma((X,)), dma,
            dma, dma, dma, dma, dma, dma, dma, dma,
        ],
        compiler_params=pltpu.CompilerParams(collective_id=0, has_side_effects=True),
    )(deal, lengths, leaves, tokens, parents, freq, cache, wq, wo)


def run_final(deal, lengths, leaves, depth, arrived, cache):
    return pl.pallas_call(
        final_kernel,
        name="final",
        grid_spec=pltpu.PrefetchScalarGridSpec(
            num_scalar_prefetch=4,
            in_specs=[whole(), pl.BlockSpec(memory_space=pl.ANY)],
            out_specs=pl.BlockSpec(memory_space=pl.ANY),
            scratch_shapes=[pltpu.SemaphoreType.DMA((ROWS,))],
        ),
        out_shape=shaped(cache.shape),
        input_output_aliases={5: 0},
    )(deal, lengths, leaves, depth, arrived, cache)


def on_device(tokens, qkv_weight, out_weight, kv_cache, lengths, parents, leaves, deal):
    cache = kv_cache.reshape(kv_cache.shape[0], kv_cache.shape[1], 2, WIDTH)
    half = HD // 2
    freq = 10000.0 ** (-2.0 * jnp.arange(half, dtype=jnp.float32) / HD)
    freq = jnp.concatenate([freq, freq])[None, :]
    wq = jnp.transpose(qkv_weight, (1, 0, 2))
    wo = jnp.transpose(out_weight, (1, 0))
    branch, arrived, depth, copied = run_whole(
        deal, lengths, leaves, tokens, parents, freq, cache, wq, wo
    )
    new_cache = run_final(deal, lengths, leaves, depth, arrived, copied)
    return branch, new_cache.reshape(kv_cache.shape)


def solution(mesh):
    placed = (
        P("seq", None),
        P("seq", None, "tp"),
        P("tp", "seq"),
        P(None, None, "seq", None, "tp"),
        P(),
        P(),
        P(),
        P(),
    )
    return jax.shard_map(
        on_device,
        mesh=mesh,
        in_specs=placed,
        out_specs=(P("seq", "tp"), P(None, None, "seq", None, "tp")),
        check_vma=False,
    )
```

```python
import functools

import jax
import jax.numpy as jnp
import numpy as np
from jax import lax
from jax.experimental import pallas as pl
from jax.experimental.pallas import tpu as pltpu
from jax.sharding import PartitionSpec as P

HD = 128
SINKS = 4
X, Z, CORES = 4, 8, 2
SEQ = X * Z * CORES
TP = 4
ROWS = 64
SLOTS = 4
WIDTH = 512
HEADS = WIDTH // HD
WINDOW = 256
DEEP = 2048
PROJ_AT = (10, 12, 14)
KV_PARTS = tuple((low, min(low + 8, SEQ)) for low in range(1, SEQ, 8))
KV_AT = (7.1, 8.1, 8.8, 9.4, 10.1, 10.8, 11.1, 11.6)


def nt(a, b):
    return lax.dot_general(
        a, b, (((1,), (1,)), ((), ())), preferred_element_type=jnp.float32
    )


def nn(a, b):
    return lax.dot_general(
        a, b, (((1,), (0,)), ((), ())), preferred_element_type=jnp.float32
    )


def whole_kernel(
    deal, lengths, leaves, tokens, parents, freq, spans, tips, cache, wq, wo,
    gathered, arrived, code_out,
    packed, sinks, WQ, WO, KV, SK, normed, acc, att, part, fresh, par_pad, G, PG,
    own_sem, ra, rb, sa, sb, sib_sa, sib_sb, sib_ra, sib_rb,
    kv_s, kv_r, sk_s, sk_r, ps, pr, gs, gr,
):
    me = lax.axis_index("seq")
    tp = lax.axis_index("tp")
    x = me // (Z * CORES)
    z = lax.rem(me // CORES, Z)
    c = lax.rem(me, CORES)

    def idx(dx, dz):
        return (
            lax.rem(x + (dx + X), X) * Z + lax.rem(z + (dz + Z), Z)
        ) * CORES + c

    barrier = pltpu.get_barrier_semaphore()

    def greet(k, carry):
        pl.semaphore_signal(barrier, 1, device_id={"seq": lax.rem(me + k, SEQ)})
        return carry

    lax.fori_loop(1, SEQ, greet, 0)
    for k in range(1, TP):
        pl.semaphore_signal(barrier, 1, device_id={"tp": lax.rem(tp + k, TP)})

    own_a = pltpu.make_async_copy(wq, WQ.at[:, me], own_sem.at[0])
    own_b = pltpu.make_async_copy(wo, WO.at[me], own_sem.at[1])
    own_a.start()
    own_b.start()

    def pack(t, carry):
        r = deal[t]
        base = jnp.maximum(lengths[r] - WINDOW, 0)
        first = lax.shift_right_logical(base - me + (SEQ - 1), 6)
        packed[t] = cache[r, pl.ds(first, SLOTS)].reshape(2 * SLOTS, WIDTH)
        sinks[t] = cache[r, 0]
        return carry

    lax.fori_loop(0, ROWS, pack, 0)

    wide = tokens[...].astype(jnp.float32)
    centred = wide - jnp.mean(wide, axis=-1, keepdims=True)
    scaling = lax.rsqrt(jnp.mean(centred * centred, axis=-1, keepdims=True) + 1e-05)
    normed[...] = (centred * scaling).astype(jnp.bfloat16)
    acc[...] = jnp.zeros_like(acc)

    pl.semaphore_wait(barrier, SEQ + TP - 2)

    sibling = me + 1 - 2 * c
    to = {
        "x+": {"seq": idx(1, 0)},
        "x-": {"seq": idx(-1, 0)},
        "z+": {"seq": idx(0, 1)},
        "z-": {"seq": idx(0, -1)},
        "s": {"seq": sibling},
    }
    shift = {"x+": (-1, 0), "x-": (1, 0), "z+": (0, -1), "z-": (0, 1)}

    def send_a(dx, dz, way):
        at = idx(dx, dz)
        src = wq if (dx, dz) == (0, 0) else WQ.at[:, at]
        if way == "s":
            send, recv = sib_sa, sib_ra.at[dx % X]
        else:
            ox, oz = shift[way]
            send, recv = sa, ra.at[(dx + ox) % X, (dz + oz) % Z]
        pltpu.make_async_remote_copy(
            src_ref=src, dst_ref=WQ.at[:, at], send_sem=send, recv_sem=recv,
            device_id=to[way],
        ).start()

    def send_b(dx, dz, way):
        at = idx(dx, dz)
        src = wo if (dx, dz) == (0, 0) else WO.at[at]
        if way == "s":
            send, recv = sib_sb, sib_rb
        else:
            ox, oz = shift[way]
            send, recv = sb, rb.at[(dx + ox) % X, (dz + oz) % Z]
        pltpu.make_async_remote_copy(
            src_ref=src, dst_ref=WO.at[at], send_sem=send, recv_sem=recv,
            device_id=to[way],
        ).start()

    def wait_a(dx, dz):
        at = idx(dx, dz)
        pltpu.make_async_copy(
            WQ.at[:, at], WQ.at[:, at], ra.at[dx % X, dz % Z]
        ).wait()

    def wait_b(dx, dz):
        at = idx(dx, dz)
        pltpu.make_async_copy(WO.at[at], WO.at[at], rb.at[dx % X, dz % Z]).wait()

    def route_a(dx, dz):
        out = []
        if dx == 0:
            if dz == 0:
                out += ["z+", "z-"]
            elif -4 < dz < 0:
                out += ["z+"]
            elif 0 < dz < 3:
                out += ["z-"]
            out += ["x+", "x-"]
        elif dx == -1 and dz % 2 == 0:
            out += ["x+"]
        elif dx == 1 and dz % 2 == 1:
            out += ["x-"]
        return out + ["s"]

    def route_b(dx, dz):
        out = []
        if dz == 0:
            if dx == 0:
                out += ["x+", "x-"]
            elif dx == -1:
                out += ["x+"]
            out += ["z+", "z-"]
        else:
            far = 4 if dx % 2 == 0 else 3
            if -far < dz < 0:
                out += ["z+"]
            elif 0 < dz < 7 - far:
                out += ["z-"]
        return out + ["s"]

    def all_of(ref, sem):
        pltpu.make_async_copy(ref, ref, sem).wait()

    for way in route_a(0, 0):
        send_a(0, 0, way)
    for way in route_b(0, 0):
        send_b(0, 0, way)
    own_kv = pltpu.make_async_copy(packed.at[me], KV.at[me], own_sem.at[2])
    own_kv.start()

    def scatter(k, carry):
        t = lax.rem(me + k, SEQ)
        pltpu.make_async_remote_copy(
            src_ref=packed.at[t], dst_ref=KV.at[me], send_sem=kv_s, recv_sem=kv_r,
            device_id={"seq": t},
        ).start()
        return carry

    @pl.when(me < SINKS)
    def _():
        pltpu.make_async_copy(sinks.at[me], SK.at[me], sk_r).start()

        def spread(k, carry):
            t = lax.rem(me + k, SEQ)
            pltpu.make_async_remote_copy(
                src_ref=sinks.at[t], dst_ref=SK.at[me], send_sem=sk_s, recv_sem=sk_r,
                device_id={"seq": t},
            ).start()
            return carry

        lax.fori_loop(1, SEQ, spread, 0)

    request = deal[me]
    length = lengths[request]
    leaf = leaves[request]
    sub = lax.broadcasted_iota(jnp.int32, (ROWS, ROWS), 0)
    lane = lax.broadcasted_iota(jnp.int32, (ROWS, ROWS), 1)
    eye = jnp.where(sub == lane, 1.0, 0.0)
    row = parents[pl.ds(request, 1), :]
    up = eye + jnp.where(row == sub, 1.0, 0.0)
    for _ in range(6):
        half = up.astype(jnp.bfloat16)
        up = jnp.minimum(nn(half, half), 1.0)
    reach = nt(eye.astype(jnp.bfloat16), up.astype(jnp.bfloat16))
    depth_row = (jnp.sum(up, axis=0, keepdims=True) - 1.0).astype(jnp.int32)
    depth_col = (jnp.sum(reach, axis=1, keepdims=True) - 1.0).astype(jnp.int32)
    places = (length + depth_col).astype(jnp.float32)
    angle = places * freq[...]
    cosine = jnp.cos(angle)
    wave = jnp.sin(angle)
    lanes = lax.broadcasted_iota(jnp.int32, (ROWS, HD), 1)
    sine = jnp.where(lanes < HD // 2, -wave, wave)
    on_path = jnp.sum(jnp.where(sub == leaf, reach, 0.0), axis=0, keepdims=True)
    offset = lax.rem(sub - length + 8 * SEQ, SEQ)
    hit = (on_path > 0.5) & (depth_row == offset)
    pick = jnp.where(hit, 1.0, 0.0).astype(jnp.bfloat16)

    par_pad[...] = lanes
    par_pad[:, 0:ROWS] = parents[...]
    par = par_pad[...]
    climb = jnp.where((lanes < ROWS) & (par >= 0), 1, 0)
    jump = jnp.where(par < 0, 0, par)
    for _ in range(6):
        climb = climb + jnp.take_along_axis(climb, jump, axis=1)
        jump = jnp.take_along_axis(jump, jump, axis=1)
    tip = jnp.sum(jnp.where(sub == lane, tips[...], 0), axis=1, keepdims=True)
    span = jnp.sum(jnp.where(sub == lane, spans[...], 0), axis=1, keepdims=True)
    end = jnp.sum(jnp.where(lanes == tip, climb, 0), axis=1, keepdims=True)
    ahead = (me - span + 8 * SEQ) & (SEQ - 1)
    code = jnp.where(
        ahead <= end, lax.shift_right_logical(span + ahead, 6), -1
    )
    code_out[...] = jnp.sum(jnp.where(sub == lane, code, 0), axis=0, keepdims=True)

    own_a.wait()
    own_b.wait()
    group = Z * CORES
    deep = group * (DEEP // SEQ)

    def project(dx, kind):
        block = lax.rem(x + (dx + X), X)
        left = normed[:, pl.ds(pl.multiple_of(block * deep, deep), deep)]
        right = WQ[kind, pl.ds(block * group, group)].reshape(deep, WIDTH)
        acc[kind] += nn(left, right)

    steps = []
    for dz in (-1, 1, -2, 2, -3, 3, -4):
        steps.append((2 * abs(dz), "a", 0, dz))
    for dx, cost in ((-1, 1), (1, 1), (-2, 2)):
        steps.append((2 * cost + 0.2, "b", dx, 0))
    for dz in (0, -1, 1, -2, 2, -3, 3, -4):
        for dx, cost in ((-1, 1), (1, 1), (-2, 2)):
            steps.append((2 * abs(dz) + 2 * cost + 0.5, "a", dx, dz))
    for dx in (0, -1, 1, -2):
        far = 4 if dx % 2 == 0 else 3
        for dz in list(range(-far, 0)) + list(range(1, 8 - far)):
            steps.append((2 * abs(dx) + 2 * abs(dz) + 0.6, "b", dx, dz))
    for turn, (low, high) in enumerate(KV_PARTS):
        steps.append((KV_AT[turn], "k", low, high))
    for turn, dx in enumerate((0, -1, 1)):
        for kind in range(3):
            steps.append((PROJ_AT[turn] + 0.7 + 0.01 * kind, "p", dx, kind))
    for _, kind, dx, dz in sorted(steps, key=lambda s: s[0]):
        if kind == "a":
            wait_a(dx, dz)
            for way in route_a(dx, dz):
                send_a(dx, dz, way)
        elif kind == "b":
            wait_b(dx, dz)
            for way in route_b(dx, dz):
                send_b(dx, dz, way)
        elif kind == "k":
            lax.fori_loop(dx, dz, scatter, 0)
        else:
            if dz == 0:
                all_of(WQ.at[:, pl.ds(0, Z)], sib_ra.at[dx % X])
            project(dx, dz)

    all_of(WQ.at[:, pl.ds(0, Z)], sib_ra.at[2])
    for kind in range(3):
        project(2, kind)

    def turn(v):
        return v * cosine + pltpu.roll(v, HD // 2, 1) * sine

    sides = [slice(h * HD, (h + 1) * HD) for h in range(HEADS)]
    keys, values = [], []
    twice = lax.broadcasted_iota(jnp.int32, (2 * SEQ, SEQ), 0)
    once = lax.broadcasted_iota(jnp.int32, (2 * SEQ, SEQ), 1)
    even = jnp.where(twice == 2 * once, 1.0, 0.0).astype(jnp.bfloat16)
    odd = jnp.where(twice == 2 * once + 1, 1.0, 0.0).astype(jnp.bfloat16)
    pick_k = nn(even, pick).astype(jnp.bfloat16)
    pick_v = nn(odd, pick).astype(jnp.bfloat16)
    for cols in sides:
        k = turn(acc[1, :, cols]).astype(jnp.bfloat16)
        v = acc[2, :, cols].astype(jnp.bfloat16)
        keys.append(k)
        values.append(v)
        mixed = (nn(pick_k, k) + nn(pick_v, v)).astype(jnp.bfloat16)
        fresh[:, :, cols] = mixed.reshape(SEQ, 2, HD)

    own_kv.wait()
    all_of(KV.at[pl.ds(0, SEQ - 1)], kv_r)
    all_of(SK, sk_r)

    scale = float(HD) ** (-0.5)
    base = jnp.maximum(length - WINDOW, 0)
    spot = lax.broadcasted_iota(jnp.int32, (ROWS, SEQ * SLOTS * 2), 1)
    shard = lax.shift_right_logical(spot, 3)
    slot = lax.shift_right_logical(spot & 7, 1)
    first = lax.shift_right_logical(base - shard + (SEQ - 1), 6)
    place = (first + slot) * SEQ + shard
    valid = (
        ((spot & 1) == 0)
        & (place < length)
        & ((place < SINKS) | (place >= length - WINDOW))
    )
    spot_s = lax.broadcasted_iota(jnp.int32, (ROWS, 2 * SINKS), 1)
    valid_s = ((spot_s & 1) == 0) & (
        length - WINDOW > lax.shift_right_logical(spot_s, 1)
    )
    tree = reach > 0.5
    small = (2 * SINKS, 2 * SINKS)
    move = jnp.where(
        lax.broadcasted_iota(jnp.int32, small, 0) + 1
        == lax.broadcasted_iota(jnp.int32, small, 1),
        1.0, 0.0,
    ).astype(jnp.bfloat16)

    def send_fresh():
        own_g = pltpu.make_async_copy(fresh.at[me], G.at[me], own_sem.at[4])
        own_g.start()

        def hand(k, carry):
            t = lax.rem(me + k, SEQ)
            pltpu.make_async_remote_copy(
                src_ref=fresh.at[t], dst_ref=G.at[me], send_sem=gs, recv_sem=gr,
                device_id={"seq": t},
            ).start()
            return carry

        lax.fori_loop(1, SEQ, hand, 0)
        return own_g

    for h, cols in enumerate(sides):
        q = turn(acc[0, :, cols]).astype(jnp.bfloat16)
        k, v = keys[h], values[h]
        old = KV[:, :, cols].reshape(SEQ * SLOTS * 2, HD)
        old_s = SK[:, :, cols].reshape(2 * SINKS, HD)
        s = jnp.where(valid, nt(q, old) * scale, -1e30)
        s_s = jnp.where(valid_s, nt(q, old_s) * scale, -1e30)
        top = jnp.maximum(
            jnp.max(s, axis=-1, keepdims=True), jnp.max(s_s, axis=-1, keepdims=True)
        )
        w = jnp.where(valid, jnp.exp(s - top), 0.0)
        w_s = jnp.where(valid_s, jnp.exp(s_s - top), 0.0)
        total = jnp.sum(w, axis=-1, keepdims=True) + jnp.sum(
            w_s, axis=-1, keepdims=True
        )
        shifted = pltpu.roll(w, 1, 1).astype(jnp.bfloat16)
        shifted_s = nn(w_s.astype(jnp.bfloat16), move).astype(jnp.bfloat16)
        weighted = nn(shifted, old) + nn(shifted_s, old_s)
        t = jnp.where(tree, nt(q, k) * scale, -1e30)
        joint = jnp.maximum(top, jnp.max(t, axis=-1, keepdims=True))
        tw = jnp.where(tree, jnp.exp(t - joint), 0.0)
        ratio = jnp.exp(top - joint)
        summed = nn(tw.astype(jnp.bfloat16), v)
        below = total * ratio + jnp.sum(tw, axis=-1, keepdims=True)
        att[:, cols] = ((weighted * ratio + summed) / below).astype(jnp.bfloat16)
        if h == 0:
            own_g = send_fresh()

    all_of(WO.at[pl.ds(0, SEQ // CORES)], sib_rb)
    a = att[...]
    wide_group = SEQ // TP
    for k in range(1, TP + 1):
        t = lax.rem(tp + k, TP)
        right = WO[pl.ds(t * wide_group, wide_group)].reshape(WIDTH, WIDTH)
        part[t] = nt(a, right).astype(jnp.bfloat16)
        if k > 1:
            t = lax.rem(tp + k - 1, TP)
            pltpu.make_async_remote_copy(
                src_ref=part.at[t], dst_ref=PG.at[tp], send_sem=ps, recv_sem=pr,
                device_id={"tp": t},
            ).start()
    own_p = pltpu.make_async_copy(part.at[tp], PG.at[tp], own_sem.at[3])
    own_p.start()

    others = pl.ds(0, SEQ - 1)
    pieces = SEQ // CORES
    all_of(WQ.at[:, pl.ds(0, pieces - 1)], sa)
    all_of(WO.at[pl.ds(0, pieces - 1)], sb)
    all_of(WQ.at[:, pl.ds(0, pieces)], sib_sa)
    all_of(WO.at[pl.ds(0, pieces)], sib_sb)
    all_of(packed.at[others], kv_s)

    @pl.when(me < SINKS)
    def _():
        all_of(sinks.at[others], sk_s)

    own_g.wait()
    all_of(G.at[others], gr)
    arrived[...] = G[...]
    own_p.wait()
    all_of(PG.at[pl.ds(0, TP - 1)], pr)
    below = PG[0].astype(jnp.float32)
    for t in range(1, TP):
        below = below + PG[t].astype(jnp.float32)
    gathered[...] = below.astype(jnp.bfloat16)
    all_of(part.at[pl.ds(0, TP - 1)], ps)
    all_of(fresh.at[others], gs)


def final_kernel(deal, code, G, cache, new_cache, sem):
    copy = pltpu.make_async_copy(cache, new_cache, sem)
    copy.start()
    copy.wait()

    def place(i, carry):
        r = deal[i]
        spot = code[0, r]

        @pl.when(spot >= 0)
        def _():
            new_cache[r, spot] = G[i]

        return carry

    lax.fori_loop(0, ROWS, place, 0, unroll=8)


def whole():
    return pl.BlockSpec(memory_space=pltpu.VMEM)


def shaped(shape, dtype=jnp.bfloat16):
    return jax.ShapeDtypeStruct(shape, dtype)


def run_whole(deal, lengths, leaves, tokens, parents, freq, spans, tips, cache, wq, wo):
    dma = pltpu.SemaphoreType.DMA
    vmem = pltpu.VMEM
    half = jnp.bfloat16
    return pl.pallas_call(
        whole_kernel,
        name="whole",
        in_specs=[pl.BlockSpec(memory_space=pltpu.SMEM)] * 3 + [whole()] * 8,
        out_specs=[whole()] * 3,
        out_shape=[
            shaped((ROWS, WIDTH)),
            shaped((SEQ, 2, WIDTH)),
            shaped((1, ROWS), jnp.int32),
        ],
        scratch_shapes=[
            vmem((SEQ, 2 * SLOTS, WIDTH), half),
            vmem((SEQ, 2, WIDTH), half),
            vmem((3, SEQ, DEEP // SEQ, WIDTH), half),
            vmem((SEQ, DEEP // SEQ, WIDTH), half),
            vmem((SEQ, 2 * SLOTS, WIDTH), half),
            vmem((SINKS, 2, WIDTH), half),
            vmem((ROWS, DEEP), half),
            vmem((3, ROWS, WIDTH), jnp.float32),
            vmem((ROWS, WIDTH), half),
            vmem((TP, ROWS, WIDTH), half),
            vmem((SEQ, 2, WIDTH), half),
            vmem((ROWS, HD), jnp.int32),
            vmem((SEQ, 2, WIDTH), half),
            vmem((TP, ROWS, WIDTH), half),
            dma((6,)), dma((X, Z)), dma((X, Z)),
            dma, dma, dma, dma, dma((X,)), dma,
            dma, dma, dma, dma, dma, dma, dma, dma,
        ],
        compiler_params=pltpu.CompilerParams(collective_id=0, has_side_effects=True),
    )(deal, lengths, leaves, tokens, parents, freq, spans, tips, cache, wq, wo)


def run_final(deal, code, arrived, cache):
    return pl.pallas_call(
        final_kernel,
        name="final",
        grid_spec=pltpu.PrefetchScalarGridSpec(
            num_scalar_prefetch=2,
            in_specs=[whole(), pl.BlockSpec(memory_space=pl.ANY)],
            out_specs=whole(),
            scratch_shapes=[pltpu.SemaphoreType.DMA],
        ),
        out_shape=shaped(cache.shape),
    )(deal, code, arrived, cache)


def on_device(tokens, qkv_weight, out_weight, kv_cache, lengths, parents, leaves, deal):
    cache = kv_cache.reshape(kv_cache.shape[0], kv_cache.shape[1], 2, WIDTH)
    half = np.arange(HD, dtype=np.float64) % (HD // 2)
    freq = jnp.asarray((10000.0 ** (-2.0 * half / HD)).astype(np.float32)[None, :])
    wq = jnp.transpose(qkv_weight, (1, 0, 2))
    wo = jnp.transpose(out_weight, (1, 0))
    branch, arrived, code = run_whole(
        deal, lengths, leaves, tokens, parents, freq,
        lengths.reshape(1, ROWS), leaves.reshape(1, ROWS), cache, wq, wo,
    )
    new_cache = run_final(deal, code, arrived, cache)
    return branch, new_cache.reshape(kv_cache.shape)


def solution(mesh):
    placed = (
        P("seq", None),
        P("seq", None, "tp"),
        P("tp", "seq"),
        P(None, None, "seq", None, "tp"),
        P(),
        P(),
        P(),
        P(),
    )
    return jax.shard_map(
        on_device,
        mesh=mesh,
        in_specs=placed,
        out_specs=(P("seq", "tp"), P(None, None, "seq", None, "tp")),
        check_vma=False,
    )
```

```python
import functools

import jax
import jax.numpy as jnp
import numpy as np
from jax import lax
from jax.experimental import pallas as pl
from jax.experimental.pallas import tpu as pltpu
from jax.sharding import PartitionSpec as P

HD = 128
SINKS = 4
X, Z, CORES = 4, 8, 2
SEQ = X * Z * CORES
TP = 4
COLUMN = Z * CORES
ROWS = 64
SLOTS = 4
WIDTH = 512
HEADS = WIDTH // HD
WINDOW = 256
DEEP = 2048
KV_PARTS = ((1, 16), (16, 28), (28, 40), (40, 52), (52, 64))


def nt(a, b):
    return lax.dot_general(
        a, b, (((1,), (1,)), ((), ())), preferred_element_type=jnp.float32
    )


def nn(a, b):
    return lax.dot_general(
        a, b, (((1,), (0,)), ((), ())), preferred_element_type=jnp.float32
    )


def whole_kernel(
    deal, lengths, leaves, tokens, parents, freq, spans, tips, cache, wq, wo,
    gathered, arrived, code_out,
    packed, sinks, N, WH, WO, KV, SK, acc, att, ATT, part, PG, fresh, G, par_pad,
    own_sem, tr, wr, br,
    t_s, wx_s, wx_r, w_s, wsib_s, wsib_r, b_s, bsib_s, bsib_r,
    kv_s, kv_r, sk_s, sk_r, a_s, a_r, ps, pr, gs, gr,
):
    me = lax.axis_index("seq")
    tp = lax.axis_index("tp")
    x = me // COLUMN
    z = lax.rem(me // CORES, Z)
    c = lax.rem(me, CORES)
    column = lax.rem(me, COLUMN)

    def xat(dx):
        return lax.rem(x + (dx + X), X)

    def qat(dz):
        return lax.rem(z + (dz + Z), Z) * CORES + c

    def idx(dx, dz):
        return xat(dx) * COLUMN + qat(dz)

    def side(h):
        return pl.ds(pl.multiple_of(h * HD, HD), HD)

    def all_of(ref, sem):
        pltpu.make_async_copy(ref, ref, sem).wait()

    def send(src, dst, there, here, target):
        pltpu.make_async_remote_copy(
            src_ref=src, dst_ref=dst, send_sem=there, recv_sem=here,
            device_id={"seq": target},
        ).start()

    barrier = pltpu.get_barrier_semaphore()

    def greet(k, carry):
        pl.semaphore_signal(barrier, 1, device_id={"seq": lax.rem(me + k, SEQ)})
        return carry

    lax.fori_loop(1, SEQ, greet, 0)
    for k in range(1, TP):
        pl.semaphore_signal(barrier, 1, device_id={"tp": lax.rem(tp + k, TP)})

    own_w = pltpu.make_async_copy(
        wq.at[:, :, side(x)], WH.at[:, x, column], own_sem.at[0]
    )
    own_w.start()
    own_b = pltpu.make_async_copy(wo, WO.at[me], own_sem.at[1])
    own_b.start()

    wide = tokens[...].astype(jnp.float32)
    centred = wide - jnp.mean(wide, axis=-1, keepdims=True)
    scaling = lax.rsqrt(jnp.mean(centred * centred, axis=-1, keepdims=True) + 1e-05)
    N[x] = (centred * scaling).astype(jnp.bfloat16)

    def pack(t, carry):
        r = deal[t]
        base = jnp.maximum(lengths[r] - WINDOW, 0)
        first = lax.shift_right_logical(base - me + (SEQ - 1), 6)
        rows = cache[r, pl.ds(first, SLOTS)].reshape(2 * SLOTS, WIDTH)
        sunk = cache[r, 0]
        far, near = t // COLUMN, lax.rem(t, COLUMN)
        for h in range(HEADS):
            packed[h * COLUMN + near, far] = rows[:, h * HD:(h + 1) * HD]
            sinks[h * COLUMN + near, far] = sunk[:, h * HD:(h + 1) * HD]
        return carry

    lax.fori_loop(0, ROWS, pack, 0)

    pl.semaphore_wait(barrier, SEQ + TP - 2)

    for k in (2, 1, 3):
        send(
            wq.at[:, :, side(xat(k))], WH.at[:, x, column], wx_s, wx_r, idx(k, 0)
        )
    send(N.at[x], N.at[x], t_s, tr.at[0], idx(1, 0))
    send(N.at[x], N.at[x], t_s, tr.at[1], idx(-1, 0))

    own_kv = pltpu.make_async_copy(packed.at[me], KV.at[me], own_sem.at[2])
    own_kv.start()

    def scatter(low, high):
        def one(k, carry):
            t = lax.rem(me + k, SEQ)
            send(packed.at[t], KV.at[me], kv_s, kv_r, t)
            return carry

        lax.fori_loop(low, high, one, 0)

    scatter(*KV_PARTS[0])

    sub = lax.broadcasted_iota(jnp.int32, (ROWS, ROWS), 0)
    lane = lax.broadcasted_iota(jnp.int32, (ROWS, ROWS), 1)
    lanes = lax.broadcasted_iota(jnp.int32, (ROWS, HD), 1)
    eye = jnp.where(sub == lane, 1.0, 0.0)

    def describe(k):
        request = deal[xat(k) * COLUMN + column]
        length = lengths[request]
        leaf = leaves[request]
        row = parents[pl.ds(request, 1), :]
        up = eye + jnp.where(row == sub, 1.0, 0.0)
        for _ in range(6):
            half = up.astype(jnp.bfloat16)
            up = jnp.minimum(nn(half, half), 1.0)
        reach = nt(eye.astype(jnp.bfloat16), up.astype(jnp.bfloat16))
        depth_row = (jnp.sum(up, axis=0, keepdims=True) - 1.0).astype(jnp.int32)
        depth_col = (jnp.sum(reach, axis=1, keepdims=True) - 1.0).astype(jnp.int32)
        angle = (length + depth_col).astype(jnp.float32) * freq[...]
        cosine = jnp.cos(angle)
        wave = jnp.sin(angle)
        sine = jnp.where(lanes < HD // 2, -wave, wave)
        on_path = jnp.sum(jnp.where(sub == leaf, reach, 0.0), axis=0, keepdims=True)
        offset = lax.rem(sub - length + 8 * SEQ, SEQ)
        hit = (on_path > 0.5) & (depth_row == offset)
        pick = jnp.where(hit, 1.0, 0.0).astype(jnp.bfloat16)
        return length, reach, cosine, sine, pick

    def table():
        par_pad[...] = lanes
        par_pad[:, 0:ROWS] = parents[...]
        par = par_pad[...]
        climb = jnp.where((lanes < ROWS) & (par >= 0), 1, 0)
        jump = jnp.where(par < 0, 0, par)
        for _ in range(6):
            climb = climb + jnp.take_along_axis(climb, jump, axis=1)
            jump = jnp.take_along_axis(jump, jump, axis=1)
        tip = jnp.sum(jnp.where(sub == lane, tips[...], 0), axis=1, keepdims=True)
        span = jnp.sum(jnp.where(sub == lane, spans[...], 0), axis=1, keepdims=True)
        end = jnp.sum(jnp.where(lanes == tip, climb, 0), axis=1, keepdims=True)
        ahead = (me - span + 8 * SEQ) & (SEQ - 1)
        code = jnp.where(
            ahead <= end, lax.shift_right_logical(span + ahead, 6), -1
        )
        code_out[...] = jnp.sum(
            jnp.where(sub == lane, code, 0), axis=0, keepdims=True
        )

    def send_w(dz, step):
        at = WH.at[:, :, qat(dz)]
        if step == 0:
            send(at, at, wsib_s, wsib_r, me + 1 - 2 * c)
        else:
            send(at, at, w_s, wr.at[(dz - step) % Z], idx(0, step))

    def hop_w(dz):
        at = WH.at[:, :, qat(dz)]
        all_of(at, wr.at[dz % Z])
        if -4 < dz < 0:
            send_w(dz, 1)
        elif 0 < dz < 3:
            send_w(dz, -1)
        send_w(dz, 0)

    def send_b(dx, dz, way):
        at = idx(dx, dz)
        src = wo if (dx, dz) == (0, 0) else WO.at[at]
        if way == "s":
            send(src, WO.at[at], bsib_s, bsib_r, me + 1 - 2 * c)
        else:
            ox, oz = {"x+": (1, 0), "x-": (-1, 0), "z+": (0, 1), "z-": (0, -1)}[way]
            send(
                src, WO.at[at], b_s, br.at[(dx - ox) % X, (dz - oz) % Z], idx(ox, oz)
            )

    def hop_b(dx, dz):
        if (dx, dz) != (0, 0):
            all_of(WO.at[idx(dx, dz)], br.at[dx % X, dz % Z])
        out = []
        if dx == 0:
            if dz == 0:
                out += ["z+", "z-"]
            elif -4 < dz < 0:
                out += ["z+"]
            elif 0 < dz < 3:
                out += ["z-"]
            out += ["x+", "x-"]
        elif dx == -1 and dz % 2 == 0:
            out += ["x+"]
        elif dx == 1 and dz % 2 == 1:
            out += ["x-"]
        for way in out + ["s"]:
            send_b(dx, dz, way)

    order = (2, 1, 3, 0)
    told = {order[0]: describe(order[0])}

    own_w.wait()
    all_of(WH.at[:, pl.ds(0, X - 1), 0], wx_r)
    send_w(0, 1)
    send_w(0, -1)
    send_w(0, 0)
    scatter(*KV_PARTS[1])
    told[order[1]] = describe(order[1])

    left, right = pl.ds(0, DEEP // 2), pl.ds(DEEP // 2, DEEP // 2)
    all_of(N.at[0], tr.at[0])
    at = N.at[xat(-1), :, left]
    send(at, at, t_s, tr.at[2], idx(1, 0))
    all_of(N.at[0], tr.at[1])
    at = N.at[xat(1), :, right]
    send(at, at, t_s, tr.at[3], idx(-1, 0))

    hop_w(-1)
    hop_w(1)
    scatter(*KV_PARTS[2])

    @pl.when(me < SINKS)
    def _():
        pltpu.make_async_copy(sinks.at[me], SK.at[me], sk_r).start()

        def spread(k, carry):
            t = lax.rem(me + k, SEQ)
            send(sinks.at[t], SK.at[me], sk_s, sk_r, t)
            return carry

        lax.fori_loop(1, SEQ, spread, 0)

    told[order[2]] = describe(order[2])
    hop_w(-2)
    hop_w(2)
    scatter(*KV_PARTS[3])
    told[order[3]] = describe(order[3])
    hop_w(-3)
    hop_w(3)
    scatter(*KV_PARTS[4])
    own_b.wait()
    hop_b(0, 0)
    table()
    hop_w(-4)

    all_of(N.at[0, :, left], tr.at[2])
    all_of(N.at[0, :, right], tr.at[3])
    hop_b(0, -1)
    hop_b(0, 1)
    all_of(WH.at[:, :, pl.ds(0, Z)], wsib_r)
    deep = COLUMN * (DEEP // SEQ)
    rows_all = X * ROWS
    for kind in range(3):
        total = None
        for block in range(X):
            mine = N[:, :, block * deep:(block + 1) * deep].reshape(rows_all, deep)
            term = nn(mine, WH[kind, block].reshape(deep, HD))
            total = term if total is None else total + term
        acc[kind] = total
        if kind == 0:
            hop_b(0, -2)
            hop_b(0, 2)

    twice = lax.broadcasted_iota(jnp.int32, (2 * SEQ, SEQ), 0)
    once = lax.broadcasted_iota(jnp.int32, (2 * SEQ, SEQ), 1)
    even = jnp.where(twice == 2 * once, 1.0, 0.0).astype(jnp.bfloat16)
    odd = jnp.where(twice == 2 * once + 1, 1.0, 0.0).astype(jnp.bfloat16)

    def block_rows(kind, k):
        return acc[kind, pl.ds(pl.multiple_of(xat(k) * ROWS, ROWS), ROWS)]

    keys, values = {}, {}
    for k in order:
        _, _, cosine, sine, pick = told[k]
        key = block_rows(1, k)
        key = key * cosine + pltpu.roll(key, HD // 2, 1) * sine
        keys[k] = key.astype(jnp.bfloat16)
        values[k] = block_rows(2, k).astype(jnp.bfloat16)
        pick_k = nn(even, pick).astype(jnp.bfloat16)
        pick_v = nn(odd, pick).astype(jnp.bfloat16)
        mixed = (nn(pick_k, keys[k]) + nn(pick_v, values[k])).astype(jnp.bfloat16)
        fresh[:, xat(k)] = mixed.reshape(SEQ, 2, HD)
    hop_b(0, -3)
    hop_b(0, 3)

    own_g = pltpu.make_async_copy(fresh.at[me], G.at[me], own_sem.at[4])
    own_g.start()

    def hand(k, carry):
        t = lax.rem(me + k, SEQ)
        send(fresh.at[t], G.at[me], gs, gr, t)
        return carry

    lax.fori_loop(1, SEQ, hand, 0)

    later = [(dx, dz) for dz in (0, -1, 1, -2, 2, -3, 3, -4) for dx in (-1, 1)]
    later.insert(8, (0, -4))
    parts = [later[0:4], later[4:9], later[9:13], later[13:17]]

    own_kv.wait()
    all_of(KV.at[pl.ds(0, SEQ - 1)], kv_r)
    all_of(SK, sk_r)

    scale = float(HD) ** (-0.5)
    spot = lax.broadcasted_iota(jnp.int32, (ROWS, SEQ * SLOTS * 2), 1)
    shard = lax.shift_right_logical(spot, 3)
    slot = lax.shift_right_logical(spot & 7, 1)
    spot_s = lax.broadcasted_iota(jnp.int32, (ROWS, 2 * SINKS), 1)
    small = (2 * SINKS, 2 * SINKS)
    move = jnp.where(
        lax.broadcasted_iota(jnp.int32, small, 0) + 1
        == lax.broadcasted_iota(jnp.int32, small, 1),
        1.0, 0.0,
    ).astype(jnp.bfloat16)

    for turn, k in enumerate(order):
        length, reach, cosine, sine, _ = told[k]
        base = jnp.maximum(length - WINDOW, 0)
        first = lax.shift_right_logical(base - shard + (SEQ - 1), 6)
        place = (first + slot) * SEQ + shard
        valid = (
            ((spot & 1) == 0)
            & (place < length)
            & ((place < SINKS) | (place >= length - WINDOW))
        )
        valid_s = ((spot_s & 1) == 0) & (
            length - WINDOW > lax.shift_right_logical(spot_s, 1)
        )
        q = block_rows(0, k)
        q = (q * cosine + pltpu.roll(q, HD // 2, 1) * sine).astype(jnp.bfloat16)
        old = KV[:, pl.ds(xat(k), 1)].reshape(SEQ * SLOTS * 2, HD)
        old_s = SK[:, pl.ds(xat(k), 1)].reshape(2 * SINKS, HD)
        s = jnp.where(valid, nt(q, old) * scale, -1e30)
        s_s = jnp.where(valid_s, nt(q, old_s) * scale, -1e30)
        top = jnp.maximum(
            jnp.max(s, axis=-1, keepdims=True), jnp.max(s_s, axis=-1, keepdims=True)
        )
        w = jnp.where(valid, jnp.exp(s - top), 0.0)
        wt_s = jnp.where(valid_s, jnp.exp(s_s - top), 0.0)
        total = jnp.sum(w, axis=-1, keepdims=True) + jnp.sum(
            wt_s, axis=-1, keepdims=True
        )
        shifted = pltpu.roll(w, 1, 1).astype(jnp.bfloat16)
        shifted_s = nn(wt_s.astype(jnp.bfloat16), move).astype(jnp.bfloat16)
        weighted = nn(shifted, old) + nn(shifted_s, old_s)
        tree = reach > 0.5
        t = jnp.where(tree, nt(q, keys[k]) * scale, -1e30)
        joint = jnp.maximum(top, jnp.max(t, axis=-1, keepdims=True))
        tw = jnp.where(tree, jnp.exp(t - joint), 0.0)
        ratio = jnp.exp(top - joint)
        summed = nn(tw.astype(jnp.bfloat16), values[k])
        below = total * ratio + jnp.sum(tw, axis=-1, keepdims=True)
        done = ((weighted * ratio + summed) / below).astype(jnp.bfloat16)
        if k == 0:
            ATT[x] = done
        else:
            att[k - 1] = done
            for dx, dz in parts[turn]:
                hop_b(dx, dz)
            send(att.at[k - 1], ATT.at[x], a_s, a_r, idx(k, 0))

    for dx, dz in parts[3]:
        hop_b(dx, dz)
    for dz in (0, -1, 1, -2, 2, -3, 3, -4):
        hop_b(-2, dz)
    all_of(ATT.at[pl.ds(0, X - 1)], a_r)
    a = jnp.concatenate([ATT[h] for h in range(HEADS)], axis=1)
    all_of(WO.at[pl.ds(0, SEQ // CORES)], bsib_r)
    wide_group = SEQ // TP
    turns = (2, 1, 3, 0)
    for at, k in enumerate(turns):
        t = lax.rem(tp + k, TP)
        right = WO[pl.ds(t * wide_group, wide_group)].reshape(WIDTH, WIDTH)
        part[t] = nt(a, right).astype(jnp.bfloat16)
        if at:
            t = lax.rem(tp + turns[at - 1], TP)
            pltpu.make_async_remote_copy(
                src_ref=part.at[t], dst_ref=PG.at[tp], send_sem=ps, recv_sem=pr,
                device_id={"tp": t},
            ).start()

    others = pl.ds(0, SEQ - 1)
    pieces = SEQ // CORES
    all_of(N.at[pl.ds(0, X - 1)], t_s)
    all_of(WH.at[:, pl.ds(0, X - 1), 0], wx_s)
    all_of(WH.at[:, :, pl.ds(0, Z - 1)], w_s)
    all_of(WH.at[:, :, pl.ds(0, Z)], wsib_s)
    all_of(WO.at[pl.ds(0, pieces - 1)], b_s)
    all_of(WO.at[pl.ds(0, pieces)], bsib_s)
    all_of(packed.at[others], kv_s)
    all_of(att, a_s)

    @pl.when(me < SINKS)
    def _():
        all_of(sinks.at[others], sk_s)

    own_g.wait()
    all_of(G.at[others], gr)
    arrived[...] = G[...]
    all_of(PG.at[pl.ds(0, TP - 1)], pr)
    below = part[tp].astype(jnp.float32)
    for k in range(1, TP):
        below = below + PG[lax.rem(tp + k, TP)].astype(jnp.float32)
    gathered[...] = below.astype(jnp.bfloat16)
    all_of(part.at[pl.ds(0, TP - 1)], ps)
    all_of(fresh.at[others], gs)


def final_kernel(deal, code, G, gathered, cache, branch, new_cache, sem):
    copy = pltpu.make_async_copy(cache, new_cache, sem)
    copy.start()
    branch[...] = gathered[...]
    copy.wait()

    def place(i, carry):
        r = deal[i]
        spot = code[0, r]
        far, near = lax.shift_right_logical(i, 4), i & (COLUMN - 1)

        @pl.when(spot >= 0)
        def _():
            for h in range(HEADS):
                new_cache[r, spot, :, h * HD:(h + 1) * HD] = G[h * COLUMN + near, far]

        return carry

    lax.fori_loop(0, ROWS, place, 0, unroll=8)


def whole():
    return pl.BlockSpec(memory_space=pltpu.VMEM)


def shaped(shape, dtype=jnp.bfloat16):
    return jax.ShapeDtypeStruct(shape, dtype)


def run_whole(deal, lengths, leaves, tokens, parents, freq, spans, tips, cache, wq, wo):
    dma = pltpu.SemaphoreType.DMA
    vmem = pltpu.VMEM
    half = jnp.bfloat16
    return pl.pallas_call(
        whole_kernel,
        name="whole",
        in_specs=[pl.BlockSpec(memory_space=pltpu.SMEM)] * 3 + [whole()] * 8,
        out_specs=[whole()] * 3,
        out_shape=[
            shaped((ROWS, WIDTH)),
            shaped((SEQ, X, 2, HD)),
            shaped((1, ROWS), jnp.int32),
        ],
        scratch_shapes=[
            vmem((SEQ, X, 2 * SLOTS, HD), half),
            vmem((SEQ, X, 2, HD), half),
            vmem((X, ROWS, DEEP), half),
            vmem((3, X, COLUMN, DEEP // SEQ, HD), half),
            vmem((SEQ, DEEP // SEQ, WIDTH), half),
            vmem((SEQ, X, 2 * SLOTS, HD), half),
            vmem((SINKS, X, 2, HD), half),
            vmem((3, X * ROWS, HD), jnp.float32),
            vmem((X - 1, ROWS, HD), half),
            vmem((X, ROWS, HD), half),
            vmem((TP, ROWS, WIDTH), half),
            vmem((TP, ROWS, WIDTH), half),
            vmem((SEQ, X, 2, HD), half),
            vmem((SEQ, X, 2, HD), half),
            vmem((ROWS, HD), jnp.int32),
            dma((5,)), dma((4,)), dma((Z,)), dma((X, Z)),
        ] + [dma] * 19,
        compiler_params=pltpu.CompilerParams(collective_id=0, has_side_effects=True),
    )(deal, lengths, leaves, tokens, parents, freq, spans, tips, cache, wq, wo)


def run_final(deal, code, arrived, gathered, cache):
    return pl.pallas_call(
        final_kernel,
        name="final",
        grid_spec=pltpu.PrefetchScalarGridSpec(
            num_scalar_prefetch=2,
            in_specs=[whole(), whole(), pl.BlockSpec(memory_space=pl.ANY)],
            out_specs=[whole()] * 2,
            scratch_shapes=[pltpu.SemaphoreType.DMA],
        ),
        out_shape=[shaped((ROWS, WIDTH)), shaped(cache.shape)],
    )(deal, code, arrived, gathered, cache)


def on_device(tokens, qkv_weight, out_weight, kv_cache, lengths, parents, leaves, deal):
    cache = kv_cache.reshape(kv_cache.shape[0], kv_cache.shape[1], 2, WIDTH)
    half = np.arange(HD, dtype=np.float64) % (HD // 2)
    freq = jnp.asarray((10000.0 ** (-2.0 * half / HD)).astype(np.float32)[None, :])
    wq = jnp.transpose(qkv_weight, (1, 0, 2))
    wo = jnp.transpose(out_weight, (1, 0))
    gathered, arrived, code = run_whole(
        deal, lengths, leaves, tokens, parents, freq,
        lengths.reshape(1, ROWS), leaves.reshape(1, ROWS), cache, wq, wo,
    )
    branch, new_cache = run_final(deal, code, arrived, gathered, cache)
    return branch, new_cache.reshape(kv_cache.shape)


def solution(mesh):
    placed = (
        P("seq", None),
        P("seq", None, "tp"),
        P("tp", "seq"),
        P(None, None, "seq", None, "tp"),
        P(),
        P(),
        P(),
        P(),
    )
    return jax.shard_map(
        on_device,
        mesh=mesh,
        in_specs=placed,
        out_specs=(P("seq", "tp"), P(None, None, "seq", None, "tp")),
        check_vma=False,
    )
```

```python
import functools

import jax
import jax.numpy as jnp
import numpy as np
from jax import lax
from jax.experimental import pallas as pl
from jax.experimental.pallas import tpu as pltpu
from jax.sharding import PartitionSpec as P

HD = 128
SINKS = 4
X, Z, CORES = 4, 8, 2
SEQ = X * Z * CORES
TP = 4
COLUMN = Z * CORES
ROWS = 64
SLOTS = 4
WIDTH = 512
HEADS = WIDTH // HD
WINDOW = 256
DEEP = 2048
KV_PARTS = ((1, 16), (16, 28), (28, 40), (40, 52), (52, 64))


def nt(a, b):
    return lax.dot_general(
        a, b, (((1,), (1,)), ((), ())), preferred_element_type=jnp.float32
    )


def nn(a, b):
    return lax.dot_general(
        a, b, (((1,), (0,)), ((), ())), preferred_element_type=jnp.float32
    )


def whole_kernel(
    deal, lengths, leaves, tokens, parents, freq, spans, tips, cache, wq, wo,
    gathered, arrived, code_out,
    packed, sinks, N, WH, WO, KV, SK, acc, att, ATT, part, PG, fresh, G, par_pad,
    own_sem, tr, wr, br,
    t_s, wx_s, wx_r, w_s, wsib_s, wsib_r, b_s, bsib_s, bsib_r,
    kv_s, kv_r, sk_s, sk_r, a_s, a_r, ps, pr, gs, gr,
):
    me = lax.axis_index("seq")
    tp = lax.axis_index("tp")
    x = me // COLUMN
    z = lax.rem(me // CORES, Z)
    c = lax.rem(me, CORES)
    column = lax.rem(me, COLUMN)

    def xat(dx):
        return lax.rem(x + (dx + X), X)

    def qat(dz):
        return lax.rem(z + (dz + Z), Z) * CORES + c

    def idx(dx, dz):
        return xat(dx) * COLUMN + qat(dz)

    def side(h):
        return pl.ds(pl.multiple_of(h * HD, HD), HD)

    def all_of(ref, sem):
        pltpu.make_async_copy(ref, ref, sem).wait()

    def send(src, dst, there, here, target):
        pltpu.make_async_remote_copy(
            src_ref=src, dst_ref=dst, send_sem=there, recv_sem=here,
            device_id={"seq": target},
        ).start()

    barrier = pltpu.get_barrier_semaphore()

    def greet(k, carry):
        pl.semaphore_signal(barrier, 1, device_id={"seq": lax.rem(me + k, SEQ)})
        return carry

    lax.fori_loop(1, SEQ, greet, 0)
    for k in range(1, TP):
        pl.semaphore_signal(barrier, 1, device_id={"tp": lax.rem(tp + k, TP)})

    own_w = pltpu.make_async_copy(
        wq.at[:, :, side(x)], WH.at[:, x, column], own_sem.at[0]
    )
    own_w.start()
    own_b = pltpu.make_async_copy(wo, WO.at[me], own_sem.at[1])
    own_b.start()

    wide = tokens[...].astype(jnp.float32)
    centred = wide - jnp.mean(wide, axis=-1, keepdims=True)
    scaling = lax.rsqrt(jnp.mean(centred * centred, axis=-1, keepdims=True) + 1e-05)
    N[x] = (centred * scaling).astype(jnp.bfloat16)

    def pack(t, carry):
        r = deal[t]
        base = jnp.maximum(lengths[r] - WINDOW, 0)
        first = lax.shift_right_logical(base - me + (SEQ - 1), 6)
        rows = cache[r, pl.ds(first, SLOTS)].reshape(2 * SLOTS, WIDTH)
        sunk = cache[r, 0]
        far, near = t // COLUMN, lax.rem(t, COLUMN)
        for h in range(HEADS):
            packed[h * COLUMN + near, far] = rows[:, h * HD:(h + 1) * HD]
            sinks[h * COLUMN + near, far] = sunk[:, h * HD:(h + 1) * HD]
        return carry

    lax.fori_loop(0, ROWS, pack, 0)

    pl.semaphore_wait(barrier, SEQ + TP - 2)

    def send_w(dz, step):
        at = WH.at[:, :, qat(dz)]
        if step == 0:
            send(at, at, wsib_s, wsib_r, me + 1 - 2 * c)
        else:
            send(at, at, w_s, wr.at[(dz - step) % Z], idx(0, step))

    def hop_w(dz):
        at = WH.at[:, :, qat(dz)]
        all_of(at, wr.at[dz % Z])
        if -4 < dz < 0:
            send_w(dz, 1)
        elif 0 < dz < 3:
            send_w(dz, -1)
        send_w(dz, 0)

    def send_b(dx, dz, way):
        at = idx(dx, dz)
        src = wo if (dx, dz) == (0, 0) else WO.at[at]
        if way == "s":
            send(src, WO.at[at], bsib_s, bsib_r, me + 1 - 2 * c)
        else:
            ox, oz = {"x+": (1, 0), "x-": (-1, 0), "z+": (0, 1), "z-": (0, -1)}[way]
            send(
                src, WO.at[at], b_s, br.at[(dx - ox) % X, (dz - oz) % Z], idx(ox, oz)
            )

    def hop_b(dx, dz):
        if (dx, dz) != (0, 0):
            all_of(WO.at[idx(dx, dz)], br.at[dx % X, dz % Z])
        out = []
        if dx == 0:
            if dz == 0:
                out += ["z+", "z-"]
            elif -4 < dz < 0:
                out += ["z+"]
            elif 0 < dz < 3:
                out += ["z-"]
            out += ["x+", "x-"]
        elif dx == -1 and dz % 2 == 0:
            out += ["x+"]
        elif dx == 1 and dz % 2 == 1:
            out += ["x-"]
        for way in out + ["s"]:
            send_b(dx, dz, way)

    for k in (2, 1, 3):
        send(
            wq.at[:, :, side(xat(k))], WH.at[:, x, column], wx_s, wx_r, idx(k, 0)
        )
    own_b.wait()
    hop_b(0, 0)
    send(N.at[x], N.at[x], t_s, tr.at[0], idx(1, 0))
    send(N.at[x], N.at[x], t_s, tr.at[1], idx(-1, 0))

    own_kv = pltpu.make_async_copy(packed.at[me], KV.at[me], own_sem.at[2])
    own_kv.start()

    def scatter(low, high):
        def one(k, carry):
            t = lax.rem(me + k, SEQ)
            send(packed.at[t], KV.at[me], kv_s, kv_r, t)
            return carry

        lax.fori_loop(low, high, one, 0)

    scatter(*KV_PARTS[0])

    sub = lax.broadcasted_iota(jnp.int32, (ROWS, ROWS), 0)
    lane = lax.broadcasted_iota(jnp.int32, (ROWS, ROWS), 1)
    lanes = lax.broadcasted_iota(jnp.int32, (ROWS, HD), 1)
    eye = jnp.where(sub == lane, 1.0, 0.0)

    def describe(k):
        request = deal[xat(k) * COLUMN + column]
        length = lengths[request]
        leaf = leaves[request]
        row = parents[pl.ds(request, 1), :]
        up = eye + jnp.where(row == sub, 1.0, 0.0)
        for _ in range(6):
            half = up.astype(jnp.bfloat16)
            up = jnp.minimum(nn(half, half), 1.0)
        reach = nt(eye.astype(jnp.bfloat16), up.astype(jnp.bfloat16))
        depth_row = (jnp.sum(up, axis=0, keepdims=True) - 1.0).astype(jnp.int32)
        depth_col = (jnp.sum(reach, axis=1, keepdims=True) - 1.0).astype(jnp.int32)
        angle = (length + depth_col).astype(jnp.float32) * freq[...]
        cosine = jnp.cos(angle)
        wave = jnp.sin(angle)
        sine = jnp.where(lanes < HD // 2, -wave, wave)
        on_path = jnp.sum(jnp.where(sub == leaf, reach, 0.0), axis=0, keepdims=True)
        offset = lax.rem(sub - length + 8 * SEQ, SEQ)
        hit = (on_path > 0.5) & (depth_row == offset)
        pick = jnp.where(hit, 1.0, 0.0).astype(jnp.bfloat16)
        return length, reach, cosine, sine, pick

    def table():
        par_pad[...] = lanes
        par_pad[:, 0:ROWS] = parents[...]
        par = par_pad[...]
        climb = jnp.where((lanes < ROWS) & (par >= 0), 1, 0)
        jump = jnp.where(par < 0, 0, par)
        for _ in range(6):
            climb = climb + jnp.take_along_axis(climb, jump, axis=1)
            jump = jnp.take_along_axis(jump, jump, axis=1)
        tip = jnp.sum(jnp.where(sub == lane, tips[...], 0), axis=1, keepdims=True)
        span = jnp.sum(jnp.where(sub == lane, spans[...], 0), axis=1, keepdims=True)
        end = jnp.sum(jnp.where(lanes == tip, climb, 0), axis=1, keepdims=True)
        ahead = (me - span + 8 * SEQ) & (SEQ - 1)
        code = jnp.where(
            ahead <= end, lax.shift_right_logical(span + ahead, 6), -1
        )
        code_out[...] = jnp.sum(
            jnp.where(sub == lane, code, 0), axis=0, keepdims=True
        )

    order = (2, 1, 3, 0)
    told = {order[0]: describe(order[0])}

    own_w.wait()
    all_of(WH.at[:, pl.ds(0, X - 1), 0], wx_r)
    send_w(0, 1)
    send_w(0, -1)
    send_w(0, 0)
    hop_b(0, -1)
    hop_b(0, 1)
    scatter(*KV_PARTS[1])
    told[order[1]] = describe(order[1])

    left, right = pl.ds(0, DEEP // 2), pl.ds(DEEP // 2, DEEP // 2)
    hop_w(-1)
    hop_w(1)
    hop_b(0, -2)
    hop_b(0, 2)
    all_of(N.at[0], tr.at[0])
    at = N.at[xat(-1), :, left]
    send(at, at, t_s, tr.at[2], idx(1, 0))
    all_of(N.at[0], tr.at[1])
    at = N.at[xat(1), :, right]
    send(at, at, t_s, tr.at[3], idx(-1, 0))
    scatter(*KV_PARTS[2])

    @pl.when(me < SINKS)
    def _():
        pltpu.make_async_copy(sinks.at[me], SK.at[me], sk_r).start()

        def spread(k, carry):
            t = lax.rem(me + k, SEQ)
            send(sinks.at[t], SK.at[me], sk_s, sk_r, t)
            return carry

        lax.fori_loop(1, SEQ, spread, 0)

    told[order[2]] = describe(order[2])
    hop_w(-2)
    hop_w(2)
    hop_b(0, -3)
    hop_b(0, 3)
    scatter(*KV_PARTS[3])
    told[order[3]] = describe(order[3])
    hop_b(-1, 0)
    hop_b(1, 0)
    hop_w(-3)
    hop_w(3)
    hop_b(0, -4)
    scatter(*KV_PARTS[4])
    table()
    for dz in (-1, 1):
        hop_b(-1, dz)
        hop_b(1, dz)
    hop_w(-4)
    for dz in (-2, 2):
        hop_b(-1, dz)
        hop_b(1, dz)

    all_of(N.at[0, :, left], tr.at[2])
    all_of(N.at[0, :, right], tr.at[3])
    all_of(WH.at[:, :, pl.ds(0, Z)], wsib_r)
    deep = COLUMN * (DEEP // SEQ)
    rows_all = X * ROWS
    for kind in range(3):
        total = None
        for block in range(X):
            mine = N[:, :, block * deep:(block + 1) * deep].reshape(rows_all, deep)
            term = nn(mine, WH[kind, block].reshape(deep, HD))
            total = term if total is None else total + term
        acc[kind] = total

    twice = lax.broadcasted_iota(jnp.int32, (2 * SEQ, SEQ), 0)
    once = lax.broadcasted_iota(jnp.int32, (2 * SEQ, SEQ), 1)
    even = jnp.where(twice == 2 * once, 1.0, 0.0).astype(jnp.bfloat16)
    odd = jnp.where(twice == 2 * once + 1, 1.0, 0.0).astype(jnp.bfloat16)

    def block_rows(kind, k):
        return acc[kind, pl.ds(pl.multiple_of(xat(k) * ROWS, ROWS), ROWS)]

    keys, values = {}, {}
    for k in order:
        _, _, cosine, sine, pick = told[k]
        key = block_rows(1, k)
        key = key * cosine + pltpu.roll(key, HD // 2, 1) * sine
        keys[k] = key.astype(jnp.bfloat16)
        values[k] = block_rows(2, k).astype(jnp.bfloat16)
        pick_k = nn(even, pick).astype(jnp.bfloat16)
        pick_v = nn(odd, pick).astype(jnp.bfloat16)
        mixed = (nn(pick_k, keys[k]) + nn(pick_v, values[k])).astype(jnp.bfloat16)
        fresh[:, xat(k)] = mixed.reshape(SEQ, 2, HD)
    for dz in (-3, 3, -4):
        hop_b(-1, dz)
        hop_b(1, dz)

    own_g = pltpu.make_async_copy(fresh.at[me], G.at[me], own_sem.at[4])
    own_g.start()

    def hand(k, carry):
        t = lax.rem(me + k, SEQ)
        send(fresh.at[t], G.at[me], gs, gr, t)
        return carry

    lax.fori_loop(1, SEQ, hand, 0)

    later = [(-2, dz) for dz in (0, -1, 1, -2, 2, -3, 3, -4)]
    parts = [later[0:3], later[3:5], later[5:7], later[7:8]]

    own_kv.wait()
    all_of(KV.at[pl.ds(0, SEQ - 1)], kv_r)
    all_of(SK, sk_r)

    scale = float(HD) ** (-0.5)
    spot = lax.broadcasted_iota(jnp.int32, (ROWS, SEQ * SLOTS * 2), 1)
    shard = lax.shift_right_logical(spot, 3)
    slot = lax.shift_right_logical(spot & 7, 1)
    spot_s = lax.broadcasted_iota(jnp.int32, (ROWS, 2 * SINKS), 1)
    small = (2 * SINKS, 2 * SINKS)
    move = jnp.where(
        lax.broadcasted_iota(jnp.int32, small, 0) + 1
        == lax.broadcasted_iota(jnp.int32, small, 1),
        1.0, 0.0,
    ).astype(jnp.bfloat16)

    for turn, k in enumerate(order):
        length, reach, cosine, sine, _ = told[k]
        base = jnp.maximum(length - WINDOW, 0)
        first = lax.shift_right_logical(base - shard + (SEQ - 1), 6)
        place = (first + slot) * SEQ + shard
        valid = (
            ((spot & 1) == 0)
            & (place < length)
            & ((place < SINKS) | (place >= length - WINDOW))
        )
        valid_s = ((spot_s & 1) == 0) & (
            length - WINDOW > lax.shift_right_logical(spot_s, 1)
        )
        q = block_rows(0, k)
        q = (q * cosine + pltpu.roll(q, HD // 2, 1) * sine).astype(jnp.bfloat16)
        old = KV[:, pl.ds(xat(k), 1)].reshape(SEQ * SLOTS * 2, HD)
        old_s = SK[:, pl.ds(xat(k), 1)].reshape(2 * SINKS, HD)
        s = jnp.where(valid, nt(q, old) * scale, -1e30)
        s_s = jnp.where(valid_s, nt(q, old_s) * scale, -1e30)
        top = jnp.maximum(
            jnp.max(s, axis=-1, keepdims=True), jnp.max(s_s, axis=-1, keepdims=True)
        )
        w = jnp.where(valid, jnp.exp(s - top), 0.0)
        wt_s = jnp.where(valid_s, jnp.exp(s_s - top), 0.0)
        total = jnp.sum(w, axis=-1, keepdims=True) + jnp.sum(
            wt_s, axis=-1, keepdims=True
        )
        shifted = pltpu.roll(w, 1, 1).astype(jnp.bfloat16)
        shifted_s = nn(wt_s.astype(jnp.bfloat16), move).astype(jnp.bfloat16)
        weighted = nn(shifted, old) + nn(shifted_s, old_s)
        tree = reach > 0.5
        t = jnp.where(tree, nt(q, keys[k]) * scale, -1e30)
        joint = jnp.maximum(top, jnp.max(t, axis=-1, keepdims=True))
        tw = jnp.where(tree, jnp.exp(t - joint), 0.0)
        ratio = jnp.exp(top - joint)
        summed = nn(tw.astype(jnp.bfloat16), values[k])
        below = total * ratio + jnp.sum(tw, axis=-1, keepdims=True)
        done = ((weighted * ratio + summed) / below).astype(jnp.bfloat16)
        if k == 0:
            ATT[x] = done
        else:
            att[k - 1] = done
            for dx, dz in parts[turn]:
                hop_b(dx, dz)
            send(att.at[k - 1], ATT.at[x], a_s, a_r, idx(k, 0))

    for dx, dz in parts[3]:
        hop_b(dx, dz)
    all_of(ATT.at[pl.ds(0, X - 1)], a_r)
    a = jnp.concatenate([ATT[h] for h in range(HEADS)], axis=1)
    all_of(WO.at[pl.ds(0, SEQ // CORES)], bsib_r)
    wide_group = SEQ // TP
    turns = (2, 1, 3, 0)
    for at, k in enumerate(turns):
        t = lax.rem(tp + k, TP)
        right = WO[pl.ds(t * wide_group, wide_group)].reshape(WIDTH, WIDTH)
        part[t] = nt(a, right).astype(jnp.bfloat16)
        if at:
            t = lax.rem(tp + turns[at - 1], TP)
            pltpu.make_async_remote_copy(
                src_ref=part.at[t], dst_ref=PG.at[tp], send_sem=ps, recv_sem=pr,
                device_id={"tp": t},
            ).start()

    others = pl.ds(0, SEQ - 1)
    pieces = SEQ // CORES
    all_of(N.at[pl.ds(0, X - 1)], t_s)
    all_of(WH.at[:, pl.ds(0, X - 1), 0], wx_s)
    all_of(WH.at[:, :, pl.ds(0, Z - 1)], w_s)
    all_of(WH.at[:, :, pl.ds(0, Z)], wsib_s)
    all_of(WO.at[pl.ds(0, pieces - 1)], b_s)
    all_of(WO.at[pl.ds(0, pieces)], bsib_s)
    all_of(packed.at[others], kv_s)
    all_of(att, a_s)

    @pl.when(me < SINKS)
    def _():
        all_of(sinks.at[others], sk_s)

    own_g.wait()
    all_of(G.at[others], gr)
    arrived[...] = G[...]
    all_of(PG.at[pl.ds(0, TP - 1)], pr)
    below = part[tp].astype(jnp.float32)
    for k in range(1, TP):
        below = below + PG[lax.rem(tp + k, TP)].astype(jnp.float32)
    gathered[...] = below.astype(jnp.bfloat16)
    all_of(part.at[pl.ds(0, TP - 1)], ps)
    all_of(fresh.at[others], gs)


def final_kernel(deal, code, G, gathered, cache, branch, new_cache, sem):
    copy = pltpu.make_async_copy(cache, new_cache, sem)
    copy.start()
    branch[...] = gathered[...]
    copy.wait()

    def place(i, carry):
        r = deal[i]
        spot = code[0, r]
        far, near = lax.shift_right_logical(i, 4), i & (COLUMN - 1)

        @pl.when(spot >= 0)
        def _():
            for h in range(HEADS):
                new_cache[r, spot, :, h * HD:(h + 1) * HD] = G[h * COLUMN + near, far]

        return carry

    lax.fori_loop(0, ROWS, place, 0, unroll=8)


def whole():
    return pl.BlockSpec(memory_space=pltpu.VMEM)


def shaped(shape, dtype=jnp.bfloat16):
    return jax.ShapeDtypeStruct(shape, dtype)


def run_whole(deal, lengths, leaves, tokens, parents, freq, spans, tips, cache, wq, wo):
    dma = pltpu.SemaphoreType.DMA
    vmem = pltpu.VMEM
    half = jnp.bfloat16
    return pl.pallas_call(
        whole_kernel,
        name="whole",
        in_specs=[pl.BlockSpec(memory_space=pltpu.SMEM)] * 3 + [whole()] * 8,
        out_specs=[whole()] * 3,
        out_shape=[
            shaped((ROWS, WIDTH)),
            shaped((SEQ, X, 2, HD)),
            shaped((1, ROWS), jnp.int32),
        ],
        scratch_shapes=[
            vmem((SEQ, X, 2 * SLOTS, HD), half),
            vmem((SEQ, X, 2, HD), half),
            vmem((X, ROWS, DEEP), half),
            vmem((3, X, COLUMN, DEEP // SEQ, HD), half),
            vmem((SEQ, DEEP // SEQ, WIDTH), half),
            vmem((SEQ, X, 2 * SLOTS, HD), half),
            vmem((SINKS, X, 2, HD), half),
            vmem((3, X * ROWS, HD), jnp.float32),
            vmem((X - 1, ROWS, HD), half),
            vmem((X, ROWS, HD), half),
            vmem((TP, ROWS, WIDTH), half),
            vmem((TP, ROWS, WIDTH), half),
            vmem((SEQ, X, 2, HD), half),
            vmem((SEQ, X, 2, HD), half),
            vmem((ROWS, HD), jnp.int32),
            dma((5,)), dma((4,)), dma((Z,)), dma((X, Z)),
        ] + [dma] * 19,
        compiler_params=pltpu.CompilerParams(collective_id=0, has_side_effects=True),
    )(deal, lengths, leaves, tokens, parents, freq, spans, tips, cache, wq, wo)


def run_final(deal, code, arrived, gathered, cache):
    return pl.pallas_call(
        final_kernel,
        name="final",
        grid_spec=pltpu.PrefetchScalarGridSpec(
            num_scalar_prefetch=2,
            in_specs=[whole(), whole(), pl.BlockSpec(memory_space=pl.ANY)],
            out_specs=[whole()] * 2,
            scratch_shapes=[pltpu.SemaphoreType.DMA],
        ),
        out_shape=[shaped((ROWS, WIDTH)), shaped(cache.shape)],
    )(deal, code, arrived, gathered, cache)


def on_device(tokens, qkv_weight, out_weight, kv_cache, lengths, parents, leaves, deal):
    cache = kv_cache.reshape(kv_cache.shape[0], kv_cache.shape[1], 2, WIDTH)
    half = np.arange(HD, dtype=np.float64) % (HD // 2)
    freq = jnp.asarray((10000.0 ** (-2.0 * half / HD)).astype(np.float32)[None, :])
    wq = jnp.transpose(qkv_weight, (1, 0, 2))
    wo = jnp.transpose(out_weight, (1, 0))
    gathered, arrived, code = run_whole(
        deal, lengths, leaves, tokens, parents, freq,
        lengths.reshape(1, ROWS), leaves.reshape(1, ROWS), cache, wq, wo,
    )
    branch, new_cache = run_final(deal, code, arrived, gathered, cache)
    return branch, new_cache.reshape(kv_cache.shape)


def solution(mesh):
    placed = (
        P("seq", None),
        P("seq", None, "tp"),
        P("tp", "seq"),
        P(None, None, "seq", None, "tp"),
        P(),
        P(),
        P(),
        P(),
    )
    return jax.shard_map(
        on_device,
        mesh=mesh,
        in_specs=placed,
        out_specs=(P("seq", "tp"), P(None, None, "seq", None, "tp")),
        check_vma=False,
    )
```

```python
import functools

import jax
import jax.numpy as jnp
import numpy as np
from jax import lax
from jax.experimental import pallas as pl
from jax.experimental.pallas import tpu as pltpu
from jax.sharding import PartitionSpec as P

HD = 128
SINKS = 4
X, Z, CORES = 4, 8, 2
SEQ = X * Z * CORES
TP = 4
COLUMN = Z * CORES
ROWS = 64
SLOTS = 4
WIDTH = 512
HEADS = WIDTH // HD
WINDOW = 256
DEEP = 2048
KV_PARTS = ((1, 16), (16, 28), (28, 40), (40, 52), (52, 64))


def nt(a, b):
    return lax.dot_general(
        a, b, (((1,), (1,)), ((), ())), preferred_element_type=jnp.float32
    )


def nn(a, b):
    return lax.dot_general(
        a, b, (((1,), (0,)), ((), ())), preferred_element_type=jnp.float32
    )


def whole_kernel(
    deal, lengths, leaves, tokens, parents, freq, spans, tips, cache, wq, wo,
    gathered, arrived, code_out,
    packed, sinks, N, WH, WO, KV, SK, acc, att, ATT, part, PG, fresh, G, par_pad,
    own_sem, tr, wr, br, gate,
    t_s, wx_s, wx_r, w_s, wsib_s, wsib_r, b_s, bsib_s, bsib_r,
    kv_s, kv_r, sk_s, sk_r, a_s, a_r, ps, pr, gs, gr,
):
    me = lax.axis_index("seq")
    tp = lax.axis_index("tp")
    x = me // COLUMN
    z = lax.rem(me // CORES, Z)
    c = lax.rem(me, CORES)
    column = lax.rem(me, COLUMN)

    def xat(dx):
        return lax.rem(x + (dx + X), X)

    def qat(dz):
        return lax.rem(z + (dz + Z), Z) * CORES + c

    def idx(dx, dz):
        return xat(dx) * COLUMN + qat(dz)

    def side(h):
        return pl.ds(pl.multiple_of(h * HD, HD), HD)

    def all_of(ref, sem):
        pltpu.make_async_copy(ref, ref, sem).wait()

    def send(src, dst, there, here, target):
        pltpu.make_async_remote_copy(
            src_ref=src, dst_ref=dst, send_sem=there, recv_sem=here,
            device_id={"seq": target},
        ).start()

    barrier = pltpu.get_barrier_semaphore()

    def mate(k):
        return x * COLUMN + lax.rem(column + k, COLUMN)

    for k in range(1, COLUMN):
        pl.semaphore_signal(barrier, 1, device_id={"seq": mate(k)})
    for k in range(1, X):
        pl.semaphore_signal(barrier, 1, device_id={"seq": xat(k) * COLUMN + column})
    for k in range(1, TP):
        pl.semaphore_signal(barrier, 1, device_id={"tp": lax.rem(tp + k, TP)})

    own_w = pltpu.make_async_copy(
        wq.at[:, :, side(x)], WH.at[:, x, column], own_sem.at[0]
    )
    own_w.start()
    own_b = pltpu.make_async_copy(wo, WO.at[me], own_sem.at[1])
    own_b.start()

    wide = tokens[...].astype(jnp.float32)
    centred = wide - jnp.mean(wide, axis=-1, keepdims=True)
    scaling = lax.rsqrt(jnp.mean(centred * centred, axis=-1, keepdims=True) + 1e-05)
    N[x] = (centred * scaling).astype(jnp.bfloat16)

    def pack(t, carry):
        r = deal[t]
        base = jnp.maximum(lengths[r] - WINDOW, 0)
        first = lax.shift_right_logical(base - me + (SEQ - 1), 6)
        rows = cache[r, pl.ds(first, SLOTS)].reshape(2 * SLOTS, WIDTH)
        sunk = cache[r, 0]
        far, near = t // COLUMN, lax.rem(t, COLUMN)
        for h in range(HEADS):
            packed[h * COLUMN + near, far] = rows[:, h * HD:(h + 1) * HD]
            sinks[h * COLUMN + near, far] = sunk[:, h * HD:(h + 1) * HD]
        return carry

    lax.fori_loop(0, ROWS, pack, 0)

    pl.semaphore_wait(barrier, COLUMN + X + TP - 3)
    for k in range(1, COLUMN):
        pl.semaphore_signal(gate, 1, device_id={"seq": mate(k)})

    def send_w(dz, step):
        at = WH.at[:, :, qat(dz)]
        if step == 0:
            send(at, at, wsib_s, wsib_r, me + 1 - 2 * c)
        else:
            send(at, at, w_s, wr.at[(dz - step) % Z], idx(0, step))

    def hop_w(dz):
        at = WH.at[:, :, qat(dz)]
        all_of(at, wr.at[dz % Z])
        if -4 < dz < 0:
            send_w(dz, 1)
        elif 0 < dz < 3:
            send_w(dz, -1)
        send_w(dz, 0)

    def send_b(dx, dz, way):
        at = idx(dx, dz)
        src = wo if (dx, dz) == (0, 0) else WO.at[at]
        if way == "s":
            send(src, WO.at[at], bsib_s, bsib_r, me + 1 - 2 * c)
        else:
            ox, oz = {"x+": (1, 0), "x-": (-1, 0), "z+": (0, 1), "z-": (0, -1)}[way]
            send(
                src, WO.at[at], b_s, br.at[(dx - ox) % X, (dz - oz) % Z], idx(ox, oz)
            )

    def hop_b(dx, dz):
        if (dx, dz) != (0, 0):
            all_of(WO.at[idx(dx, dz)], br.at[dx % X, dz % Z])
        out = []
        if dx == 0:
            if dz == 0:
                out += ["z+", "z-"]
            elif -3 < dz < 0:
                out += ["z+"]
            elif 0 < dz < 4:
                out += ["z-"]
            out += ["x+", "x-"]
        elif dx == -1 and dz % 2 == 0:
            out += ["x+"]
        elif dx == 1 and dz % 2 == 1:
            out += ["x-"]
        for way in out + ["s"]:
            send_b(dx, dz, way)

    for k in (2, 1, 3):
        send(
            wq.at[:, :, side(xat(k))], WH.at[:, x, column], wx_s, wx_r, idx(k, 0)
        )
    own_b.wait()
    hop_b(0, 0)
    send(N.at[x], N.at[x], t_s, tr.at[0], idx(1, 0))
    send(N.at[x], N.at[x], t_s, tr.at[1], idx(-1, 0))

    own_kv = pltpu.make_async_copy(packed.at[me], KV.at[me], own_sem.at[2])
    own_kv.start()

    def scatter(low, high):
        def one(k, carry):
            t = xat(k // COLUMN) * COLUMN + lax.rem(column + k, COLUMN)
            send(packed.at[t], KV.at[me], kv_s, kv_r, t)
            return carry

        lax.fori_loop(low, high, one, 0)

    scatter(*KV_PARTS[0])
    pl.semaphore_wait(gate, COLUMN - 1)

    sub = lax.broadcasted_iota(jnp.int32, (ROWS, ROWS), 0)
    lane = lax.broadcasted_iota(jnp.int32, (ROWS, ROWS), 1)
    lanes = lax.broadcasted_iota(jnp.int32, (ROWS, HD), 1)
    eye = jnp.where(sub == lane, 1.0, 0.0)

    def describe(k):
        request = deal[xat(k) * COLUMN + column]
        length = lengths[request]
        leaf = leaves[request]
        row = parents[pl.ds(request, 1), :]
        up = eye + jnp.where(row == sub, 1.0, 0.0)
        for _ in range(6):
            half = up.astype(jnp.bfloat16)
            up = jnp.minimum(nn(half, half), 1.0)
        reach = nt(eye.astype(jnp.bfloat16), up.astype(jnp.bfloat16))
        depth_row = (jnp.sum(up, axis=0, keepdims=True) - 1.0).astype(jnp.int32)
        depth_col = (jnp.sum(reach, axis=1, keepdims=True) - 1.0).astype(jnp.int32)
        angle = (length + depth_col).astype(jnp.float32) * freq[...]
        cosine = jnp.cos(angle)
        wave = jnp.sin(angle)
        sine = jnp.where(lanes < HD // 2, -wave, wave)
        on_path = jnp.sum(jnp.where(sub == leaf, reach, 0.0), axis=0, keepdims=True)
        offset = lax.rem(sub - length + 8 * SEQ, SEQ)
        hit = (on_path > 0.5) & (depth_row == offset)
        pick = jnp.where(hit, 1.0, 0.0).astype(jnp.bfloat16)
        return length, reach, cosine, sine, pick

    def table():
        par_pad[...] = lanes
        par_pad[:, 0:ROWS] = parents[...]
        par = par_pad[...]
        climb = jnp.where((lanes < ROWS) & (par >= 0), 1, 0)
        jump = jnp.where(par < 0, 0, par)
        for _ in range(6):
            climb = climb + jnp.take_along_axis(climb, jump, axis=1)
            jump = jnp.take_along_axis(jump, jump, axis=1)
        tip = jnp.sum(jnp.where(sub == lane, tips[...], 0), axis=1, keepdims=True)
        span = jnp.sum(jnp.where(sub == lane, spans[...], 0), axis=1, keepdims=True)
        end = jnp.sum(jnp.where(lanes == tip, climb, 0), axis=1, keepdims=True)
        ahead = (me - span + 8 * SEQ) & (SEQ - 1)
        code = jnp.where(
            ahead <= end, lax.shift_right_logical(span + ahead, 6), -1
        )
        code_out[...] = jnp.sum(
            jnp.where(sub == lane, code, 0), axis=0, keepdims=True
        )

    order = (2, 1, 3, 0)
    told = {order[0]: describe(order[0])}

    own_w.wait()
    all_of(WH.at[:, pl.ds(0, X - 1), 0], wx_r)
    send_w(0, 1)
    send_w(0, -1)
    send_w(0, 0)
    hop_b(0, -1)
    hop_b(0, 1)
    scatter(*KV_PARTS[1])
    told[order[1]] = describe(order[1])

    left, right = pl.ds(0, DEEP // 2), pl.ds(DEEP // 2, DEEP // 2)
    hop_w(-1)
    hop_w(1)
    hop_b(0, -2)
    hop_b(0, 2)
    all_of(N.at[0], tr.at[0])
    at = N.at[xat(-1), :, left]
    send(at, at, t_s, tr.at[2], idx(1, 0))
    all_of(N.at[0], tr.at[1])
    at = N.at[xat(1), :, right]
    send(at, at, t_s, tr.at[3], idx(-1, 0))
    scatter(*KV_PARTS[2])

    @pl.when(me < SINKS)
    def _():
        pltpu.make_async_copy(sinks.at[me], SK.at[me], sk_r).start()

        def spread(k, carry):
            t = lax.rem(me + k, SEQ)
            send(sinks.at[t], SK.at[me], sk_s, sk_r, t)
            return carry

        lax.fori_loop(1, SEQ, spread, 0)

    told[order[2]] = describe(order[2])
    hop_w(-2)
    hop_w(2)
    hop_b(0, -3)
    hop_b(0, 3)
    scatter(*KV_PARTS[3])
    told[order[3]] = describe(order[3])
    hop_b(-1, 0)
    hop_b(1, 0)
    hop_w(-3)
    hop_w(3)
    hop_b(0, -4)
    scatter(*KV_PARTS[4])
    table()
    for dz in (-1, 1):
        hop_b(-1, dz)
        hop_b(1, dz)
    hop_w(-4)
    for dz in (-2, 2):
        hop_b(-1, dz)
        hop_b(1, dz)

    all_of(N.at[0, :, left], tr.at[2])
    all_of(N.at[0, :, right], tr.at[3])
    all_of(WH.at[:, :, pl.ds(0, Z)], wsib_r)
    deep = COLUMN * (DEEP // SEQ)
    rows_all = X * ROWS
    for kind in range(3):
        total = None
        for block in range(X):
            mine = N[:, :, block * deep:(block + 1) * deep].reshape(rows_all, deep)
            term = nn(mine, WH[kind, block].reshape(deep, HD))
            total = term if total is None else total + term
        acc[kind] = total

    twice = lax.broadcasted_iota(jnp.int32, (2 * SEQ, SEQ), 0)
    once = lax.broadcasted_iota(jnp.int32, (2 * SEQ, SEQ), 1)
    even = jnp.where(twice == 2 * once, 1.0, 0.0).astype(jnp.bfloat16)
    odd = jnp.where(twice == 2 * once + 1, 1.0, 0.0).astype(jnp.bfloat16)

    def block_rows(kind, k):
        return acc[kind, pl.ds(pl.multiple_of(xat(k) * ROWS, ROWS), ROWS)]

    keys, values = {}, {}
    for k in order:
        _, _, cosine, sine, pick = told[k]
        key = block_rows(1, k)
        key = key * cosine + pltpu.roll(key, HD // 2, 1) * sine
        keys[k] = key.astype(jnp.bfloat16)
        values[k] = block_rows(2, k).astype(jnp.bfloat16)
        pick_k = nn(even, pick).astype(jnp.bfloat16)
        pick_v = nn(odd, pick).astype(jnp.bfloat16)
        mixed = (nn(pick_k, keys[k]) + nn(pick_v, values[k])).astype(jnp.bfloat16)
        fresh[:, xat(k)] = mixed.reshape(SEQ, 2, HD)
    for dz in (-3, 3, -4):
        hop_b(-1, dz)
        hop_b(1, dz)

    own_g = pltpu.make_async_copy(fresh.at[me], G.at[me], own_sem.at[4])
    own_g.start()

    def hand(k, carry):
        t = lax.rem(me + k, SEQ)
        send(fresh.at[t], G.at[me], gs, gr, t)
        return carry

    lax.fori_loop(1, SEQ, hand, 0)

    later = [(-2, dz) for dz in (0, -1, 1, -2, 2, -3, 3, -4)]
    parts = [later[0:3], later[3:5], later[5:7], later[7:8]]

    own_kv.wait()
    all_of(KV.at[pl.ds(0, SEQ - 1)], kv_r)
    all_of(SK, sk_r)

    scale = float(HD) ** (-0.5)
    spot = lax.broadcasted_iota(jnp.int32, (ROWS, SEQ * SLOTS * 2), 1)
    shard = lax.shift_right_logical(spot, 3)
    slot = lax.shift_right_logical(spot & 7, 1)
    spot_s = lax.broadcasted_iota(jnp.int32, (ROWS, 2 * SINKS), 1)
    small = (2 * SINKS, 2 * SINKS)
    move = jnp.where(
        lax.broadcasted_iota(jnp.int32, small, 0) + 1
        == lax.broadcasted_iota(jnp.int32, small, 1),
        1.0, 0.0,
    ).astype(jnp.bfloat16)

    for turn, k in enumerate(order):
        length, reach, cosine, sine, _ = told[k]
        base = jnp.maximum(length - WINDOW, 0)
        first = lax.shift_right_logical(base - shard + (SEQ - 1), 6)
        place = (first + slot) * SEQ + shard
        valid = (
            ((spot & 1) == 0)
            & (place < length)
            & ((place < SINKS) | (place >= length - WINDOW))
        )
        valid_s = ((spot_s & 1) == 0) & (
            length - WINDOW > lax.shift_right_logical(spot_s, 1)
        )
        q = block_rows(0, k)
        q = (q * cosine + pltpu.roll(q, HD // 2, 1) * sine).astype(jnp.bfloat16)
        old = KV[:, pl.ds(xat(k), 1)].reshape(SEQ * SLOTS * 2, HD)
        old_s = SK[:, pl.ds(xat(k), 1)].reshape(2 * SINKS, HD)
        s = jnp.where(valid, nt(q, old) * scale, -1e30)
        s_s = jnp.where(valid_s, nt(q, old_s) * scale, -1e30)
        top = jnp.maximum(
            jnp.max(s, axis=-1, keepdims=True), jnp.max(s_s, axis=-1, keepdims=True)
        )
        w = jnp.where(valid, jnp.exp(s - top), 0.0)
        wt_s = jnp.where(valid_s, jnp.exp(s_s - top), 0.0)
        total = jnp.sum(w, axis=-1, keepdims=True) + jnp.sum(
            wt_s, axis=-1, keepdims=True
        )
        shifted = pltpu.roll(w, 1, 1).astype(jnp.bfloat16)
        shifted_s = nn(wt_s.astype(jnp.bfloat16), move).astype(jnp.bfloat16)
        weighted = nn(shifted, old) + nn(shifted_s, old_s)
        tree = reach > 0.5
        t = jnp.where(tree, nt(q, keys[k]) * scale, -1e30)
        joint = jnp.maximum(top, jnp.max(t, axis=-1, keepdims=True))
        tw = jnp.where(tree, jnp.exp(t - joint), 0.0)
        ratio = jnp.exp(top - joint)
        summed = nn(tw.astype(jnp.bfloat16), values[k])
        below = total * ratio + jnp.sum(tw, axis=-1, keepdims=True)
        done = ((weighted * ratio + summed) / below).astype(jnp.bfloat16)
        if k == 0:
            ATT[x] = done
        else:
            att[k - 1] = done
            for dx, dz in parts[turn]:
                hop_b(dx, dz)
            send(att.at[k - 1], ATT.at[x], a_s, a_r, idx(k, 0))

    for dx, dz in parts[3]:
        hop_b(dx, dz)
    all_of(ATT.at[pl.ds(0, X - 1)], a_r)
    a = jnp.concatenate([ATT[h] for h in range(HEADS)], axis=1)
    all_of(WO.at[pl.ds(0, SEQ // CORES)], bsib_r)
    wide_group = SEQ // TP
    turns = (2, 1, 3, 0)
    for at, k in enumerate(turns):
        t = lax.rem(tp + k, TP)
        right = WO[pl.ds(t * wide_group, wide_group)].reshape(WIDTH, WIDTH)
        part[t] = nt(a, right).astype(jnp.bfloat16)
        if at:
            t = lax.rem(tp + turns[at - 1], TP)
            pltpu.make_async_remote_copy(
                src_ref=part.at[t], dst_ref=PG.at[tp], send_sem=ps, recv_sem=pr,
                device_id={"tp": t},
            ).start()

    others = pl.ds(0, SEQ - 1)
    pieces = SEQ // CORES
    all_of(N.at[pl.ds(0, X - 1)], t_s)
    all_of(WH.at[:, pl.ds(0, X - 1), 0], wx_s)
    all_of(WH.at[:, :, pl.ds(0, Z - 1)], w_s)
    all_of(WH.at[:, :, pl.ds(0, Z)], wsib_s)
    all_of(WO.at[pl.ds(0, pieces - 1)], b_s)
    all_of(WO.at[pl.ds(0, pieces)], bsib_s)
    all_of(packed.at[others], kv_s)
    all_of(att, a_s)

    @pl.when(me < SINKS)
    def _():
        all_of(sinks.at[others], sk_s)

    own_g.wait()
    all_of(G.at[others], gr)
    arrived[...] = G[...]
    all_of(PG.at[pl.ds(0, TP - 1)], pr)
    below = part[tp].astype(jnp.float32)
    for k in range(1, TP):
        below = below + PG[lax.rem(tp + k, TP)].astype(jnp.float32)
    gathered[...] = below.astype(jnp.bfloat16)
    all_of(part.at[pl.ds(0, TP - 1)], ps)
    all_of(fresh.at[others], gs)


def final_kernel(deal, code, G, gathered, cache, branch, new_cache, sem):
    copy = pltpu.make_async_copy(cache, new_cache, sem)
    copy.start()
    branch[...] = gathered[...]
    copy.wait()

    def place(i, carry):
        r = deal[i]
        spot = code[0, r]
        far, near = lax.shift_right_logical(i, 4), i & (COLUMN - 1)

        @pl.when(spot >= 0)
        def _():
            for h in range(HEADS):
                new_cache[r, spot, :, h * HD:(h + 1) * HD] = G[h * COLUMN + near, far]

        return carry

    lax.fori_loop(0, ROWS, place, 0, unroll=8)


def whole():
    return pl.BlockSpec(memory_space=pltpu.VMEM)


def shaped(shape, dtype=jnp.bfloat16):
    return jax.ShapeDtypeStruct(shape, dtype)


def run_whole(deal, lengths, leaves, tokens, parents, freq, spans, tips, cache, wq, wo):
    dma = pltpu.SemaphoreType.DMA
    vmem = pltpu.VMEM
    half = jnp.bfloat16
    return pl.pallas_call(
        whole_kernel,
        name="whole",
        in_specs=[pl.BlockSpec(memory_space=pltpu.SMEM)] * 3 + [whole()] * 8,
        out_specs=[whole()] * 3,
        out_shape=[
            shaped((ROWS, WIDTH)),
            shaped((SEQ, X, 2, HD)),
            shaped((1, ROWS), jnp.int32),
        ],
        scratch_shapes=[
            vmem((SEQ, X, 2 * SLOTS, HD), half),
            vmem((SEQ, X, 2, HD), half),
            vmem((X, ROWS, DEEP), half),
            vmem((3, X, COLUMN, DEEP // SEQ, HD), half),
            vmem((SEQ, DEEP // SEQ, WIDTH), half),
            vmem((SEQ, X, 2 * SLOTS, HD), half),
            vmem((SINKS, X, 2, HD), half),
            vmem((3, X * ROWS, HD), jnp.float32),
            vmem((X - 1, ROWS, HD), half),
            vmem((X, ROWS, HD), half),
            vmem((TP, ROWS, WIDTH), half),
            vmem((TP, ROWS, WIDTH), half),
            vmem((SEQ, X, 2, HD), half),
            vmem((SEQ, X, 2, HD), half),
            vmem((ROWS, HD), jnp.int32),
            dma((5,)), dma((4,)), dma((Z,)), dma((X, Z)),
            pltpu.SemaphoreType.REGULAR,
        ] + [dma] * 19,
        compiler_params=pltpu.CompilerParams(collective_id=0, has_side_effects=True),
    )(deal, lengths, leaves, tokens, parents, freq, spans, tips, cache, wq, wo)


def run_final(deal, code, arrived, gathered, cache):
    return pl.pallas_call(
        final_kernel,
        name="final",
        grid_spec=pltpu.PrefetchScalarGridSpec(
            num_scalar_prefetch=2,
            in_specs=[whole(), whole(), pl.BlockSpec(memory_space=pl.ANY)],
            out_specs=[whole()] * 2,
            scratch_shapes=[pltpu.SemaphoreType.DMA],
        ),
        out_shape=[shaped((ROWS, WIDTH)), shaped(cache.shape)],
    )(deal, code, arrived, gathered, cache)


def on_device(tokens, qkv_weight, out_weight, kv_cache, lengths, parents, leaves, deal):
    cache = kv_cache.reshape(kv_cache.shape[0], kv_cache.shape[1], 2, WIDTH)
    half = np.arange(HD, dtype=np.float64) % (HD // 2)
    freq = jnp.asarray((10000.0 ** (-2.0 * half / HD)).astype(np.float32)[None, :])
    wq = jnp.transpose(qkv_weight, (1, 0, 2))
    wo = jnp.transpose(out_weight, (1, 0))
    gathered, arrived, code = run_whole(
        deal, lengths, leaves, tokens, parents, freq,
        lengths.reshape(1, ROWS), leaves.reshape(1, ROWS), cache, wq, wo,
    )
    branch, new_cache = run_final(deal, code, arrived, gathered, cache)
    return branch, new_cache.reshape(kv_cache.shape)


def solution(mesh):
    placed = (
        P("seq", None),
        P("seq", None, "tp"),
        P("tp", "seq"),
        P(None, None, "seq", None, "tp"),
        P(),
        P(),
        P(),
        P(),
    )
    return jax.shard_map(
        on_device,
        mesh=mesh,
        in_specs=placed,
        out_specs=(P("seq", "tp"), P(None, None, "seq", None, "tp")),
        check_vma=False,
    )
```

```python
import functools

import jax
import jax.numpy as jnp
import numpy as np
from jax import lax
from jax.experimental import pallas as pl
from jax.experimental.pallas import tpu as pltpu
from jax.sharding import PartitionSpec as P

HD = 128
SINKS = 4
X, Z, CORES = 4, 8, 2
SEQ = X * Z * CORES
TP = 4
COLUMN = Z * CORES
ROWS = 64
CPOS = 8
CHUNKS = 4
SLOTS = 4
WIDTH = 512
HEADS = WIDTH // HD
WINDOW = 256
DEEP = 2048
KV_PARTS = ((1, 16), (16, 28), (28, 40), (40, 52), (52, 64))


def nt(a, b):
    return lax.dot_general(
        a, b, (((1,), (1,)), ((), ())), preferred_element_type=jnp.float32
    )


def nn(a, b):
    return lax.dot_general(
        a, b, (((1,), (0,)), ((), ())), preferred_element_type=jnp.float32
    )


def whole_kernel(
    deal, lengths, leaves, tokens, parents, freq, spans, tips, deals, cache, wq, wo,
    gathered, arrived, code_out,
    packed, sinks, N, WH, WO, KV, SK, acc, att, ATT, part, PG, fresh, G, par_pad, held,
    own_sem, tr, wr, br, gate,
    t_s, wx_s, wx_r, w_s, wsib_s, wsib_r, b_s, bsib_s, bsib_r,
    kv_s, kv_r, sk_s, sk_r, a_s, a_r, ps, pr, gs, gr,
):
    me = lax.axis_index("seq")
    tp = lax.axis_index("tp")
    x = me // COLUMN
    z = lax.rem(me // CORES, Z)
    c = lax.rem(me, CORES)
    column = lax.rem(me, COLUMN)

    def xat(dx):
        return lax.rem(x + (dx + X), X)

    def qat(dz):
        return lax.rem(z + (dz + Z), Z) * CORES + c

    def idx(dx, dz):
        return xat(dx) * COLUMN + qat(dz)

    def side(h):
        return pl.ds(pl.multiple_of(h * HD, HD), HD)

    def all_of(ref, sem):
        pltpu.make_async_copy(ref, ref, sem).wait()

    def send(src, dst, there, here, target):
        pltpu.make_async_remote_copy(
            src_ref=src, dst_ref=dst, send_sem=there, recv_sem=here,
            device_id={"seq": target},
        ).start()

    own_cache = pltpu.make_async_copy(cache, held, own_sem.at[3])
    own_cache.start()
    barrier = pltpu.get_barrier_semaphore()

    def mate(k):
        return x * COLUMN + lax.rem(column + k, COLUMN)

    for k in range(1, COLUMN):
        pl.semaphore_signal(barrier, 1, device_id={"seq": mate(k)})
    for k in range(1, X):
        pl.semaphore_signal(barrier, 1, device_id={"seq": xat(k) * COLUMN + column})
    for k in range(1, TP):
        pl.semaphore_signal(barrier, 1, device_id={"tp": lax.rem(tp + k, TP)})

    own_w = pltpu.make_async_copy(
        wq.at[:, :, side(x)], WH.at[:, x, column], own_sem.at[0]
    )
    own_w.start()
    own_b = pltpu.make_async_copy(wo, WO.at[me], own_sem.at[1])
    own_b.start()

    wide = tokens[...].astype(jnp.float32)
    centred = wide - jnp.mean(wide, axis=-1, keepdims=True)
    scaling = lax.rsqrt(jnp.mean(centred * centred, axis=-1, keepdims=True) + 1e-05)
    N[x] = (centred * scaling).astype(jnp.bfloat16)

    def pack(t, carry):
        r = deal[t]
        base = jnp.maximum(lengths[r] - WINDOW, 0)
        first = lax.shift_right_logical(base - me + (SEQ - 1), 6)
        rows = held[r, pl.ds(first, SLOTS)].reshape(2 * SLOTS, WIDTH)
        sunk = held[r, 0]
        far, near = t // COLUMN, lax.rem(t, COLUMN)
        for h in range(HEADS):
            packed[h * COLUMN + near, far] = rows[:, h * HD:(h + 1) * HD]
            sinks[h * COLUMN + near, far] = sunk[:, h * HD:(h + 1) * HD]
        return carry

    own_cache.wait()
    lax.fori_loop(0, ROWS, pack, 0)

    pl.semaphore_wait(barrier, COLUMN + X + TP - 3)
    for k in range(1, COLUMN):
        pl.semaphore_signal(gate, 1, device_id={"seq": mate(k)})

    def send_w(dz, step):
        at = WH.at[:, :, qat(dz)]
        if step == 0:
            send(at, at, wsib_s, wsib_r, me + 1 - 2 * c)
        else:
            send(at, at, w_s, wr.at[(dz - step) % Z], idx(0, step))

    def hop_w(dz):
        at = WH.at[:, :, qat(dz)]
        all_of(at, wr.at[dz % Z])
        if -4 < dz < 0:
            send_w(dz, 1)
        elif 0 < dz < 3:
            send_w(dz, -1)
        send_w(dz, 0)

    def send_b(dx, dz, way):
        at = idx(dx, dz)
        src = wo if (dx, dz) == (0, 0) else WO.at[at]
        if way == "s":
            send(src, WO.at[at], bsib_s, bsib_r, me + 1 - 2 * c)
        else:
            ox, oz = {"x+": (1, 0), "x-": (-1, 0), "z+": (0, 1), "z-": (0, -1)}[way]
            send(
                src, WO.at[at], b_s, br.at[(dx - ox) % X, (dz - oz) % Z], idx(ox, oz)
            )

    def hop_b(dx, dz):
        if (dx, dz) != (0, 0):
            all_of(WO.at[idx(dx, dz)], br.at[dx % X, dz % Z])
        out = []
        if dx == 0:
            if dz == 0:
                out += ["z+", "z-"]
            elif -3 < dz < 0:
                out += ["z+"]
            elif 0 < dz < 4:
                out += ["z-"]
            out += ["x+", "x-"]
        elif dx == -1 and dz % 2 == 0:
            out += ["x+"]
        elif dx == 1 and dz % 2 == 1:
            out += ["x-"]
        for way in out + ["s"]:
            send_b(dx, dz, way)

    for k in (2, 1, 3):
        send(
            wq.at[:, :, side(xat(k))], WH.at[:, x, column], wx_s, wx_r, idx(k, 0)
        )
    own_b.wait()
    hop_b(0, 0)
    send(N.at[x], N.at[x], t_s, tr.at[0], idx(1, 0))
    send(N.at[x], N.at[x], t_s, tr.at[1], idx(-1, 0))

    own_kv = pltpu.make_async_copy(packed.at[me], KV.at[me], own_sem.at[2])
    own_kv.start()

    def scatter(low, high):
        def one(k, carry):
            t = xat(k // COLUMN) * COLUMN + lax.rem(column + k, COLUMN)
            send(packed.at[t], KV.at[me], kv_s, kv_r, t)
            return carry

        lax.fori_loop(low, high, one, 0)

    scatter(*KV_PARTS[0])
    pl.semaphore_wait(gate, COLUMN - 1)

    sub = lax.broadcasted_iota(jnp.int32, (ROWS, ROWS), 0)
    lane = lax.broadcasted_iota(jnp.int32, (ROWS, ROWS), 1)
    lanes = lax.broadcasted_iota(jnp.int32, (ROWS, HD), 1)
    eye = jnp.where(sub == lane, 1.0, 0.0)

    def describe(k):
        request = deal[xat(k) * COLUMN + column]
        length = lengths[request]
        leaf = leaves[request]
        row = parents[pl.ds(request, 1), :]
        up = eye + jnp.where(row == sub, 1.0, 0.0)
        for _ in range(6):
            half = up.astype(jnp.bfloat16)
            up = jnp.minimum(nn(half, half), 1.0)
        reach = nt(eye.astype(jnp.bfloat16), up.astype(jnp.bfloat16))
        depth_row = (jnp.sum(up, axis=0, keepdims=True) - 1.0).astype(jnp.int32)
        depth_col = (jnp.sum(reach, axis=1, keepdims=True) - 1.0).astype(jnp.int32)
        angle = (length + depth_col).astype(jnp.float32) * freq[...]
        cosine = jnp.cos(angle)
        wave = jnp.sin(angle)
        sine = jnp.where(lanes < HD // 2, -wave, wave)
        on_path = jnp.sum(jnp.where(sub == leaf, reach, 0.0), axis=0, keepdims=True)
        offset = lax.rem(sub - length + 8 * SEQ, SEQ)
        hit = (on_path > 0.5) & (depth_row == offset)
        pick = jnp.where(hit, 1.0, 0.0).astype(jnp.bfloat16)
        return length, reach, cosine, sine, pick

    def table():
        par_pad[...] = lanes
        par_pad[:, 0:ROWS] = parents[...]
        par = par_pad[...]
        climb = jnp.where((lanes < ROWS) & (par >= 0), 1, 0)
        jump = jnp.where(par < 0, 0, par)
        for _ in range(6):
            climb = climb + jnp.take_along_axis(climb, jump, axis=1)
            jump = jnp.take_along_axis(jump, jump, axis=1)
        tip = jnp.sum(jnp.where(sub == lane, tips[...], 0), axis=1, keepdims=True)
        span = jnp.sum(jnp.where(sub == lane, spans[...], 0), axis=1, keepdims=True)
        end = jnp.sum(jnp.where(lanes == tip, climb, 0), axis=1, keepdims=True)
        tree_of = jnp.sum(jnp.where(deals[...] == sub, lane, 0), axis=1, keepdims=True)
        ahead = (me - span + 8 * SEQ) & (SEQ - 1)
        code = jnp.where(
            ahead <= end, lax.shift_right_logical(span + ahead, 6) + CPOS * tree_of, -1
        )
        code_out[...] = jnp.sum(
            jnp.where(sub == lane, code, 0), axis=0, keepdims=True
        )

    order = (2, 1, 3, 0)
    told = {order[0]: describe(order[0])}

    own_w.wait()
    all_of(WH.at[:, pl.ds(0, X - 1), 0], wx_r)
    send_w(0, 1)
    send_w(0, -1)
    send_w(0, 0)
    hop_b(0, -1)
    hop_b(0, 1)
    scatter(*KV_PARTS[1])
    told[order[1]] = describe(order[1])

    left, right = pl.ds(0, DEEP // 2), pl.ds(DEEP // 2, DEEP // 2)
    hop_w(-1)
    hop_w(1)
    hop_b(0, -2)
    hop_b(0, 2)
    all_of(N.at[0], tr.at[0])
    at = N.at[xat(-1), :, left]
    send(at, at, t_s, tr.at[2], idx(1, 0))
    all_of(N.at[0], tr.at[1])
    at = N.at[xat(1), :, right]
    send(at, at, t_s, tr.at[3], idx(-1, 0))
    scatter(*KV_PARTS[2])

    @pl.when(me < SINKS)
    def _():
        pltpu.make_async_copy(sinks.at[me], SK.at[me], sk_r).start()

        def spread(k, carry):
            t = lax.rem(me + k, SEQ)
            send(sinks.at[t], SK.at[me], sk_s, sk_r, t)
            return carry

        lax.fori_loop(1, SEQ, spread, 0)

    told[order[2]] = describe(order[2])
    hop_w(-2)
    hop_w(2)
    hop_b(0, -3)
    hop_b(0, 3)
    scatter(*KV_PARTS[3])
    told[order[3]] = describe(order[3])
    hop_b(-1, 0)
    hop_b(1, 0)
    hop_w(-3)
    hop_w(3)
    hop_b(0, -4)
    scatter(*KV_PARTS[4])
    table()
    for dz in (-1, 1):
        hop_b(-1, dz)
        hop_b(1, dz)
    hop_w(-4)
    for dz in (-2, 2):
        hop_b(-1, dz)
        hop_b(1, dz)

    all_of(N.at[0, :, left], tr.at[2])
    all_of(N.at[0, :, right], tr.at[3])
    all_of(WH.at[:, :, pl.ds(0, Z)], wsib_r)
    deep = COLUMN * (DEEP // SEQ)
    rows_all = X * ROWS
    for kind in range(3):
        total = None
        for block in range(X):
            mine = N[:, :, block * deep:(block + 1) * deep].reshape(rows_all, deep)
            term = nn(mine, WH[kind, block].reshape(deep, HD))
            total = term if total is None else total + term
        acc[kind] = total

    twice = lax.broadcasted_iota(jnp.int32, (2 * SEQ, SEQ), 0)
    once = lax.broadcasted_iota(jnp.int32, (2 * SEQ, SEQ), 1)
    even = jnp.where(twice == 2 * once, 1.0, 0.0).astype(jnp.bfloat16)
    odd = jnp.where(twice == 2 * once + 1, 1.0, 0.0).astype(jnp.bfloat16)

    def block_rows(kind, k):
        return acc[kind, pl.ds(pl.multiple_of(xat(k) * ROWS, ROWS), ROWS)]

    keys, values = {}, {}
    for k in order:
        _, _, cosine, sine, pick = told[k]
        key = block_rows(1, k)
        key = key * cosine + pltpu.roll(key, HD // 2, 1) * sine
        keys[k] = key.astype(jnp.bfloat16)
        values[k] = block_rows(2, k).astype(jnp.bfloat16)
        pick_k = nn(even, pick).astype(jnp.bfloat16)
        pick_v = nn(odd, pick).astype(jnp.bfloat16)
        mixed = (nn(pick_k, keys[k]) + nn(pick_v, values[k])).astype(jnp.bfloat16)
        fresh[:, xat(k)] = mixed.reshape(SEQ, 2, HD)
    for dz in (-3, 3, -4):
        hop_b(-1, dz)
        hop_b(1, dz)

    own_g = pltpu.make_async_copy(fresh.at[me], G.at[me], own_sem.at[4])
    own_g.start()

    def hand(k, carry):
        t = lax.rem(me + k, SEQ)
        send(fresh.at[t], G.at[me], gs, gr, t)
        return carry

    lax.fori_loop(1, SEQ, hand, 0)

    later = [(-2, dz) for dz in (0, -1, 1, -2, 2, -3, 3, -4)]
    parts = [later[0:3], later[3:5], later[5:7], later[7:8]]

    own_kv.wait()
    all_of(KV.at[pl.ds(0, SEQ - 1)], kv_r)
    all_of(SK, sk_r)

    scale = float(HD) ** (-0.5)
    spot = lax.broadcasted_iota(jnp.int32, (ROWS, SEQ * SLOTS * 2), 1)
    shard = lax.shift_right_logical(spot, 3)
    slot = lax.shift_right_logical(spot & 7, 1)
    spot_s = lax.broadcasted_iota(jnp.int32, (ROWS, 2 * SINKS), 1)
    small = (2 * SINKS, 2 * SINKS)
    move = jnp.where(
        lax.broadcasted_iota(jnp.int32, small, 0) + 1
        == lax.broadcasted_iota(jnp.int32, small, 1),
        1.0, 0.0,
    ).astype(jnp.bfloat16)

    for turn, k in enumerate(order):
        length, reach, cosine, sine, _ = told[k]
        base = jnp.maximum(length - WINDOW, 0)
        first = lax.shift_right_logical(base - shard + (SEQ - 1), 6)
        place = (first + slot) * SEQ + shard
        valid = (
            ((spot & 1) == 0)
            & (place < length)
            & ((place < SINKS) | (place >= length - WINDOW))
        )
        valid_s = ((spot_s & 1) == 0) & (
            length - WINDOW > lax.shift_right_logical(spot_s, 1)
        )
        q = block_rows(0, k)
        q = (q * cosine + pltpu.roll(q, HD // 2, 1) * sine).astype(jnp.bfloat16)
        old = KV[:, pl.ds(xat(k), 1)].reshape(SEQ * SLOTS * 2, HD)
        old_s = SK[:, pl.ds(xat(k), 1)].reshape(2 * SINKS, HD)
        s = jnp.where(valid, nt(q, old) * scale, -1e30)
        s_s = jnp.where(valid_s, nt(q, old_s) * scale, -1e30)
        top = jnp.maximum(
            jnp.max(s, axis=-1, keepdims=True), jnp.max(s_s, axis=-1, keepdims=True)
        )
        w = jnp.where(valid, jnp.exp(s - top), 0.0)
        wt_s = jnp.where(valid_s, jnp.exp(s_s - top), 0.0)
        total = jnp.sum(w, axis=-1, keepdims=True) + jnp.sum(
            wt_s, axis=-1, keepdims=True
        )
        shifted = pltpu.roll(w, 1, 1).astype(jnp.bfloat16)
        shifted_s = nn(wt_s.astype(jnp.bfloat16), move).astype(jnp.bfloat16)
        weighted = nn(shifted, old) + nn(shifted_s, old_s)
        tree = reach > 0.5
        t = jnp.where(tree, nt(q, keys[k]) * scale, -1e30)
        joint = jnp.maximum(top, jnp.max(t, axis=-1, keepdims=True))
        tw = jnp.where(tree, jnp.exp(t - joint), 0.0)
        ratio = jnp.exp(top - joint)
        summed = nn(tw.astype(jnp.bfloat16), values[k])
        below = total * ratio + jnp.sum(tw, axis=-1, keepdims=True)
        done = ((weighted * ratio + summed) / below).astype(jnp.bfloat16)
        if k == 0:
            ATT[x] = done
        else:
            att[k - 1] = done
            for dx, dz in parts[turn]:
                hop_b(dx, dz)
            send(att.at[k - 1], ATT.at[x], a_s, a_r, idx(k, 0))

    for dx, dz in parts[3]:
        hop_b(dx, dz)
    all_of(ATT.at[pl.ds(0, X - 1)], a_r)
    a = jnp.concatenate([ATT[h] for h in range(HEADS)], axis=1)
    all_of(WO.at[pl.ds(0, SEQ // CORES)], bsib_r)
    wide_group = SEQ // TP
    turns = (2, 1, 3, 0)
    for at, k in enumerate(turns):
        t = lax.rem(tp + k, TP)
        right = WO[pl.ds(t * wide_group, wide_group)].reshape(WIDTH, WIDTH)
        part[t] = nt(a, right).astype(jnp.bfloat16)
        if at:
            t = lax.rem(tp + turns[at - 1], TP)
            pltpu.make_async_remote_copy(
                src_ref=part.at[t], dst_ref=PG.at[tp], send_sem=ps, recv_sem=pr,
                device_id={"tp": t},
            ).start()

    others = pl.ds(0, SEQ - 1)
    pieces = SEQ // CORES
    all_of(N.at[pl.ds(0, X - 1)], t_s)
    all_of(WH.at[:, pl.ds(0, X - 1), 0], wx_s)
    all_of(WH.at[:, :, pl.ds(0, Z - 1)], w_s)
    all_of(WH.at[:, :, pl.ds(0, Z)], wsib_s)
    all_of(WO.at[pl.ds(0, pieces - 1)], b_s)
    all_of(WO.at[pl.ds(0, pieces)], bsib_s)
    all_of(packed.at[others], kv_s)
    all_of(att, a_s)

    @pl.when(me < SINKS)
    def _():
        all_of(sinks.at[others], sk_s)

    own_g.wait()
    all_of(G.at[others], gr)
    arrived[...] = G[...]
    all_of(PG.at[pl.ds(0, TP - 1)], pr)
    below = part[tp].astype(jnp.float32)
    for k in range(1, TP):
        below = below + PG[lax.rem(tp + k, TP)].astype(jnp.float32)
    gathered[...] = below.astype(jnp.bfloat16)
    all_of(part.at[pl.ds(0, TP - 1)], ps)
    all_of(fresh.at[others], gs)


def final_kernel(code, G, gathered, cache, branch, new_cache, held, come, leave):
    chunk = ROWS // CHUNKS
    spans = [pl.ds(j * chunk, chunk) for j in range(CHUNKS)]
    ins = [
        pltpu.make_async_copy(cache.at[at], held.at[at], come.at[j])
        for j, at in enumerate(spans)
    ]
    outs = [
        pltpu.make_async_copy(held.at[at], new_cache.at[at], leave.at[j])
        for j, at in enumerate(spans)
    ]
    for copy in ins:
        copy.start()
    branch[...] = gathered[...]
    for j in range(CHUNKS):
        ins[j].wait()
        for r in range(j * chunk, (j + 1) * chunk):
            tag = code[0, r]

            @pl.when(tag >= 0)
            def _():
                spot = tag & (CPOS - 1)
                near = lax.shift_right_logical(tag, 3) & (COLUMN - 1)
                far = lax.shift_right_logical(tag, 7)
                for h in range(HEADS):
                    held[r, spot, :, h * HD:(h + 1) * HD] = G[h * COLUMN + near, far]

        outs[j].start()
    for copy in outs:
        copy.wait()


def whole():
    return pl.BlockSpec(memory_space=pltpu.VMEM)


def shaped(shape, dtype=jnp.bfloat16):
    return jax.ShapeDtypeStruct(shape, dtype)


def run_whole(deal, lengths, leaves, tokens, parents, freq, spans, tips, deals, cache, wq, wo):
    dma = pltpu.SemaphoreType.DMA
    vmem = pltpu.VMEM
    half = jnp.bfloat16
    return pl.pallas_call(
        whole_kernel,
        name="whole",
        in_specs=[pl.BlockSpec(memory_space=pltpu.SMEM)] * 3 + [whole()] * 6
        + [pl.BlockSpec(memory_space=pl.ANY)] + [whole()] * 2,
        out_specs=[whole()] * 3,
        out_shape=[
            shaped((ROWS, WIDTH)),
            shaped((SEQ, X, 2, HD)),
            shaped((1, ROWS), jnp.int32),
        ],
        scratch_shapes=[
            vmem((SEQ, X, 2 * SLOTS, HD), half),
            vmem((SEQ, X, 2, HD), half),
            vmem((X, ROWS, DEEP), half),
            vmem((3, X, COLUMN, DEEP // SEQ, HD), half),
            vmem((SEQ, DEEP // SEQ, WIDTH), half),
            vmem((SEQ, X, 2 * SLOTS, HD), half),
            vmem((SINKS, X, 2, HD), half),
            vmem((3, X * ROWS, HD), jnp.float32),
            vmem((X - 1, ROWS, HD), half),
            vmem((X, ROWS, HD), half),
            vmem((TP, ROWS, WIDTH), half),
            vmem((TP, ROWS, WIDTH), half),
            vmem((SEQ, X, 2, HD), half),
            vmem((SEQ, X, 2, HD), half),
            vmem((ROWS, HD), jnp.int32),
            vmem(cache.shape, half),
            dma((5,)), dma((4,)), dma((Z,)), dma((X, Z)),
            pltpu.SemaphoreType.REGULAR,
        ] + [dma] * 19,
        compiler_params=pltpu.CompilerParams(collective_id=0, has_side_effects=True),
    )(deal, lengths, leaves, tokens, parents, freq, spans, tips, deals, cache, wq, wo)


def run_final(code, arrived, gathered, cache):
    dma = pltpu.SemaphoreType.DMA
    outside = pl.BlockSpec(memory_space=pl.ANY)
    return pl.pallas_call(
        final_kernel,
        name="final",
        in_specs=[pl.BlockSpec(memory_space=pltpu.SMEM), whole(), whole(), outside],
        out_specs=[whole(), outside],
        out_shape=[shaped((ROWS, WIDTH)), shaped(cache.shape)],
        scratch_shapes=[
            pltpu.VMEM(cache.shape, jnp.bfloat16), dma((CHUNKS,)), dma((CHUNKS,)),
        ],
    )(code, arrived, gathered, cache)


def on_device(tokens, qkv_weight, out_weight, kv_cache, lengths, parents, leaves, deal):
    cache = kv_cache.reshape(kv_cache.shape[0], kv_cache.shape[1], 2, WIDTH)
    half = np.arange(HD, dtype=np.float64) % (HD // 2)
    freq = jnp.asarray((10000.0 ** (-2.0 * half / HD)).astype(np.float32)[None, :])
    wq = jnp.transpose(qkv_weight, (1, 0, 2))
    wo = jnp.transpose(out_weight, (1, 0))
    gathered, arrived, code = run_whole(
        deal, lengths, leaves, tokens, parents, freq,
        lengths.reshape(1, ROWS), leaves.reshape(1, ROWS), deal.reshape(1, ROWS),
        cache, wq, wo,
    )
    branch, new_cache = run_final(code, arrived, gathered, cache)
    return branch, new_cache.reshape(kv_cache.shape)


def solution(mesh):
    placed = (
        P("seq", None),
        P("seq", None, "tp"),
        P("tp", "seq"),
        P(None, None, "seq", None, "tp"),
        P(),
        P(),
        P(),
        P(),
    )
    return jax.shard_map(
        on_device,
        mesh=mesh,
        in_specs=placed,
        out_specs=(P("seq", "tp"), P(None, None, "seq", None, "tp")),
        check_vma=False,
    )
```

```python
import functools

import jax
import jax.numpy as jnp
import numpy as np
from jax import lax
from jax.experimental import pallas as pl
from jax.experimental.pallas import tpu as pltpu
from jax.sharding import PartitionSpec as P

HD = 128
SINKS = 4
X, Z, CORES = 4, 8, 2
SEQ = X * Z * CORES
TP = 4
COLUMN = Z * CORES
ROWS = 64
CPOS = 8
CHUNKS = 4
SLOTS = 4
WIDTH = 512
HEADS = WIDTH // HD
WINDOW = 256
DEEP = 2048
KV_PARTS = ((1, 16), (16, 28), (28, 40), (40, 52), (52, 64))


def nt(a, b):
    return lax.dot_general(
        a, b, (((1,), (1,)), ((), ())), preferred_element_type=jnp.float32
    )


def nn(a, b):
    return lax.dot_general(
        a, b, (((1,), (0,)), ((), ())), preferred_element_type=jnp.float32
    )


def whole_kernel(
    deal, lengths, leaves, tokens, parents, freq, spans, tips, deals, cache, wq, wo,
    gathered, arrived, code_out,
    packed, sinks, N, WH, WO, KV, SK, acc, att, ATT, part, PG, fresh, G, par_pad, held,
    own_sem, tr, wr, br, gate,
    t_s, wx_s, wx_r, w_s, wsib_s, wsib_r, b_s, bsib_s, bsib_r,
    kv_s, kv_r, sk_s, sk_r, a_s, a_r, ps, pr, gs, gr,
):
    me = lax.axis_index("seq")
    tp = lax.axis_index("tp")
    x = me // COLUMN
    z = lax.rem(me // CORES, Z)
    c = lax.rem(me, CORES)
    column = lax.rem(me, COLUMN)

    def xat(dx):
        return lax.rem(x + (dx + X), X)

    def qat(dz):
        return lax.rem(z + (dz + Z), Z) * CORES + c

    def idx(dx, dz):
        return xat(dx) * COLUMN + qat(dz)

    def side(h):
        return pl.ds(pl.multiple_of(h * HD, HD), HD)

    def all_of(ref, sem):
        pltpu.make_async_copy(ref, ref, sem).wait()

    def send(src, dst, there, here, target):
        pltpu.make_async_remote_copy(
            src_ref=src, dst_ref=dst, send_sem=there, recv_sem=here,
            device_id={"seq": target},
        ).start()

    own_cache = pltpu.make_async_copy(cache, held, own_sem.at[3])
    own_cache.start()
    barrier = pltpu.get_barrier_semaphore()

    def mate(k):
        return x * COLUMN + lax.rem(column + k, COLUMN)

    for k in range(1, COLUMN):
        pl.semaphore_signal(barrier, 1, device_id={"seq": mate(k)})
    for k in range(1, X):
        pl.semaphore_signal(barrier, 1, device_id={"seq": xat(k) * COLUMN + column})
    for k in range(1, TP):
        pl.semaphore_signal(barrier, 1, device_id={"tp": lax.rem(tp + k, TP)})

    own_w = pltpu.make_async_copy(
        wq.at[:, :, side(x)], WH.at[:, x, column], own_sem.at[0]
    )
    own_w.start()
    own_b = pltpu.make_async_copy(wo, WO.at[me], own_sem.at[1])
    own_b.start()

    wide = tokens[...].astype(jnp.float32)
    centred = wide - jnp.mean(wide, axis=-1, keepdims=True)
    scaling = lax.rsqrt(jnp.mean(centred * centred, axis=-1, keepdims=True) + 1e-05)
    N[x] = (centred * scaling).astype(jnp.bfloat16)

    def pack(t, carry):
        r = deal[t]
        base = jnp.maximum(lengths[r] - WINDOW, 0)
        first = lax.shift_right_logical(base - me + (SEQ - 1), 6)
        rows = held[r, pl.ds(first, SLOTS)].reshape(2 * SLOTS, WIDTH)
        sunk = held[r, 0]
        far, near = t // COLUMN, lax.rem(t, COLUMN)
        for h in range(HEADS):
            packed[h * COLUMN + near, far] = rows[:, h * HD:(h + 1) * HD]
            sinks[h * COLUMN + near, far] = sunk[:, h * HD:(h + 1) * HD]
        return carry

    own_cache.wait()
    lax.fori_loop(0, ROWS, pack, 0)

    pl.semaphore_wait(barrier, COLUMN + X + TP - 3)
    for k in range(1, COLUMN):
        pl.semaphore_signal(gate, 1, device_id={"seq": mate(k)})

    def half_w(dz, half):
        return WH.at[:, pl.ds(half * (X // 2), X // 2), qat(dz)]

    def send_w(dz, step, half):
        at = half_w(dz, half)
        send(at, at, w_s, wr.at[(dz - step) % Z, half], idx(0, step))

    def pass_w(dz):
        at = WH.at[:, :, qat(dz)]
        send(at, at, wsib_s, wsib_r, me + 1 - 2 * c)

    def hop_w(dz):
        for half in range(2):
            all_of(half_w(dz, half), wr.at[dz % Z, half])
            if -4 < dz < 0:
                send_w(dz, 1, half)
            elif 0 < dz < 3:
                send_w(dz, -1, half)
        pass_w(dz)

    def send_b(dx, dz, way):
        at = idx(dx, dz)
        src = wo if (dx, dz) == (0, 0) else WO.at[at]
        if way == "s":
            send(src, WO.at[at], bsib_s, bsib_r, me + 1 - 2 * c)
        else:
            ox, oz = {"x+": (1, 0), "x-": (-1, 0), "z+": (0, 1), "z-": (0, -1)}[way]
            send(
                src, WO.at[at], b_s, br.at[(dx - ox) % X, (dz - oz) % Z], idx(ox, oz)
            )

    def hop_b(dx, dz):
        if (dx, dz) != (0, 0):
            all_of(WO.at[idx(dx, dz)], br.at[dx % X, dz % Z])
        out = []
        if dx == 0:
            if dz == 0:
                out += ["z+", "z-"]
            elif -3 < dz < 0:
                out += ["z+"]
            elif 0 < dz < 4:
                out += ["z-"]
            out += ["x+", "x-"]
        elif dx == -1 and dz % 2 == 0:
            out += ["x+"]
        elif dx == 1 and dz % 2 == 1:
            out += ["x-"]
        for way in out + ["s"]:
            send_b(dx, dz, way)

    for k in (2, 1, 3):
        send(
            wq.at[:, :, side(xat(k))], WH.at[:, x, column], wx_s, wx_r, idx(k, 0)
        )
    own_b.wait()
    hop_b(0, 0)
    send(N.at[x], N.at[x], t_s, tr.at[0], idx(1, 0))
    send(N.at[x], N.at[x], t_s, tr.at[1], idx(-1, 0))

    own_kv = pltpu.make_async_copy(packed.at[me], KV.at[me], own_sem.at[2])
    own_kv.start()

    def scatter(low, high):
        def one(k, carry):
            t = xat(k // COLUMN) * COLUMN + lax.rem(column + k, COLUMN)
            send(packed.at[t], KV.at[me], kv_s, kv_r, t)
            return carry

        lax.fori_loop(low, high, one, 0)

    scatter(*KV_PARTS[0])
    pl.semaphore_wait(gate, COLUMN - 1)

    sub = lax.broadcasted_iota(jnp.int32, (ROWS, ROWS), 0)
    lane = lax.broadcasted_iota(jnp.int32, (ROWS, ROWS), 1)
    lanes = lax.broadcasted_iota(jnp.int32, (ROWS, HD), 1)
    eye = jnp.where(sub == lane, 1.0, 0.0)

    def describe(k):
        request = deal[xat(k) * COLUMN + column]
        length = lengths[request]
        leaf = leaves[request]
        row = parents[pl.ds(request, 1), :]
        up = eye + jnp.where(row == sub, 1.0, 0.0)
        for _ in range(6):
            half = up.astype(jnp.bfloat16)
            up = jnp.minimum(nn(half, half), 1.0)
        reach = nt(eye.astype(jnp.bfloat16), up.astype(jnp.bfloat16))
        depth_row = (jnp.sum(up, axis=0, keepdims=True) - 1.0).astype(jnp.int32)
        depth_col = (jnp.sum(reach, axis=1, keepdims=True) - 1.0).astype(jnp.int32)
        angle = (length + depth_col).astype(jnp.float32) * freq[...]
        cosine = jnp.cos(angle)
        wave = jnp.sin(angle)
        sine = jnp.where(lanes < HD // 2, -wave, wave)
        on_path = jnp.sum(jnp.where(sub == leaf, reach, 0.0), axis=0, keepdims=True)
        offset = lax.rem(sub - length + 8 * SEQ, SEQ)
        hit = (on_path > 0.5) & (depth_row == offset)
        pick = jnp.where(hit, 1.0, 0.0).astype(jnp.bfloat16)
        return length, reach, cosine, sine, pick

    def table():
        par_pad[...] = lanes
        par_pad[:, 0:ROWS] = parents[...]
        par = par_pad[...]
        climb = jnp.where((lanes < ROWS) & (par >= 0), 1, 0)
        jump = jnp.where(par < 0, 0, par)
        for _ in range(6):
            climb = climb + jnp.take_along_axis(climb, jump, axis=1)
            jump = jnp.take_along_axis(jump, jump, axis=1)
        tip = jnp.sum(jnp.where(sub == lane, tips[...], 0), axis=1, keepdims=True)
        span = jnp.sum(jnp.where(sub == lane, spans[...], 0), axis=1, keepdims=True)
        end = jnp.sum(jnp.where(lanes == tip, climb, 0), axis=1, keepdims=True)
        tree_of = jnp.sum(jnp.where(deals[...] == sub, lane, 0), axis=1, keepdims=True)
        ahead = (me - span + 8 * SEQ) & (SEQ - 1)
        code = jnp.where(
            ahead <= end, lax.shift_right_logical(span + ahead, 6) + CPOS * tree_of, -1
        )
        code_out[...] = jnp.sum(
            jnp.where(sub == lane, code, 0), axis=0, keepdims=True
        )

    order = (2, 1, 3, 0)
    told = {order[0]: describe(order[0])}

    own_w.wait()
    all_of(WH.at[:, pl.ds(0, X - 1), 0], wx_r)
    for half in range(2):
        send_w(0, 1, half)
        send_w(0, -1, half)
    pass_w(0)
    hop_b(0, -1)
    hop_b(0, 1)
    scatter(*KV_PARTS[1])
    told[order[1]] = describe(order[1])

    left, right = pl.ds(0, DEEP // 2), pl.ds(DEEP // 2, DEEP // 2)
    hop_w(-1)
    hop_w(1)
    hop_b(0, -2)
    hop_b(0, 2)
    all_of(N.at[0], tr.at[0])
    at = N.at[xat(-1), :, left]
    send(at, at, t_s, tr.at[2], idx(1, 0))
    all_of(N.at[0], tr.at[1])
    at = N.at[xat(1), :, right]
    send(at, at, t_s, tr.at[3], idx(-1, 0))
    scatter(*KV_PARTS[2])

    @pl.when(me < SINKS)
    def _():
        pltpu.make_async_copy(sinks.at[me], SK.at[me], sk_r).start()

        def spread(k, carry):
            t = lax.rem(me + k, SEQ)
            send(sinks.at[t], SK.at[me], sk_s, sk_r, t)
            return carry

        lax.fori_loop(1, SEQ, spread, 0)

    told[order[2]] = describe(order[2])
    hop_w(-2)
    hop_w(2)
    hop_b(0, -3)
    hop_b(0, 3)
    scatter(*KV_PARTS[3])
    told[order[3]] = describe(order[3])
    hop_b(-1, 0)
    hop_b(1, 0)
    hop_w(-3)
    hop_w(3)
    hop_b(0, -4)
    scatter(*KV_PARTS[4])
    table()
    for dz in (-1, 1):
        hop_b(-1, dz)
        hop_b(1, dz)
    hop_w(-4)
    for dz in (-2, 2):
        hop_b(-1, dz)
        hop_b(1, dz)

    all_of(N.at[0, :, left], tr.at[2])
    all_of(N.at[0, :, right], tr.at[3])
    all_of(WH.at[:, :, pl.ds(0, Z)], wsib_r)
    deep = COLUMN * (DEEP // SEQ)
    rows_all = X * ROWS
    for kind in range(3):
        total = None
        for block in range(X):
            mine = N[:, :, block * deep:(block + 1) * deep].reshape(rows_all, deep)
            term = nn(mine, WH[kind, block].reshape(deep, HD))
            total = term if total is None else total + term
        acc[kind] = total

    twice = lax.broadcasted_iota(jnp.int32, (2 * SEQ, SEQ), 0)
    once = lax.broadcasted_iota(jnp.int32, (2 * SEQ, SEQ), 1)
    even = jnp.where(twice == 2 * once, 1.0, 0.0).astype(jnp.bfloat16)
    odd = jnp.where(twice == 2 * once + 1, 1.0, 0.0).astype(jnp.bfloat16)

    def block_rows(kind, k):
        return acc[kind, pl.ds(pl.multiple_of(xat(k) * ROWS, ROWS), ROWS)]

    keys, values = {}, {}
    for k in order:
        _, _, cosine, sine, pick = told[k]
        key = block_rows(1, k)
        key = key * cosine + pltpu.roll(key, HD // 2, 1) * sine
        keys[k] = key.astype(jnp.bfloat16)
        values[k] = block_rows(2, k).astype(jnp.bfloat16)
        pick_k = nn(even, pick).astype(jnp.bfloat16)
        pick_v = nn(odd, pick).astype(jnp.bfloat16)
        mixed = (nn(pick_k, keys[k]) + nn(pick_v, values[k])).astype(jnp.bfloat16)
        fresh[:, xat(k)] = mixed.reshape(SEQ, 2, HD)
    for dz in (-3, 3, -4):
        hop_b(-1, dz)
        hop_b(1, dz)

    own_g = pltpu.make_async_copy(fresh.at[me], G.at[me], own_sem.at[4])
    own_g.start()

    def hand(k, carry):
        t = lax.rem(me + k, SEQ)
        send(fresh.at[t], G.at[me], gs, gr, t)
        return carry

    lax.fori_loop(1, SEQ, hand, 0)

    later = [(-2, dz) for dz in (0, -1, 1, -2, 2, -3, 3, -4)]
    parts = [later[0:3], later[3:5], later[5:7], later[7:8]]

    own_kv.wait()
    all_of(KV.at[pl.ds(0, SEQ - 1)], kv_r)
    all_of(SK, sk_r)

    scale = float(HD) ** (-0.5)
    spot = lax.broadcasted_iota(jnp.int32, (ROWS, SEQ * SLOTS * 2), 1)
    shard = lax.shift_right_logical(spot, 3)
    slot = lax.shift_right_logical(spot & 7, 1)
    spot_s = lax.broadcasted_iota(jnp.int32, (ROWS, 2 * SINKS), 1)
    small = (2 * SINKS, 2 * SINKS)
    move = jnp.where(
        lax.broadcasted_iota(jnp.int32, small, 0) + 1
        == lax.broadcasted_iota(jnp.int32, small, 1),
        1.0, 0.0,
    ).astype(jnp.bfloat16)

    for turn, k in enumerate(order):
        length, reach, cosine, sine, _ = told[k]
        base = jnp.maximum(length - WINDOW, 0)
        first = lax.shift_right_logical(base - shard + (SEQ - 1), 6)
        place = (first + slot) * SEQ + shard
        valid = (
            ((spot & 1) == 0)
            & (place < length)
            & ((place < SINKS) | (place >= length - WINDOW))
        )
        valid_s = ((spot_s & 1) == 0) & (
            length - WINDOW > lax.shift_right_logical(spot_s, 1)
        )
        q = block_rows(0, k)
        q = (q * cosine + pltpu.roll(q, HD // 2, 1) * sine).astype(jnp.bfloat16)
        old = KV[:, pl.ds(xat(k), 1)].reshape(SEQ * SLOTS * 2, HD)
        old_s = SK[:, pl.ds(xat(k), 1)].reshape(2 * SINKS, HD)
        s = jnp.where(valid, nt(q, old) * scale, -1e30)
        s_s = jnp.where(valid_s, nt(q, old_s) * scale, -1e30)
        top = jnp.maximum(
            jnp.max(s, axis=-1, keepdims=True), jnp.max(s_s, axis=-1, keepdims=True)
        )
        w = jnp.where(valid, jnp.exp(s - top), 0.0)
        wt_s = jnp.where(valid_s, jnp.exp(s_s - top), 0.0)
        total = jnp.sum(w, axis=-1, keepdims=True) + jnp.sum(
            wt_s, axis=-1, keepdims=True
        )
        shifted = pltpu.roll(w, 1, 1).astype(jnp.bfloat16)
        shifted_s = nn(wt_s.astype(jnp.bfloat16), move).astype(jnp.bfloat16)
        weighted = nn(shifted, old) + nn(shifted_s, old_s)
        tree = reach > 0.5
        t = jnp.where(tree, nt(q, keys[k]) * scale, -1e30)
        joint = jnp.maximum(top, jnp.max(t, axis=-1, keepdims=True))
        tw = jnp.where(tree, jnp.exp(t - joint), 0.0)
        ratio = jnp.exp(top - joint)
        summed = nn(tw.astype(jnp.bfloat16), values[k])
        below = total * ratio + jnp.sum(tw, axis=-1, keepdims=True)
        done = ((weighted * ratio + summed) / below).astype(jnp.bfloat16)
        if k == 0:
            ATT[x] = done
        else:
            att[k - 1] = done
            for dx, dz in parts[turn]:
                hop_b(dx, dz)
            send(att.at[k - 1], ATT.at[x], a_s, a_r, idx(k, 0))

    for dx, dz in parts[3]:
        hop_b(dx, dz)
    all_of(ATT.at[pl.ds(0, X - 1)], a_r)
    a = jnp.concatenate([ATT[h] for h in range(HEADS)], axis=1)
    all_of(WO.at[pl.ds(0, SEQ // CORES)], bsib_r)
    wide_group = SEQ // TP
    turns = (2, 1, 3, 0)
    for at, k in enumerate(turns):
        t = lax.rem(tp + k, TP)
        right = WO[pl.ds(t * wide_group, wide_group)].reshape(WIDTH, WIDTH)
        part[t] = nt(a, right).astype(jnp.bfloat16)
        if at:
            t = lax.rem(tp + turns[at - 1], TP)
            pltpu.make_async_remote_copy(
                src_ref=part.at[t], dst_ref=PG.at[tp], send_sem=ps, recv_sem=pr,
                device_id={"tp": t},
            ).start()

    others = pl.ds(0, SEQ - 1)
    pieces = SEQ // CORES
    all_of(N.at[pl.ds(0, X - 1)], t_s)
    all_of(WH.at[:, pl.ds(0, X - 1), 0], wx_s)
    all_of(WH.at[:, :, pl.ds(0, Z - 1)], w_s)
    all_of(WH.at[:, :, pl.ds(0, Z)], wsib_s)
    all_of(WO.at[pl.ds(0, pieces - 1)], b_s)
    all_of(WO.at[pl.ds(0, pieces)], bsib_s)
    all_of(packed.at[others], kv_s)
    all_of(att, a_s)

    @pl.when(me < SINKS)
    def _():
        all_of(sinks.at[others], sk_s)

    own_g.wait()
    all_of(G.at[others], gr)
    arrived[...] = G[...]
    all_of(PG.at[pl.ds(0, TP - 1)], pr)
    below = part[tp].astype(jnp.float32)
    for k in range(1, TP):
        below = below + PG[lax.rem(tp + k, TP)].astype(jnp.float32)
    gathered[...] = below.astype(jnp.bfloat16)
    all_of(part.at[pl.ds(0, TP - 1)], ps)
    all_of(fresh.at[others], gs)


def final_kernel(code, G, gathered, cache, branch, new_cache, held, come, leave):
    chunk = ROWS // CHUNKS
    spans = [pl.ds(j * chunk, chunk) for j in range(CHUNKS)]
    ins = [
        pltpu.make_async_copy(cache.at[at], held.at[at], come.at[j])
        for j, at in enumerate(spans)
    ]
    outs = [
        pltpu.make_async_copy(held.at[at], new_cache.at[at], leave.at[j])
        for j, at in enumerate(spans)
    ]
    for copy in ins:
        copy.start()
    branch[...] = gathered[...]
    for j in range(CHUNKS):
        ins[j].wait()
        for r in range(j * chunk, (j + 1) * chunk):
            tag = code[0, r]

            @pl.when(tag >= 0)
            def _():
                spot = tag & (CPOS - 1)
                near = lax.shift_right_logical(tag, 3) & (COLUMN - 1)
                far = lax.shift_right_logical(tag, 7)
                for h in range(HEADS):
                    held[r, spot, :, h * HD:(h + 1) * HD] = G[h * COLUMN + near, far]

        outs[j].start()
    for copy in outs:
        copy.wait()


def whole():
    return pl.BlockSpec(memory_space=pltpu.VMEM)


def shaped(shape, dtype=jnp.bfloat16):
    return jax.ShapeDtypeStruct(shape, dtype)


def run_whole(deal, lengths, leaves, tokens, parents, freq, spans, tips, deals, cache, wq, wo):
    dma = pltpu.SemaphoreType.DMA
    vmem = pltpu.VMEM
    half = jnp.bfloat16
    return pl.pallas_call(
        whole_kernel,
        name="whole",
        in_specs=[pl.BlockSpec(memory_space=pltpu.SMEM)] * 3 + [whole()] * 6
        + [pl.BlockSpec(memory_space=pl.ANY)] + [whole()] * 2,
        out_specs=[whole()] * 3,
        out_shape=[
            shaped((ROWS, WIDTH)),
            shaped((SEQ, X, 2, HD)),
            shaped((1, ROWS), jnp.int32),
        ],
        scratch_shapes=[
            vmem((SEQ, X, 2 * SLOTS, HD), half),
            vmem((SEQ, X, 2, HD), half),
            vmem((X, ROWS, DEEP), half),
            vmem((3, X, COLUMN, DEEP // SEQ, HD), half),
            vmem((SEQ, DEEP // SEQ, WIDTH), half),
            vmem((SEQ, X, 2 * SLOTS, HD), half),
            vmem((SINKS, X, 2, HD), half),
            vmem((3, X * ROWS, HD), jnp.float32),
            vmem((X - 1, ROWS, HD), half),
            vmem((X, ROWS, HD), half),
            vmem((TP, ROWS, WIDTH), half),
            vmem((TP, ROWS, WIDTH), half),
            vmem((SEQ, X, 2, HD), half),
            vmem((SEQ, X, 2, HD), half),
            vmem((ROWS, HD), jnp.int32),
            vmem(cache.shape, half),
            dma((5,)), dma((4,)), dma((Z, 2)), dma((X, Z)),
            pltpu.SemaphoreType.REGULAR,
        ] + [dma] * 19,
        compiler_params=pltpu.CompilerParams(collective_id=0, has_side_effects=True),
    )(deal, lengths, leaves, tokens, parents, freq, spans, tips, deals, cache, wq, wo)


def run_final(code, arrived, gathered, cache):
    dma = pltpu.SemaphoreType.DMA
    outside = pl.BlockSpec(memory_space=pl.ANY)
    return pl.pallas_call(
        final_kernel,
        name="final",
        in_specs=[pl.BlockSpec(memory_space=pltpu.SMEM), whole(), whole(), outside],
        out_specs=[whole(), outside],
        out_shape=[shaped((ROWS, WIDTH)), shaped(cache.shape)],
        scratch_shapes=[
            pltpu.VMEM(cache.shape, jnp.bfloat16), dma((CHUNKS,)), dma((CHUNKS,)),
        ],
    )(code, arrived, gathered, cache)


def on_device(tokens, qkv_weight, out_weight, kv_cache, lengths, parents, leaves, deal):
    cache = kv_cache.reshape(kv_cache.shape[0], kv_cache.shape[1], 2, WIDTH)
    half = np.arange(HD, dtype=np.float64) % (HD // 2)
    freq = jnp.asarray((10000.0 ** (-2.0 * half / HD)).astype(np.float32)[None, :])
    wq = jnp.transpose(qkv_weight, (1, 0, 2))
    wo = jnp.transpose(out_weight, (1, 0))
    gathered, arrived, code = run_whole(
        deal, lengths, leaves, tokens, parents, freq,
        lengths.reshape(1, ROWS), leaves.reshape(1, ROWS), deal.reshape(1, ROWS),
        cache, wq, wo,
    )
    branch, new_cache = run_final(code, arrived, gathered, cache)
    return branch, new_cache.reshape(kv_cache.shape)


def solution(mesh):
    placed = (
        P("seq", None),
        P("seq", None, "tp"),
        P("tp", "seq"),
        P(None, None, "seq", None, "tp"),
        P(),
        P(),
        P(),
        P(),
    )
    return jax.shard_map(
        on_device,
        mesh=mesh,
        in_specs=placed,
        out_specs=(P("seq", "tp"), P(None, None, "seq", None, "tp")),
        check_vma=False,
    )
```

```python
import functools

import jax
import jax.numpy as jnp
import numpy as np
from jax import lax
from jax.experimental import pallas as pl
from jax.experimental.pallas import tpu as pltpu
from jax.sharding import PartitionSpec as P

HD = 128
SINKS = 4
X, Z, CORES = 4, 8, 2
SEQ = X * Z * CORES
TP = 4
COLUMN = Z * CORES
ROWS = 64
CPOS = 8
CHUNKS = 4
SLOTS = 4
WIDTH = 512
HEADS = WIDTH // HD
WINDOW = 256
DEEP = 2048
KV_PARTS = ((1, 16), (16, 28), (28, 40), (40, 52), (52, 64))


def nt(a, b):
    return lax.dot_general(
        a, b, (((1,), (1,)), ((), ())), preferred_element_type=jnp.float32
    )


def nn(a, b):
    return lax.dot_general(
        a, b, (((1,), (0,)), ((), ())), preferred_element_type=jnp.float32
    )


def whole_kernel(
    deal, lengths, leaves, tokens, parents, freq, spans, tips, deals, cache, wq, wo,
    gathered, arrived, code_out,
    packed, sinks, N, WH, WO, KV, SK, acc, att, ATT, part, PG, fresh, G, par_pad, held,
    own_sem, tr, wr, br, gate,
    t_s, wx_s, wx_r, w_s, wsib_s, wsib_r, b_s, bsib_s, bsib_r,
    kv_s, kv_r, sk_s, sk_r, a_s, a_r, ps, pr, gs, gr,
):
    me = lax.axis_index("seq")
    tp = lax.axis_index("tp")
    x = me // COLUMN
    z = lax.rem(me // CORES, Z)
    c = lax.rem(me, CORES)
    column = lax.rem(me, COLUMN)

    def xat(dx):
        return lax.rem(x + (dx + X), X)

    def qat(dz):
        return lax.rem(z + (dz + Z), Z) * CORES + c

    def idx(dx, dz):
        return xat(dx) * COLUMN + qat(dz)

    def side(h):
        return pl.ds(pl.multiple_of(h * HD, HD), HD)

    def all_of(ref, sem):
        pltpu.make_async_copy(ref, ref, sem).wait()

    def send(src, dst, there, here, target):
        pltpu.make_async_remote_copy(
            src_ref=src, dst_ref=dst, send_sem=there, recv_sem=here,
            device_id={"seq": target},
        ).start()

    own_cache = pltpu.make_async_copy(cache, held, own_sem.at[3])
    own_cache.start()
    barrier = pltpu.get_barrier_semaphore()

    def mate(k):
        return x * COLUMN + lax.rem(column + k, COLUMN)

    for k in range(1, COLUMN):
        pl.semaphore_signal(barrier, 1, device_id={"seq": mate(k)})
    for k in range(1, X):
        pl.semaphore_signal(barrier, 1, device_id={"seq": xat(k) * COLUMN + column})
    for k in range(1, TP):
        pl.semaphore_signal(barrier, 1, device_id={"tp": lax.rem(tp + k, TP)})

    own_w = pltpu.make_async_copy(
        wq.at[:, :, side(x)], WH.at[:, x, column], own_sem.at[0]
    )
    own_w.start()
    own_b = pltpu.make_async_copy(wo, WO.at[me], own_sem.at[1])
    own_b.start()

    wide = tokens[...].astype(jnp.float32)
    centred = wide - jnp.mean(wide, axis=-1, keepdims=True)
    scaling = lax.rsqrt(jnp.mean(centred * centred, axis=-1, keepdims=True) + 1e-05)
    N[x] = (centred * scaling).astype(jnp.bfloat16)

    def pack(t, carry):
        r = deal[t]
        base = jnp.maximum(lengths[r] - WINDOW, 0)
        first = lax.shift_right_logical(base - me + (SEQ - 1), 6)
        rows = held[r, pl.ds(first, SLOTS)].reshape(2 * SLOTS, WIDTH)
        sunk = held[r, 0]
        far, near = t // COLUMN, lax.rem(t, COLUMN)
        for h in range(HEADS):
            packed[h * COLUMN + near, far] = rows[:, h * HD:(h + 1) * HD]
            sinks[h * COLUMN + near, far] = sunk[:, h * HD:(h + 1) * HD]
        return carry

    own_cache.wait()
    lax.fori_loop(0, ROWS, pack, 0)

    pl.semaphore_wait(barrier, COLUMN + X + TP - 3)
    for k in range(1, COLUMN):
        pl.semaphore_signal(gate, 1, device_id={"seq": mate(k)})

    def half_w(dz, half):
        return WH.at[:, pl.ds(half * (X // 2), X // 2), qat(dz)]

    def send_w(dz, step, half):
        at = half_w(dz, half)
        send(at, at, w_s, wr.at[(dz - step) % Z, half], idx(0, step))

    def pass_w(dz):
        at = WH.at[:, :, qat(dz)]
        send(at, at, wsib_s, wsib_r, me + 1 - 2 * c)

    def hop_w(dz):
        for half in range(2):
            all_of(half_w(dz, half), wr.at[dz % Z, half])
            if -4 < dz < 0:
                send_w(dz, 1, half)
            elif 0 < dz < 3:
                send_w(dz, -1, half)
        pass_w(dz)

    def send_b(dx, dz, way):
        at = idx(dx, dz)
        src = wo if (dx, dz) == (0, 0) else WO.at[at]
        if way == "s":
            send(src, WO.at[at], bsib_s, bsib_r, me + 1 - 2 * c)
        else:
            ox, oz = {"x+": (1, 0), "x-": (-1, 0), "z+": (0, 1), "z-": (0, -1)}[way]
            send(
                src, WO.at[at], b_s, br.at[(dx - ox) % X, (dz - oz) % Z], idx(ox, oz)
            )

    def hop_b(dx, dz):
        if (dx, dz) != (0, 0):
            all_of(WO.at[idx(dx, dz)], br.at[dx % X, dz % Z])
        out = []
        if dx == 0:
            if dz == 0:
                out += ["z+", "z-"]
            elif -3 < dz < 0:
                out += ["z+"]
            elif 0 < dz < 4:
                out += ["z-"]
            out += ["x+", "x-"]
        elif dx == -1 and dz % 2 == 0:
            out += ["x+"]
        elif dx == 1 and dz % 2 == 1:
            out += ["x-"]
        for way in out + ["s"]:
            send_b(dx, dz, way)

    for k in (2, 1, 3):
        send(
            wq.at[:, :, side(xat(k))], WH.at[:, x, column], wx_s, wx_r, idx(k, 0)
        )
    own_b.wait()
    hop_b(0, 0)
    send(N.at[x], N.at[x], t_s, tr.at[0], idx(1, 0))
    send(N.at[x], N.at[x], t_s, tr.at[1], idx(-1, 0))

    own_kv = pltpu.make_async_copy(packed.at[me], KV.at[me], own_sem.at[2])
    own_kv.start()

    def scatter(low, high):
        def one(k, carry):
            t = xat(k // COLUMN) * COLUMN + lax.rem(column + k, COLUMN)
            send(packed.at[t], KV.at[me], kv_s, kv_r, t)
            return carry

        lax.fori_loop(low, high, one, 0)

    scatter(*KV_PARTS[0])
    pl.semaphore_wait(gate, COLUMN - 1)

    sub = lax.broadcasted_iota(jnp.int32, (ROWS, ROWS), 0)
    lane = lax.broadcasted_iota(jnp.int32, (ROWS, ROWS), 1)
    lanes = lax.broadcasted_iota(jnp.int32, (ROWS, HD), 1)
    eye = jnp.where(sub == lane, 1.0, 0.0)

    def describe(k):
        request = deal[xat(k) * COLUMN + column]
        length = lengths[request]
        leaf = leaves[request]
        row = parents[pl.ds(request, 1), :]
        up = eye + jnp.where(row == sub, 1.0, 0.0)
        for _ in range(6):
            half = up.astype(jnp.bfloat16)
            up = jnp.minimum(nn(half, half), 1.0)
        reach = nt(eye.astype(jnp.bfloat16), up.astype(jnp.bfloat16))
        depth_row = (jnp.sum(up, axis=0, keepdims=True) - 1.0).astype(jnp.int32)
        depth_col = (jnp.sum(reach, axis=1, keepdims=True) - 1.0).astype(jnp.int32)
        angle = (length + depth_col).astype(jnp.float32) * freq[...]
        cosine = jnp.cos(angle)
        wave = jnp.sin(angle)
        sine = jnp.where(lanes < HD // 2, -wave, wave)
        on_path = jnp.sum(jnp.where(sub == leaf, reach, 0.0), axis=0, keepdims=True)
        offset = lax.rem(sub - length + 8 * SEQ, SEQ)
        hit = (on_path > 0.5) & (depth_row == offset)
        pick = jnp.where(hit, 1.0, 0.0).astype(jnp.bfloat16)
        return length, reach, cosine, sine, pick

    def table():
        par_pad[...] = lanes
        par_pad[:, 0:ROWS] = parents[...]
        par = par_pad[...]
        climb = jnp.where((lanes < ROWS) & (par >= 0), 1, 0)
        jump = jnp.where(par < 0, 0, par)
        for _ in range(6):
            climb = climb + jnp.take_along_axis(climb, jump, axis=1)
            jump = jnp.take_along_axis(jump, jump, axis=1)
        tip = jnp.sum(jnp.where(sub == lane, tips[...], 0), axis=1, keepdims=True)
        span = jnp.sum(jnp.where(sub == lane, spans[...], 0), axis=1, keepdims=True)
        end = jnp.sum(jnp.where(lanes == tip, climb, 0), axis=1, keepdims=True)
        tree_of = jnp.sum(jnp.where(deals[...] == sub, lane, 0), axis=1, keepdims=True)
        ahead = (me - span + 8 * SEQ) & (SEQ - 1)
        code = jnp.where(
            ahead <= end, lax.shift_right_logical(span + ahead, 6) + CPOS * tree_of, -1
        )
        code_out[...] = jnp.sum(
            jnp.where(sub == lane, code, 0), axis=0, keepdims=True
        )

    order = (2, 1, 3, 0)
    told = {order[0]: describe(order[0])}

    own_w.wait()
    all_of(WH.at[:, pl.ds(0, X - 1), 0], wx_r)
    for half in range(2):
        send_w(0, 1, half)
        send_w(0, -1, half)
    pass_w(0)
    hop_b(0, -1)
    hop_b(0, 1)
    scatter(*KV_PARTS[1])
    told[order[1]] = describe(order[1])

    left, right = pl.ds(0, DEEP // 2), pl.ds(DEEP // 2, DEEP // 2)
    all_of(N.at[0], tr.at[0])
    at = N.at[xat(-1), :, left]
    send(at, at, t_s, tr.at[2], idx(1, 0))
    all_of(N.at[0], tr.at[1])
    at = N.at[xat(1), :, right]
    send(at, at, t_s, tr.at[3], idx(-1, 0))
    hop_w(-1)
    hop_w(1)
    hop_b(0, -2)
    hop_b(0, 2)
    scatter(*KV_PARTS[2])

    @pl.when(me < SINKS)
    def _():
        pltpu.make_async_copy(sinks.at[me], SK.at[me], sk_r).start()

        def spread(k, carry):
            t = lax.rem(me + k, SEQ)
            send(sinks.at[t], SK.at[me], sk_s, sk_r, t)
            return carry

        lax.fori_loop(1, SEQ, spread, 0)

    told[order[2]] = describe(order[2])
    hop_w(-2)
    hop_w(2)
    hop_b(0, -3)
    hop_b(0, 3)
    scatter(*KV_PARTS[3])
    told[order[3]] = describe(order[3])
    hop_b(-1, 0)
    hop_b(1, 0)
    hop_w(-3)
    hop_w(3)
    hop_b(0, -4)
    scatter(*KV_PARTS[4])
    table()
    for dz in (-1, 1):
        hop_b(-1, dz)
        hop_b(1, dz)
    hop_w(-4)
    for dz in (-2, 2):
        hop_b(-1, dz)
        hop_b(1, dz)

    all_of(N.at[0, :, left], tr.at[2])
    all_of(N.at[0, :, right], tr.at[3])
    all_of(WH.at[:, :, pl.ds(0, Z)], wsib_r)
    deep = COLUMN * (DEEP // SEQ)
    rows_all = X * ROWS
    for kind in range(3):
        total = None
        for block in range(X):
            mine = N[:, :, block * deep:(block + 1) * deep].reshape(rows_all, deep)
            term = nn(mine, WH[kind, block].reshape(deep, HD))
            total = term if total is None else total + term
        acc[kind] = total

    twice = lax.broadcasted_iota(jnp.int32, (2 * SEQ, SEQ), 0)
    once = lax.broadcasted_iota(jnp.int32, (2 * SEQ, SEQ), 1)
    even = jnp.where(twice == 2 * once, 1.0, 0.0).astype(jnp.bfloat16)
    odd = jnp.where(twice == 2 * once + 1, 1.0, 0.0).astype(jnp.bfloat16)

    def block_rows(kind, k):
        return acc[kind, pl.ds(pl.multiple_of(xat(k) * ROWS, ROWS), ROWS)]

    keys, values = {}, {}
    for k in order:
        _, _, cosine, sine, pick = told[k]
        key = block_rows(1, k)
        key = key * cosine + pltpu.roll(key, HD // 2, 1) * sine
        keys[k] = key.astype(jnp.bfloat16)
        values[k] = block_rows(2, k).astype(jnp.bfloat16)
        pick_k = nn(even, pick).astype(jnp.bfloat16)
        pick_v = nn(odd, pick).astype(jnp.bfloat16)
        mixed = (nn(pick_k, keys[k]) + nn(pick_v, values[k])).astype(jnp.bfloat16)
        fresh[:, xat(k)] = mixed.reshape(SEQ, 2, HD)
    for dz in (-3, 3, -4):
        hop_b(-1, dz)
        hop_b(1, dz)

    own_g = pltpu.make_async_copy(fresh.at[me], G.at[me], own_sem.at[4])
    own_g.start()

    def hand(k, carry):
        t = lax.rem(me + k, SEQ)
        send(fresh.at[t], G.at[me], gs, gr, t)
        return carry

    lax.fori_loop(1, SEQ, hand, 0)

    later = [(-2, dz) for dz in (0, -1, 1, -2, 2, -3, 3, -4)]
    parts = [later[0:3], later[3:5], later[5:7], later[7:8]]

    own_kv.wait()
    all_of(KV.at[pl.ds(0, SEQ - 1)], kv_r)
    all_of(SK, sk_r)

    scale = float(HD) ** (-0.5)
    spot = lax.broadcasted_iota(jnp.int32, (ROWS, SEQ * SLOTS * 2), 1)
    shard = lax.shift_right_logical(spot, 3)
    slot = lax.shift_right_logical(spot & 7, 1)
    spot_s = lax.broadcasted_iota(jnp.int32, (ROWS, 2 * SINKS), 1)
    small = (2 * SINKS, 2 * SINKS)
    move = jnp.where(
        lax.broadcasted_iota(jnp.int32, small, 0) + 1
        == lax.broadcasted_iota(jnp.int32, small, 1),
        1.0, 0.0,
    ).astype(jnp.bfloat16)

    for turn, k in enumerate(order):
        length, reach, cosine, sine, _ = told[k]
        base = jnp.maximum(length - WINDOW, 0)
        first = lax.shift_right_logical(base - shard + (SEQ - 1), 6)
        place = (first + slot) * SEQ + shard
        valid = (
            ((spot & 1) == 0)
            & (place < length)
            & ((place < SINKS) | (place >= length - WINDOW))
        )
        valid_s = ((spot_s & 1) == 0) & (
            length - WINDOW > lax.shift_right_logical(spot_s, 1)
        )
        q = block_rows(0, k)
        q = (q * cosine + pltpu.roll(q, HD // 2, 1) * sine).astype(jnp.bfloat16)
        old = KV[:, pl.ds(xat(k), 1)].reshape(SEQ * SLOTS * 2, HD)
        old_s = SK[:, pl.ds(xat(k), 1)].reshape(2 * SINKS, HD)
        s = jnp.where(valid, nt(q, old) * scale, -1e30)
        s_s = jnp.where(valid_s, nt(q, old_s) * scale, -1e30)
        top = jnp.maximum(
            jnp.max(s, axis=-1, keepdims=True), jnp.max(s_s, axis=-1, keepdims=True)
        )
        w = jnp.where(valid, jnp.exp(s - top), 0.0)
        wt_s = jnp.where(valid_s, jnp.exp(s_s - top), 0.0)
        total = jnp.sum(w, axis=-1, keepdims=True) + jnp.sum(
            wt_s, axis=-1, keepdims=True
        )
        shifted = pltpu.roll(w, 1, 1).astype(jnp.bfloat16)
        shifted_s = nn(wt_s.astype(jnp.bfloat16), move).astype(jnp.bfloat16)
        weighted = nn(shifted, old) + nn(shifted_s, old_s)
        tree = reach > 0.5
        t = jnp.where(tree, nt(q, keys[k]) * scale, -1e30)
        joint = jnp.maximum(top, jnp.max(t, axis=-1, keepdims=True))
        tw = jnp.where(tree, jnp.exp(t - joint), 0.0)
        ratio = jnp.exp(top - joint)
        summed = nn(tw.astype(jnp.bfloat16), values[k])
        below = total * ratio + jnp.sum(tw, axis=-1, keepdims=True)
        done = ((weighted * ratio + summed) / below).astype(jnp.bfloat16)
        if k == 0:
            ATT[x] = done
        else:
            att[k - 1] = done
            for dx, dz in parts[turn]:
                hop_b(dx, dz)
            send(att.at[k - 1], ATT.at[x], a_s, a_r, idx(k, 0))

    for dx, dz in parts[3]:
        hop_b(dx, dz)
    all_of(ATT.at[pl.ds(0, X - 1)], a_r)
    a = jnp.concatenate([ATT[h] for h in range(HEADS)], axis=1)
    all_of(WO.at[pl.ds(0, SEQ // CORES)], bsib_r)
    wide_group = SEQ // TP
    turns = (2, 1, 3, 0)
    for at, k in enumerate(turns):
        t = lax.rem(tp + k, TP)
        right = WO[pl.ds(t * wide_group, wide_group)].reshape(WIDTH, WIDTH)
        part[t] = nt(a, right).astype(jnp.bfloat16)
        if at:
            t = lax.rem(tp + turns[at - 1], TP)
            pltpu.make_async_remote_copy(
                src_ref=part.at[t], dst_ref=PG.at[tp], send_sem=ps, recv_sem=pr,
                device_id={"tp": t},
            ).start()

    others = pl.ds(0, SEQ - 1)
    pieces = SEQ // CORES
    all_of(N.at[pl.ds(0, X - 1)], t_s)
    all_of(WH.at[:, pl.ds(0, X - 1), 0], wx_s)
    all_of(WH.at[:, :, pl.ds(0, Z - 1)], w_s)
    all_of(WH.at[:, :, pl.ds(0, Z)], wsib_s)
    all_of(WO.at[pl.ds(0, pieces - 1)], b_s)
    all_of(WO.at[pl.ds(0, pieces)], bsib_s)
    all_of(packed.at[others], kv_s)
    all_of(att, a_s)

    @pl.when(me < SINKS)
    def _():
        all_of(sinks.at[others], sk_s)

    own_g.wait()
    all_of(G.at[others], gr)
    arrived[...] = G[...]
    all_of(PG.at[pl.ds(0, TP - 1)], pr)
    below = part[tp].astype(jnp.float32)
    for k in range(1, TP):
        below = below + PG[lax.rem(tp + k, TP)].astype(jnp.float32)
    gathered[...] = below.astype(jnp.bfloat16)
    all_of(part.at[pl.ds(0, TP - 1)], ps)
    all_of(fresh.at[others], gs)


def final_kernel(code, G, gathered, cache, branch, new_cache, held, come, leave):
    chunk = ROWS // CHUNKS
    spans = [pl.ds(j * chunk, chunk) for j in range(CHUNKS)]
    ins = [
        pltpu.make_async_copy(cache.at[at], held.at[at], come.at[j])
        for j, at in enumerate(spans)
    ]
    outs = [
        pltpu.make_async_copy(held.at[at], new_cache.at[at], leave.at[j])
        for j, at in enumerate(spans)
    ]
    for copy in ins:
        copy.start()
    branch[...] = gathered[...]
    for j in range(CHUNKS):
        ins[j].wait()
        for r in range(j * chunk, (j + 1) * chunk):
            tag = code[0, r]

            @pl.when(tag >= 0)
            def _():
                spot = tag & (CPOS - 1)
                near = lax.shift_right_logical(tag, 3) & (COLUMN - 1)
                far = lax.shift_right_logical(tag, 7)
                for h in range(HEADS):
                    held[r, spot, :, h * HD:(h + 1) * HD] = G[h * COLUMN + near, far]

        outs[j].start()
    for copy in outs:
        copy.wait()


def whole():
    return pl.BlockSpec(memory_space=pltpu.VMEM)


def shaped(shape, dtype=jnp.bfloat16):
    return jax.ShapeDtypeStruct(shape, dtype)


def run_whole(deal, lengths, leaves, tokens, parents, freq, spans, tips, deals, cache, wq, wo):
    dma = pltpu.SemaphoreType.DMA
    vmem = pltpu.VMEM
    half = jnp.bfloat16
    return pl.pallas_call(
        whole_kernel,
        name="whole",
        in_specs=[pl.BlockSpec(memory_space=pltpu.SMEM)] * 3 + [whole()] * 6
        + [pl.BlockSpec(memory_space=pl.ANY)] + [whole()] * 2,
        out_specs=[whole()] * 3,
        out_shape=[
            shaped((ROWS, WIDTH)),
            shaped((SEQ, X, 2, HD)),
            shaped((1, ROWS), jnp.int32),
        ],
        scratch_shapes=[
            vmem((SEQ, X, 2 * SLOTS, HD), half),
            vmem((SEQ, X, 2, HD), half),
            vmem((X, ROWS, DEEP), half),
            vmem((3, X, COLUMN, DEEP // SEQ, HD), half),
            vmem((SEQ, DEEP // SEQ, WIDTH), half),
            vmem((SEQ, X, 2 * SLOTS, HD), half),
            vmem((SINKS, X, 2, HD), half),
            vmem((3, X * ROWS, HD), jnp.float32),
            vmem((X - 1, ROWS, HD), half),
            vmem((X, ROWS, HD), half),
            vmem((TP, ROWS, WIDTH), half),
            vmem((TP, ROWS, WIDTH), half),
            vmem((SEQ, X, 2, HD), half),
            vmem((SEQ, X, 2, HD), half),
            vmem((ROWS, HD), jnp.int32),
            vmem(cache.shape, half),
            dma((5,)), dma((4,)), dma((Z, 2)), dma((X, Z)),
            pltpu.SemaphoreType.REGULAR,
        ] + [dma] * 19,
        compiler_params=pltpu.CompilerParams(collective_id=0, has_side_effects=True),
    )(deal, lengths, leaves, tokens, parents, freq, spans, tips, deals, cache, wq, wo)


def run_final(code, arrived, gathered, cache):
    dma = pltpu.SemaphoreType.DMA
    outside = pl.BlockSpec(memory_space=pl.ANY)
    return pl.pallas_call(
        final_kernel,
        name="final",
        in_specs=[pl.BlockSpec(memory_space=pltpu.SMEM), whole(), whole(), outside],
        out_specs=[whole(), outside],
        out_shape=[shaped((ROWS, WIDTH)), shaped(cache.shape)],
        scratch_shapes=[
            pltpu.VMEM(cache.shape, jnp.bfloat16), dma((CHUNKS,)), dma((CHUNKS,)),
        ],
    )(code, arrived, gathered, cache)


def on_device(tokens, qkv_weight, out_weight, kv_cache, lengths, parents, leaves, deal):
    cache = kv_cache.reshape(kv_cache.shape[0], kv_cache.shape[1], 2, WIDTH)
    half = np.arange(HD, dtype=np.float64) % (HD // 2)
    freq = jnp.asarray((10000.0 ** (-2.0 * half / HD)).astype(np.float32)[None, :])
    wq = jnp.transpose(qkv_weight, (1, 0, 2))
    wo = jnp.transpose(out_weight, (1, 0))
    gathered, arrived, code = run_whole(
        deal, lengths, leaves, tokens, parents, freq,
        lengths.reshape(1, ROWS), leaves.reshape(1, ROWS), deal.reshape(1, ROWS),
        cache, wq, wo,
    )
    branch, new_cache = run_final(code, arrived, gathered, cache)
    return branch, new_cache.reshape(kv_cache.shape)


def solution(mesh):
    placed = (
        P("seq", None),
        P("seq", None, "tp"),
        P("tp", "seq"),
        P(None, None, "seq", None, "tp"),
        P(),
        P(),
        P(),
        P(),
    )
    return jax.shard_map(
        on_device,
        mesh=mesh,
        in_specs=placed,
        out_specs=(P("seq", "tp"), P(None, None, "seq", None, "tp")),
        check_vma=False,
    )
```
